32 devices in a mesh: shot: 2 (over y), gx: 16 (over z, x, core).
Axes of the slice: x: 2, y: 2, z: 4, core: 2. Of those that a mesh axis runs over, the one named last changes fastest.
Arguments:
- wave_now: float32 [4, 128, 16, 128], P('shot', 'gx'), parts along dimension 0, may hold values from -6 to 6
- wave_prev: float32 [4, 128, 16, 128], P('shot', 'gx'), parts along dimension 0, may hold values from -6 to 6
- speed_term: float32 [128, 16, 128], P('gx'), may hold values from 0.02 to 0.07
- thomsen_epsilon: float32 [128, 16, 128], P('gx'), may hold values from 0.15 to 0.35
- thomsen_delta: float32 [128, 16, 128], P('gx'), may hold values from 0 to 0.1
- tilt_angle: float32 [128, 16, 128], P('gx'), may hold values from -3.140625 to 3.140625
- source_store: bfloat16 [4, 4, 128, 16, 128], P('shot', None, None, 'gx'), parts along dimension 0, may hold values from -6 to 6
- receiver_row: int32 [256], P('shot'), parts along dimension 0, may hold values from 0 to 127
- receiver_column: int32 [256], P('shot'), parts along dimension 0, may hold values from 0 to 15
- receiver_traces: float32 [8, 128], P('shot'), parts along dimension 0, may hold values from -12 to 12
- angle_table: int32 [32], replicated, may hold values from 0 to 7, as said below
Outputs:
- angle_images: bfloat16 [16, 128, 16, 128], P('shot', 'gx'), parts along dimension 0
- wave_final: float32 [4, 128, 16, 128], P('shot', 'gx'), parts along dimension 0
The draws below stay inside these ranges and needn't reach their ends.
There are 2 independent parts, one for each index of `shot`. The reference program is written for one: setup_inputs(seed, part) draws one part's arguments, and reference() takes and returns one part's arrays. A program takes and returns all parts, laid end to end along the dimension named above; an argument that names none is the same for every part. Nothing has to cross between parts.
Inputs may be any that keep to these rules, and one draw needn't show every extreme that they name: angle_table is non-decreasing: angle_table[f] <= angle_table[f+1] for every fine bin f, and every one of the 8 angle images is named by at least one fine bin.
All inputs are finite; a program needn't handle non-finite values.
Results may differ from the reference program's by a relative error of at most 0.001.
Values may be sent and summed in bfloat16 or wider, within the bound.
No kernel may reach another device: no remote copies, remote signals or barrier semaphores. Data moves between devices by JAX's collectives and lax.ppermute only.
A program may use at most 128 MiB of HBM per device.

```python
import jax
import jax.numpy as jnp
from jax import lax

NZ = 128
STEPS = 4
IMAGE_EVERY = 2
NBIN = 8
FINE = 32
REC_DEPTH = 2
NSNAP = 2
NX = 128
NY = 16
NREC = 128


def draw_angle_table(key, part):
    boundary = jax.random.permutation(key, FINE - 1)[:NBIN - 1] + 1
    positions = jnp.arange(FINE, dtype=jnp.int32)
    return jnp.sum((boundary[None, :] <= positions[:, None]).astype(jnp.int32), axis=1).astype(jnp.int32)


def touch_ends(entries, own_key, smallest, high):
    longest = entries.shape.index(max(entries.shape))
    spots = []
    for shift in (0, 1):
        where = [jax.random.randint(jax.random.fold_in(own_key, axis), (), 0, length) for axis, length in enumerate(entries.shape)]
        where[longest] = (where[longest] + shift) % entries.shape[longest]
        spots.append(tuple(where))
    return entries.at[spots[0]].set(smallest).at[spots[1]].set(high)


def block_scale(key, dims, shards, low, largest):
    def one(dim, parts):
        draws = jax.random.uniform(jax.random.fold_in(jax.random.fold_in(key, 6), dim), (parts,), jnp.float32, low / len(shards), largest / len(shards))
        return jnp.repeat(jnp.exp(draws), dims[dim] // parts).reshape((-1,) + (1,) * (len(dims) - dim - 1))

    factor_of = one(*shards[0])
    for cut in shards[1:]:
        factor_of = factor_of * one(*cut)
    return factor_of


def gaussian(key, shape, deviation, most, split=(), kind=jnp.bfloat16):
    drawn = deviation * jax.random.normal(key, shape, jnp.float32)
    if split:
        drawn = drawn * block_scale(key, shape, split, -0.22, 0.18)
    return jnp.clip(drawn, -most, most).astype(kind)


def setup_inputs(seed: int = 0, part: int = 0) -> dict:
    keys = jax.random.split(jax.random.key(seed), 12)
    part_keys = jax.random.split(jax.random.fold_in(keys[11], part), 12)
    return {
        "wave_now": gaussian(part_keys[0], (2, NX, NY, NZ), 1.0, 6.0, ((1, 16),), jnp.float32),
        "wave_prev": gaussian(part_keys[1], (2, NX, NY, NZ), 1.0, 6.0, ((1, 16),), jnp.float32),
        "speed_term": jnp.clip(0.02 + 0.05 * jax.random.uniform(keys[2], (NX, NY, NZ), jnp.float32) ** block_scale(keys[2], (NX, NY, NZ), ((0, 16),), -0.2, 0.2), 0.02, 0.07),
        "thomsen_epsilon": jnp.clip(0.15 + 0.19999999 * jax.random.uniform(keys[3], (NX, NY, NZ), jnp.float32) ** block_scale(keys[3], (NX, NY, NZ), ((0, 16),), -0.2, 0.2), 0.15, 0.35),
        "thomsen_delta": jnp.clip(0.1 * jax.random.uniform(keys[4], (NX, NY, NZ), jnp.float32) ** block_scale(keys[4], (NX, NY, NZ), ((0, 16),), -0.2, 0.2), 0.0, 0.1),
        "tilt_angle": jnp.clip(jax.random.uniform(keys[5], (NX, NY, NZ), jnp.float32, -3.140625, 3.140625), -3.140625, 3.140625),
        "source_store": gaussian(part_keys[6], (NSNAP, 4, NX, NY, NZ), 1.0, 6.0, ((3, 16),)),
        "receiver_row": touch_ends(jax.random.randint(part_keys[7], (NREC,), 0, NX), jax.random.fold_in(part_keys[7], 1), 0, NX - 1).astype(jnp.int32),
        "receiver_column": touch_ends(jax.random.randint(part_keys[8], (NREC,), 0, NY), jax.random.fold_in(part_keys[8], 1), 0, NY - 1).astype(jnp.int32),
        "receiver_traces": gaussian(part_keys[9], (STEPS, NREC), 2.0, 12.0, (), jnp.float32),
        "angle_table": draw_angle_table(jax.random.fold_in(keys[11], 71), part),
    }


second_coeffs = (-205.0 / 72.0, 8.0 / 5.0, -1.0 / 5.0, 8.0 / 315.0, -1.0 / 560.0)
first_coeffs = (4.0 / 5.0, -1.0 / 5.0, 4.0 / 105.0, -1.0 / 280.0)
stencil_reach = 4

def window(array_in, direction, begin_at, extent):
    return lax.slice_in_dim(array_in, begin_at, begin_at + extent, axis=direction)

def moved(field, direction, offset):
    length = field.shape[direction]
    shape = list(field.shape)
    shape[direction] = abs(offset)
    zeros = jnp.zeros(tuple(shape), field.dtype)
    if offset > 0:
        return jnp.concatenate([lax.slice_in_dim(field, offset, length, axis=direction), zeros], axis=direction)
    return jnp.concatenate([zeros, lax.slice_in_dim(field, 0, length + offset, axis=direction)], axis=direction)

def second_along(field, direction):
    summed = second_coeffs[0] * field
    for offset in range(1, 5):
        summed = summed + second_coeffs[offset] * (moved(field, direction, offset) + moved(field, direction, -offset))
    return summed

def first_along(field, direction):
    summed = first_coeffs[0] * (moved(field, direction, 1) - moved(field, direction, -1))
    for offset in range(2, 5):
        summed = summed + first_coeffs[offset - 1] * (moved(field, direction, offset) - moved(field, direction, -offset))
    return summed

def second_diff(padded, direction, extent):
    summed = second_coeffs[0] * window(padded, direction, stencil_reach, extent)
    for offset in range(1, 5):
        summed = summed + second_coeffs[offset] * (window(padded, direction, stencil_reach + offset, extent) + window(padded, direction, stencil_reach - offset, extent))
    return summed

def first_diff(padded, direction, extent):
    summed = first_coeffs[0] * (window(padded, direction, stencil_reach + 1, extent) - window(padded, direction, stencil_reach - 1, extent))
    for offset in range(2, 5):
        summed = summed + first_coeffs[offset - 1] * (window(padded, direction, stencil_reach + offset, extent) - window(padded, direction, stencil_reach - offset, extent))
    return summed

def advance(padded, earlier, medium, traces_now, receiver_row, receiver_column, first_row):
    extent_x = earlier.shape[1]
    extent_y = earlier.shape[2]
    speed, epsilon, thomsen, tilt = medium
    second_x = second_diff(padded, 1, extent_x)
    inner_rows = padded[:, 4:-4]
    second_y = second_along(inner_rows[0], 1)
    second_z = second_along(inner_rows, 3)
    slope_z_all = first_along(padded, 3)
    mixed = first_diff(slope_z_all, 1, extent_x)
    slope_x = first_diff(padded[0], 0, extent_x)
    slope_y = first_along(inner_rows[0], 1)
    slope_z = slope_z_all[0, 4:-4]
    cosine = jnp.cos(tilt)
    sine = jnp.sin(tilt)
    rotated = cosine * cosine * second_z + sine * sine * second_x + 2.0 * sine * cosine * mixed
    across_p = second_x[0] + second_y + second_z[0] - rotated[0]
    ratio = jnp.sqrt(1.0 + 2.0 * thomsen)
    centre = inner_rows
    p_next = 2.0 * centre[0] - earlier[0] + speed * ((1.0 + 2.0 * epsilon) * across_p + ratio * rotated[1])
    q_next = 2.0 * centre[1] - earlier[1] + speed * (ratio * across_p + rotated[1])
    local_row = receiver_row - first_row
    inside = (local_row >= 0) & (local_row < extent_x)
    flat_index = jnp.where(inside, local_row * extent_y + receiver_column, extent_x * extent_y)
    plane = jnp.zeros((extent_x * extent_y,), jnp.float32).at[flat_index].add(traces_now, mode='drop')
    p_next = p_next.at[:, :, REC_DEPTH].add(plane.reshape(extent_x, extent_y))
    return (jnp.stack([p_next, q_next]), (slope_x, slope_y, slope_z))

def angle_image(snapshot, wave_field, earlier_field, slopes, selector):
    fine_count = selector.shape[1]
    rate = wave_field - earlier_field
    flux_x = -rate * slopes[0]
    flux_y = -rate * slopes[1]
    flux_z = -rate * slopes[2]
    inner = snapshot[1] * flux_x + snapshot[2] * flux_y + snapshot[3] * flux_z
    lengths = jnp.sqrt(snapshot[1] * snapshot[1] + snapshot[2] * snapshot[2] + snapshot[3] * snapshot[3]) * jnp.sqrt(flux_x * flux_x + flux_y * flux_y + flux_z * flux_z)
    cosine = inner / jnp.maximum(lengths, 1.0)
    scaled = (cosine + 1.0) * (0.5 * (fine_count - 1))
    centres = jnp.arange(fine_count, dtype=jnp.float32).reshape((fine_count,) + (1,) * scaled.ndim)
    weights = jnp.maximum(0.0, 1.0 - jnp.abs(scaled[None] - centres)) * (snapshot[0] * wave_field)[None]
    summed = jnp.dot(selector, weights.reshape(fine_count, -1), precision=lax.Precision.HIGHEST, preferred_element_type=jnp.float32)
    return summed.reshape((selector.shape[0],) + wave_field.shape)

def sliced_image(snapshot, current, earlier, slopes, selector):
    inputs = (jnp.moveaxis(snapshot, 1, 0), current, earlier, slopes[0], slopes[1], slopes[2])

    def one_slab(pieces):
        return angle_image(pieces[0], pieces[1], pieces[2], (pieces[3], pieces[4], pieces[5]), selector)
    return jnp.moveaxis(lax.map(one_slab, inputs), 1, 0)

def reference(wave_now, wave_prev, speed_term, thomsen_epsilon, thomsen_delta, tilt_angle, source_store, receiver_row, receiver_column, receiver_traces, angle_table):
    medium = (speed_term, thomsen_epsilon, thomsen_delta, tilt_angle)
    selector = (angle_table[None, :] == jnp.arange(NBIN, dtype=jnp.int32)[:, None]).astype(jnp.float32)
    current = wave_now
    earlier = wave_prev
    images = jnp.zeros((NBIN, NX, NY, NZ), jnp.float32)
    for time_step in range(STEPS):
        padded = jnp.pad(current, ((0, 0), (4, 4), (0, 0), (0, 0)))
        following, slopes = advance(padded, earlier, medium, receiver_traces[time_step], receiver_row, receiver_column, 0)
        if time_step % IMAGE_EVERY == IMAGE_EVERY - 1:
            snapshot = source_store[time_step // IMAGE_EVERY].astype(jnp.float32)
            images = images + sliced_image(snapshot, current[0], earlier[0], slopes, selector)
        earlier = current
        current = following
    return (images.astype(jnp.bfloat16), current)
```

```python
import functools

import jax
import jax.numpy as jnp
from jax import lax
from jax.experimental import pallas as pl
from jax.experimental.pallas import tpu as pltpu
from jax.sharding import PartitionSpec as P

STEPS = 4
IMAGE_EVERY = 2
NBIN = 8
REC_DEPTH = 2
REACH = 4
HALO = 2 * REACH
YPAD = 8

SECOND = (-205.0 / 72.0, 8.0 / 5.0, -1.0 / 5.0, 8.0 / 315.0, -1.0 / 560.0)
FIRST = (4.0 / 5.0, -1.0 / 5.0, 4.0 / 105.0, -1.0 / 280.0)


def each_row(count, width, body):
    if width <= 16:
        for row in range(count):
            body(row)
    else:
        lax.fori_loop(0, count, lambda row, carry: (body(row), carry)[1], 0)


def second(centre, pairs):
    total = SECOND[0] * centre
    for k in range(1, 5):
        plus, minus = pairs(k)
        total = total + SECOND[k] * (plus + minus)
    return total


def first(pairs):
    total = None
    for k in range(1, 5):
        plus, minus = pairs(k)
        term = FIRST[k - 1] * (plus - minus)
        total = term if total is None else total + term
    return total


def depth_diffs(field, want_second):
    depth = field.shape[-1]
    lane = lax.broadcasted_iota(jnp.int32, field.shape, 1)
    shifted = {}
    for k in range(1, 5):
        plus = jnp.where(lane < depth - k, pltpu.roll(field, depth - k, axis=1), 0.0)
        minus = jnp.where(lane >= k, pltpu.roll(field, k, axis=1), 0.0)
        shifted[k] = (plus, minus)
    slope = first(lambda k: shifted[k])
    return slope, second(field, lambda k: shifted[k]) if want_second else None


def sine_terms(angle):
    half = 0.5 * angle
    sq = half * half
    s = 1.0
    for n in (12 * 13, 10 * 11, 8 * 9, 6 * 7, 4 * 5, 2 * 3):
        s = 1.0 - sq * s * (1.0 / n)
    s = s * half
    c = 1.0
    for n in (13 * 14, 11 * 12, 9 * 10, 7 * 8, 5 * 6, 3 * 4, 1 * 2):
        c = 1.0 - sq * c * (1.0 / n)
    sine = 2.0 * s * c
    cosine = 1.0 - 2.0 * s * s
    return sine * sine, 2.0 * sine * cosine


def injected(flat, traces, step, row, width):
    cell = lax.broadcasted_iota(jnp.int32, (width, flat.shape[1]), 0) + row * width
    hit = jnp.where(cell == flat, traces[step : step + 1, :], 0.0)
    return jnp.sum(hit, axis=1, keepdims=True)


def time_step(rows, width, fields, earlier, coeffs, slopes, curves, inject, emit):
    p, q = fields
    slope_p, slope_q = slopes
    curve_p, curve_q = curves
    inner = slice(YPAD, YPAD + width)

    def along_depth(row):
        slope_p[row], curve_p[row] = depth_diffs(p[row, inner, :], True)
        slope_q[row], curve_q[row] = depth_diffs(q[row], True)

    each_row(rows + 2 * REACH, width, along_depth)

    def update(row):
        at = row + REACH
        now_p = p[at, inner, :]
        now_q = q[at]
        xx_p = second(now_p, lambda k: (p[at + k, inner, :], p[at - k, inner, :]))
        xx_q = second(now_q, lambda k: (q[at + k], q[at - k]))
        xz_p = first(lambda k: (slope_p[at + k], slope_p[at - k]))
        xz_q = first(lambda k: (slope_q[at + k], slope_q[at - k]))
        yy_p = second(
            now_p,
            lambda k: (
                p[at, YPAD + k : YPAD + k + width, :],
                p[at, YPAD - k : YPAD - k + width, :],
            ),
        )
        speed, gain, mixed, sine_sq, sine_double = coeffs(row)
        tilt_p = sine_sq * (xx_p - curve_p[at]) + sine_double * xz_p
        tilt_q = sine_sq * (xx_q - curve_q[at]) + sine_double * xz_q
        across = xx_p + yy_p - tilt_p
        rotated = curve_q[at] + tilt_q
        prev_p, prev_q = earlier(row)
        next_p = 2.0 * now_p - prev_p + (gain * across + mixed * rotated)
        next_q = 2.0 * now_q - prev_q + (mixed * across + speed * rotated)
        lane = lax.broadcasted_iota(jnp.int32, next_p.shape, 1)
        next_p = next_p + jnp.where(lane == REC_DEPTH, inject(row), 0.0)
        emit(row, next_p, next_q)

    each_row(rows, width, update)


def flux_row(row, width, p, slope_p, before):
    at = row + REACH
    now = p[at, YPAD : YPAD + width, :]
    back = before - now
    slope_x = first(
        lambda k: (p[at + k, YPAD : YPAD + width, :], p[at - k, YPAD : YPAD + width, :])
    )
    slope_y = first(
        lambda k: (p[at, YPAD + k : YPAD + k + width, :], p[at, YPAD - k : YPAD - k + width, :])
    )
    return now, (back * slope_x, back * slope_y, back * slope_p[at])


def clear_pads(ref, width):
    rows, _, depth = ref.shape
    zeros = jnp.zeros((rows, YPAD, depth), jnp.float32)
    ref[:, :YPAD, :] = zeros
    ref[:, YPAD + width :, :] = zeros


def place(dst_p, dst_q, centre, sides, width):
    rows = centre.shape[1]
    inner = pl.ds(YPAD, width)
    dst_p[pl.ds(HALO, rows), inner, :] = centre[0]
    dst_q[pl.ds(HALO, rows)] = centre[1]
    for at, read in sides:
        dst_p[pl.ds(at, HALO), inner, :] = read(0, HALO)
        dst_q[pl.ds(at, HALO)] = read(HALO, HALO)


def side_starts(rows, reach):
    odd = lax.rem(lax.axis_index("gx"), 2)
    on_chip = jnp.where(odd == 1, 0, rows + reach)
    off_chip = jnp.where(odd == 1, rows + reach, 0)
    return on_chip, off_chip


def receivers(row_ref, column_ref, rows, width):
    begin = lax.axis_index("gx") * rows - REACH
    count = row_ref.shape[0]
    local_row = row_ref[...].reshape(1, count) - begin
    inside = (local_row >= 0) & (local_row < rows + 2 * REACH)
    return jnp.where(inside, local_row * width + column_ref[...].reshape(1, count), -1)


def two_steps(
    t, rows, width, p, q, first_prev, coeffs, flat, traces, scratch, mid_emit, emit, second_prev
):
    slope_p, slope_q, curve_p, curve_q, p1, q1 = scratch
    inner = slice(YPAD, YPAD + width)
    clear_pads(p1, width)

    def keep(row, next_p, next_q):
        p1[row, inner, :] = next_p
        q1[row] = next_q
        mid_emit(row, next_p, next_q)

    time_step(
        rows + 2 * REACH,
        width,
        (p, q),
        first_prev,
        lambda row: [coeffs[c, row] for c in range(5)],
        (slope_p, slope_q),
        (curve_p, curve_q),
        lambda row: injected(flat, traces, t, row, width),
        keep,
    )
    time_step(
        rows,
        width,
        (p1, q1),
        second_prev,
        lambda row: [coeffs[c, row + REACH] for c in range(5)],
        (slope_p, slope_q),
        (curve_p, curve_q),
        lambda row: injected(flat, traces, t + 1, row + REACH, width),
        emit,
    )


def early_kernel(
    now,
    prev,
    speed,
    epsilon,
    delta,
    tilt,
    on_chip,
    off_chip,
    receiver_row,
    receiver_column,
    traces,
    out,
    mid,
    flux,
    coeffs,
    p,
    q,
    prev_ext,
    *scratch,
):
    rows, width = now.shape[1], now.shape[2]
    near, far = side_starts(rows, HALO)
    clear_pads(p, width)
    place(
        p,
        q,
        now,
        (
            (near, lambda a, n: on_chip[pl.ds(a, n)]),
            (far, lambda a, n: off_chip[pl.ds(a, n)]),
        ),
        width,
    )
    near, far = side_starts(rows, REACH)
    base = 2 * HALO

    def derive(at, s, e, d, a):
        coeffs[0, at] = s
        coeffs[1, at] = s * (1.0 + 2.0 * e)
        coeffs[2, at] = s * jnp.sqrt(1.0 + 2.0 * d)
        coeffs[3, at], coeffs[4, at] = sine_terms(a)

    each_row(
        rows,
        width,
        lambda r: derive(r + REACH, speed[r], epsilon[r], delta[r], tilt[r]),
    )
    for f in range(2):
        prev_ext[f, pl.ds(REACH, rows)] = prev[f]
    for at, part in ((near, on_chip), (far, off_chip)):
        for f in range(2):
            prev_ext[f, pl.ds(at, REACH)] = part[pl.ds(base + f * REACH, REACH)]
        for r in range(REACH):
            derive(at + r, *[part[base + (2 + m) * REACH + r] for m in range(4)])

    flat = receivers(receiver_row, receiver_column, rows, width)

    def mid_emit(row, next_p, next_q):
        mid[0, row] = next_p
        mid[1, row] = next_q

    def emit(row, next_p, next_q):
        out[0, row] = next_p
        out[1, row] = next_q

    two_steps(
        0,
        rows,
        width,
        p,
        q,
        lambda row: (prev_ext[0, row], prev_ext[1, row]),
        coeffs,
        flat,
        traces,
        scratch,
        mid_emit,
        emit,
        lambda row: (now[0, row], now[1, row]),
    )
    slope_p, p1 = scratch[0], scratch[4]

    def fluxes(row):
        _, parts = flux_row(row, width, p1, slope_p, now[0, row])
        for a in range(3):
            flux[a, row] = parts[a]

    each_row(rows, width, fluxes)


def late_kernel(
    now,
    mid,
    flux,
    coeffs,
    on_chip,
    off_chip,
    receiver_row,
    receiver_column,
    traces,
    source,
    table,
    images,
    out,
    p,
    q,
    *scratch,
):
    rows, width = now.shape[1], now.shape[2]
    near, far = side_starts(rows, HALO)
    clear_pads(p, width)
    place(
        p,
        q,
        now,
        (
            (near, lambda a, n: on_chip[a // HALO]),
            (far, lambda a, n: off_chip[a // HALO]),
        ),
        width,
    )
    flat = receivers(receiver_row, receiver_column, rows, width)

    def emit(row, next_p, next_q):
        out[0, row] = next_p
        out[1, row] = next_q

    two_steps(
        2,
        rows,
        width,
        p,
        q,
        lambda row: (mid[0, row], mid[1, row]),
        coeffs,
        flat,
        traces,
        scratch,
        lambda row, next_p, next_q: None,
        emit,
        lambda row: (now[0, row], now[1, row]),
    )
    slope_p, p1 = scratch[0], scratch[4]

    fine = table.shape[0]
    starts = [jnp.int32(0)] * NBIN
    for f in range(fine):
        named = table[f]
        for b in range(1, NBIN):
            starts[b] = starts[b] + (named < b).astype(jnp.int32)
    offsets = [s.astype(jnp.float32) - 1.0 for s in starts] + [jnp.float32(fine - 1)]

    def image_row(row):
        totals = [None] * NBIN
        late = flux_row(row, width, p1, slope_p, now[0, row])
        early = (mid[0, row + REACH], (flux[0, row], flux[1, row], flux[2, row]))
        for n, (field, (fx, fy, fz)) in enumerate((early, late)):
            s0, s1, s2, s3 = [source[n, c, row].astype(jnp.float32) for c in range(4)]
            dot = s1 * fx + s2 * fy + s3 * fz
            lengths = jnp.sqrt(s1 * s1 + s2 * s2 + s3 * s3) * jnp.sqrt(fx * fx + fy * fy + fz * fz)
            cosine = dot / jnp.maximum(lengths, 1.0)
            scaled = (cosine + 1.0) * (0.5 * (fine - 1))
            strength = s0 * field
            ramps = [jnp.clip(scaled - o, 0.0, 1.0) * strength for o in offsets]
            for b in range(NBIN):
                term = ramps[b] - ramps[b + 1]
                totals[b] = term if totals[b] is None else totals[b] + term
        for b in range(NBIN):
            images[b, row] = totals[b].astype(images.dtype)

    each_row(rows, width, image_row)


def local(
    wave_now,
    wave_prev,
    speed_term,
    thomsen_epsilon,
    thomsen_delta,
    tilt_angle,
    source_store,
    receiver_row,
    receiver_column,
    receiver_traces,
    angle_table,
):
    _, rows, width, depth = wave_now.shape
    count = lax.axis_size("gx")
    odd = lax.rem(lax.axis_index("gx"), 2)
    on_chip_pairs = [(i, i ^ 1) for i in range(count)]
    off_chip_pairs = [(i, i + 1) for i in range(1, count - 1, 2)]
    off_chip_pairs = off_chip_pairs + [(b, a) for a, b in off_chip_pairs]

    def pack(tail):
        def edge(x, n, dim):
            return lax.dynamic_slice_in_dim(x, jnp.where(tail, rows - n, 0), n, axis=dim)

        wave = wave_now if rows == HALO else edge(wave_now, HALO, 1)
        parts = [wave.reshape(2 * HALO, width, depth)]
        parts.append(edge(wave_prev, REACH, 1).reshape(2 * REACH, width, depth))
        for x in (speed_term, thomsen_epsilon, thomsen_delta, tilt_angle):
            parts.append(edge(x, REACH, 0))
        return jnp.concatenate(parts, axis=0)

    off_chip = lax.ppermute(pack(odd == 1), "gx", off_chip_pairs)
    on_chip = lax.ppermute(pack(odd == 0), "gx", on_chip_pairs)
    arrived = lax.all_to_all(source_store, "gx", split_axis=2, concat_axis=3, tiled=True)

    f32 = jnp.float32
    ext, wide = rows + 2 * REACH, rows + 2 * HALO
    vmem = pl.BlockSpec(memory_space=pltpu.VMEM)
    smem = pl.BlockSpec(memory_space=pltpu.SMEM)
    plane = (width, depth)
    padded = (width + 2 * YPAD, depth)
    steps_scratch = [
        pltpu.VMEM((wide,) + plane, f32),
        pltpu.VMEM((wide,) + plane, f32),
        pltpu.VMEM((wide,) + plane, f32),
        pltpu.VMEM((wide,) + plane, f32),
        pltpu.VMEM((ext,) + padded, f32),
        pltpu.VMEM((ext,) + plane, f32),
    ]
    wave_scratch = [pltpu.VMEM((wide,) + padded, f32), pltpu.VMEM((wide,) + plane, f32)]
    cells = rows * width * depth
    limit = 60 * 1024 * 1024
    now, mid, flux, coeffs = pl.pallas_call(
        early_kernel,
        out_shape=(
            jax.ShapeDtypeStruct((2, rows) + plane, f32),
            jax.ShapeDtypeStruct((2, ext) + plane, f32),
            jax.ShapeDtypeStruct((3, rows) + plane, f32),
            jax.ShapeDtypeStruct((5, ext) + plane, f32),
        ),
        in_specs=[vmem] * 11,
        out_specs=(vmem,) * 4,
        scratch_shapes=wave_scratch + [pltpu.VMEM((2, ext) + plane, f32)] + steps_scratch,
        compiler_params=pltpu.CompilerParams(vmem_limit_bytes=limit),
        cost_estimate=pl.CostEstimate(flops=600 * cells, bytes_accessed=120 * cells, transcendentals=0),
        name="early",
    )(
        wave_now,
        wave_prev,
        speed_term,
        thomsen_epsilon,
        thomsen_delta,
        tilt_angle,
        on_chip,
        off_chip,
        receiver_row,
        receiver_column,
        receiver_traces,
    )

    def sides(x, tail):
        if rows == HALO:
            return x
        return lax.dynamic_slice_in_dim(x, jnp.where(tail, rows - HALO, 0), HALO, axis=1)

    off_chip = lax.ppermute(sides(now, odd == 1), "gx", off_chip_pairs)
    on_chip = lax.ppermute(sides(now, odd == 0), "gx", on_chip_pairs)
    return pl.pallas_call(
        late_kernel,
        out_shape=(
            jax.ShapeDtypeStruct((NBIN, rows) + plane, jnp.bfloat16),
            jax.ShapeDtypeStruct((2, rows) + plane, f32),
        ),
        in_specs=[vmem] * 10 + [smem],
        out_specs=(vmem, vmem),
        scratch_shapes=wave_scratch + steps_scratch,
        compiler_params=pltpu.CompilerParams(vmem_limit_bytes=limit),
        cost_estimate=pl.CostEstimate(flops=700 * cells, bytes_accessed=120 * cells, transcendentals=0),
        name="late",
    )(
        now,
        mid,
        flux,
        coeffs,
        on_chip,
        off_chip,
        receiver_row,
        receiver_column,
        receiver_traces,
        arrived,
        angle_table,
    )


def solution(mesh):
    placed = (
        P("shot", "gx", None, None),
        P("shot", "gx", None, None),
        P("gx", None, None),
        P("gx", None, None),
        P("gx", None, None),
        P("gx", None, None),
        P("shot", None, None, "gx", None),
        P("shot"),
        P("shot"),
        P("shot", None),
        P(),
    )
    return jax.shard_map(
        local,
        mesh=mesh,
        in_specs=placed,
        out_specs=(P("shot", "gx", None, None), P("shot", "gx", None, None)),
        check_vma=False,
    )
```

```python
import jax
import jax.numpy as jnp
from jax import lax
from jax.experimental import pallas as pl
from jax.experimental.pallas import tpu as pltpu
from jax.sharding import PartitionSpec as P


NBIN = 8
REC_DEPTH = 2
REACH = 4
HALO = 2 * REACH
YPAD = 8

SECOND = (-205.0 / 72.0, 8.0 / 5.0, -1.0 / 5.0, 8.0 / 315.0, -1.0 / 560.0)
FIRST = (4.0 / 5.0, -1.0 / 5.0, 4.0 / 105.0, -1.0 / 280.0)


def each_row(count, width, body):
    if width <= 16:
        for row in range(count):
            body(row)
    else:
        lax.fori_loop(0, count, lambda row, carry: (body(row), carry)[1], 0)


def second(centre, pairs):
    total = SECOND[0] * centre
    for k in range(1, 5):
        plus, minus = pairs(k)
        total = total + SECOND[k] * (plus + minus)
    return total


def first(pairs):
    total = None
    for k in range(1, 5):
        plus, minus = pairs(k)
        term = FIRST[k - 1] * (plus - minus)
        total = term if total is None else total + term
    return total


def depth_diffs(field, want_second):
    depth = field.shape[-1]
    lane = lax.broadcasted_iota(jnp.int32, field.shape, 1)
    shifted = {}
    for k in range(1, 5):
        plus = jnp.where(lane < depth - k, pltpu.roll(field, depth - k, axis=1), 0.0)
        minus = jnp.where(lane >= k, pltpu.roll(field, k, axis=1), 0.0)
        shifted[k] = (plus, minus)
    slope = first(lambda k: shifted[k])
    return slope, second(field, lambda k: shifted[k]) if want_second else None


def sine_terms(angle):
    half = 0.5 * angle
    sq = half * half
    s = 1.0
    for n in (12 * 13, 10 * 11, 8 * 9, 6 * 7, 4 * 5, 2 * 3):
        s = 1.0 - sq * s * (1.0 / n)
    s = s * half
    c = 1.0
    for n in (13 * 14, 11 * 12, 9 * 10, 7 * 8, 5 * 6, 3 * 4, 1 * 2):
        c = 1.0 - sq * c * (1.0 / n)
    sine = 2.0 * s * c
    cosine = 1.0 - 2.0 * s * s
    return sine * sine, 2.0 * sine * cosine


def injected(flat, traces, step, row, width):
    cell = lax.broadcasted_iota(jnp.int32, (width, flat.shape[1]), 0) + row * width
    hit = jnp.where(cell == flat, traces[step : step + 1, :], 0.0)
    return jnp.sum(hit, axis=1, keepdims=True)


def time_step(rows, width, fields, earlier, coeffs, slopes, curves, inject, emit):
    p, q = fields
    slope_p, slope_q = slopes
    curve_p, curve_q = curves
    inner = slice(YPAD, YPAD + width)

    def along_depth(row):
        slope_p[row], curve_p[row] = depth_diffs(p[row, inner, :], True)
        slope_q[row], curve_q[row] = depth_diffs(q[row], True)

    each_row(rows + 2 * REACH, width, along_depth)

    def update(row):
        at = row + REACH
        now_p = p[at, inner, :]
        now_q = q[at]
        xx_p = second(now_p, lambda k: (p[at + k, inner, :], p[at - k, inner, :]))
        xx_q = second(now_q, lambda k: (q[at + k], q[at - k]))
        xz_p = first(lambda k: (slope_p[at + k], slope_p[at - k]))
        xz_q = first(lambda k: (slope_q[at + k], slope_q[at - k]))
        yy_p = second(
            now_p,
            lambda k: (
                p[at, YPAD + k : YPAD + k + width, :],
                p[at, YPAD - k : YPAD - k + width, :],
            ),
        )
        speed, gain, mixed, sine_sq, sine_double = coeffs(row)
        tilt_p = sine_sq * (xx_p - curve_p[at]) + sine_double * xz_p
        tilt_q = sine_sq * (xx_q - curve_q[at]) + sine_double * xz_q
        across = xx_p + yy_p - tilt_p
        rotated = curve_q[at] + tilt_q
        prev_p, prev_q = earlier(row)
        next_p = 2.0 * now_p - prev_p + (gain * across + mixed * rotated)
        next_q = 2.0 * now_q - prev_q + (mixed * across + speed * rotated)
        lane = lax.broadcasted_iota(jnp.int32, next_p.shape, 1)
        next_p = next_p + jnp.where(lane == REC_DEPTH, inject(row), 0.0)
        emit(row, next_p, next_q)

    each_row(rows, width, update)


def flux_row(row, width, p, slope_p, before):
    at = row + REACH
    now = p[at, YPAD : YPAD + width, :]
    back = before - now
    slope_x = first(
        lambda k: (p[at + k, YPAD : YPAD + width, :], p[at - k, YPAD : YPAD + width, :])
    )
    slope_y = first(
        lambda k: (p[at, YPAD + k : YPAD + k + width, :], p[at, YPAD - k : YPAD - k + width, :])
    )
    return now, (back * slope_x, back * slope_y, back * slope_p[at])


def clear_pads(ref, width):
    rows, _, depth = ref.shape
    zeros = jnp.zeros((rows, YPAD, depth), jnp.float32)
    ref[:, :YPAD, :] = zeros
    ref[:, YPAD + width :, :] = zeros


def place(dst_p, dst_q, centre, sides, width):
    rows = centre.shape[1]
    inner = pl.ds(YPAD, width)
    dst_p[pl.ds(HALO, rows), inner, :] = centre[0]
    dst_q[pl.ds(HALO, rows)] = centre[1]
    for at, read in sides:
        dst_p[pl.ds(at, HALO), inner, :] = read(0, HALO)
        dst_q[pl.ds(at, HALO)] = read(HALO, HALO)


def side_starts(rows, reach):
    odd = lax.rem(lax.axis_index("gx"), 2)
    on_chip = jnp.where(odd == 1, 0, rows + reach)
    off_chip = jnp.where(odd == 1, rows + reach, 0)
    return on_chip, off_chip


def receivers(row_ref, column_ref, rows, width):
    begin = lax.axis_index("gx") * rows - REACH
    count = row_ref.shape[0]
    local_row = row_ref[...].reshape(1, count) - begin
    inside = (local_row >= 0) & (local_row < rows + 2 * REACH)
    return jnp.where(inside, local_row * width + column_ref[...].reshape(1, count), -1)


def two_steps(
    t, rows, width, p, q, first_prev, coeffs, flat, traces, scratch, mid_emit, emit, second_prev
):
    slope_p, slope_q, curve_p, curve_q, p1, q1 = scratch
    inner = slice(YPAD, YPAD + width)
    clear_pads(p1, width)

    def keep(row, next_p, next_q):
        p1[row, inner, :] = next_p
        q1[row] = next_q
        mid_emit(row, next_p, next_q)

    time_step(
        rows + 2 * REACH,
        width,
        (p, q),
        first_prev,
        lambda row: [coeffs[c, row] for c in range(5)],
        (slope_p, slope_q),
        (curve_p, curve_q),
        lambda row: injected(flat, traces, t, row, width),
        keep,
    )
    time_step(
        rows,
        width,
        (p1, q1),
        second_prev,
        lambda row: [coeffs[c, row + REACH] for c in range(5)],
        (slope_p, slope_q),
        (curve_p, curve_q),
        lambda row: injected(flat, traces, t + 1, row + REACH, width),
        emit,
    )


def pack_kernel(now, prev, speed, epsilon, delta, tilt, far, near, sems):
    rows = now.shape[1]
    odd = lax.rem(lax.axis_index("gx"), 2)
    copies = []

    def copy(src, dst):
        copies.append(pltpu.make_async_copy(src, dst, sems.at[len(copies)]))
        copies[-1].start()

    for out, tail in ((far, odd), (near, 1 - odd)):
        wave_at = tail * (rows - HALO)
        edge_at = tail * (rows - REACH)
        for f in range(2):
            copy(now.at[f, pl.ds(wave_at, HALO)], out.at[pl.ds(f * HALO, HALO)])
        for f in range(2):
            copy(
                prev.at[f, pl.ds(edge_at, REACH)],
                out.at[pl.ds(2 * HALO + f * REACH, REACH)],
            )
        for m, field in enumerate((speed, epsilon, delta, tilt)):
            copy(
                field.at[pl.ds(edge_at, REACH)],
                out.at[pl.ds(2 * HALO + (2 + m) * REACH, REACH)],
            )
    for one in copies:
        one.wait()


def early_kernel(
    now,
    prev,
    speed,
    epsilon,
    delta,
    tilt,
    on_chip,
    off_chip,
    receiver_row,
    receiver_column,
    traces,
    out,
    mid,
    flux,
    coeffs,
    p,
    q,
    prev_ext,
    *scratch,
):
    rows, width = now.shape[1], now.shape[2]
    near, far = side_starts(rows, HALO)
    clear_pads(p, width)
    place(
        p,
        q,
        now,
        (
            (near, lambda a, n: on_chip[pl.ds(a, n)]),
            (far, lambda a, n: off_chip[pl.ds(a, n)]),
        ),
        width,
    )
    near, far = side_starts(rows, REACH)
    base = 2 * HALO

    def derive(at, s, e, d, a):
        coeffs[0, at] = s
        coeffs[1, at] = s * (1.0 + 2.0 * e)
        coeffs[2, at] = s * jnp.sqrt(1.0 + 2.0 * d)
        coeffs[3, at], coeffs[4, at] = sine_terms(a)

    each_row(
        rows,
        width,
        lambda r: derive(r + REACH, speed[r], epsilon[r], delta[r], tilt[r]),
    )
    for f in range(2):
        prev_ext[f, pl.ds(REACH, rows)] = prev[f]
    for at, part in ((near, on_chip), (far, off_chip)):
        for f in range(2):
            prev_ext[f, pl.ds(at, REACH)] = part[pl.ds(base + f * REACH, REACH)]
        for r in range(REACH):
            derive(at + r, *[part[base + (2 + m) * REACH + r] for m in range(4)])

    flat = receivers(receiver_row, receiver_column, rows, width)

    def mid_emit(row, next_p, next_q):
        mid[0, row] = next_p
        mid[1, row] = next_q

    def emit(row, next_p, next_q):
        out[0, row] = next_p
        out[1, row] = next_q

    two_steps(
        0,
        rows,
        width,
        p,
        q,
        lambda row: (prev_ext[0, row], prev_ext[1, row]),
        coeffs,
        flat,
        traces,
        scratch,
        mid_emit,
        emit,
        lambda row: (now[0, row], now[1, row]),
    )
    slope_p, p1 = scratch[0], scratch[4]

    def fluxes(row):
        _, parts = flux_row(row, width, p1, slope_p, now[0, row])
        for a in range(3):
            flux[a, row] = parts[a]

    each_row(rows, width, fluxes)


def late_kernel(
    now,
    mid,
    flux,
    coeffs,
    on_chip,
    off_chip,
    receiver_row,
    receiver_column,
    traces,
    source,
    table,
    images,
    out,
    p,
    q,
    *scratch,
):
    rows, width = now.shape[1], now.shape[2]
    near, far = side_starts(rows, HALO)
    clear_pads(p, width)
    place(
        p,
        q,
        now,
        (
            (near, lambda a, n: on_chip[a // HALO]),
            (far, lambda a, n: off_chip[a // HALO]),
        ),
        width,
    )
    flat = receivers(receiver_row, receiver_column, rows, width)

    def emit(row, next_p, next_q):
        out[0, row] = next_p
        out[1, row] = next_q

    two_steps(
        2,
        rows,
        width,
        p,
        q,
        lambda row: (mid[0, row], mid[1, row]),
        coeffs,
        flat,
        traces,
        scratch,
        lambda row, next_p, next_q: None,
        emit,
        lambda row: (now[0, row], now[1, row]),
    )
    slope_p, p1 = scratch[0], scratch[4]

    fine = table.shape[0]
    starts = [jnp.int32(0)] * NBIN
    for f in range(fine):
        named = table[f]
        for b in range(1, NBIN):
            starts[b] = starts[b] + (named < b).astype(jnp.int32)
    offsets = [s.astype(jnp.float32) - 1.0 for s in starts] + [jnp.float32(fine - 1)]

    def image_row(row):
        totals = [None] * NBIN
        late = flux_row(row, width, p1, slope_p, now[0, row])
        early = (mid[0, row + REACH], (flux[0, row], flux[1, row], flux[2, row]))
        for n, (field, (fx, fy, fz)) in enumerate((early, late)):
            s0, s1, s2, s3 = [source[n, c, row].astype(jnp.float32) for c in range(4)]
            dot = s1 * fx + s2 * fy + s3 * fz
            lengths = jnp.sqrt(s1 * s1 + s2 * s2 + s3 * s3) * jnp.sqrt(fx * fx + fy * fy + fz * fz)
            cosine = dot / jnp.maximum(lengths, 1.0)
            scaled = (cosine + 1.0) * (0.5 * (fine - 1))
            strength = s0 * field
            ramps = [jnp.clip(scaled - o, 0.0, 1.0) * strength for o in offsets]
            for b in range(NBIN):
                term = ramps[b] - ramps[b + 1]
                totals[b] = term if totals[b] is None else totals[b] + term
        for b in range(NBIN):
            images[b, row] = totals[b].astype(images.dtype)

    each_row(rows, width, image_row)


def local(
    wave_now,
    wave_prev,
    speed_term,
    thomsen_epsilon,
    thomsen_delta,
    tilt_angle,
    source_store,
    receiver_row,
    receiver_column,
    receiver_traces,
    angle_table,
):
    _, rows, width, depth = wave_now.shape
    count = lax.axis_size("gx")
    odd = lax.rem(lax.axis_index("gx"), 2)
    on_chip_pairs = [(i, i ^ 1) for i in range(count)]
    off_chip_pairs = [(i, i + 1) for i in range(1, count - 1, 2)]
    off_chip_pairs = off_chip_pairs + [(b, a) for a, b in off_chip_pairs]

    f32 = jnp.float32
    ext, wide = rows + 2 * REACH, rows + 2 * HALO
    vmem = pl.BlockSpec(memory_space=pltpu.VMEM)
    smem = pl.BlockSpec(memory_space=pltpu.SMEM)
    plane = (width, depth)
    padded = (width + 2 * YPAD, depth)
    steps_scratch = [
        pltpu.VMEM((wide,) + plane, f32),
        pltpu.VMEM((wide,) + plane, f32),
        pltpu.VMEM((wide,) + plane, f32),
        pltpu.VMEM((wide,) + plane, f32),
        pltpu.VMEM((ext,) + padded, f32),
        pltpu.VMEM((ext,) + plane, f32),
    ]
    wave_scratch = [pltpu.VMEM((wide,) + padded, f32), pltpu.VMEM((wide,) + plane, f32)]
    cells = rows * width * depth
    plane_bytes = 4 * width * depth

    def limit(planes):
        return 4 * 1024 * 1024 + planes * plane_bytes

    packed = jax.ShapeDtypeStruct((2 * HALO + 6 * REACH,) + plane, f32)
    medium = (speed_term, thomsen_epsilon, thomsen_delta, tilt_angle)
    in_hbm = pl.BlockSpec(memory_space=pltpu.HBM)
    far_pack, near_pack = pl.pallas_call(
        pack_kernel,
        out_shape=(packed, packed),
        in_specs=[in_hbm] * 6,
        out_specs=(vmem, vmem),
        scratch_shapes=[pltpu.SemaphoreType.DMA((16,))],
        compiler_params=pltpu.CompilerParams(vmem_limit_bytes=limit(80)),
        name="pack",
    )(
        *[
            pltpu.with_memory_space_constraint(x, pltpu.HBM)
            for x in (wave_now, wave_prev, *medium)
        ]
    )
    off_chip = lax.ppermute(far_pack, "gx", off_chip_pairs)
    on_chip = lax.ppermute(near_pack, "gx", on_chip_pairs)
    arrived = lax.all_to_all(
        source_store, "gx", split_axis=2, concat_axis=3, tiled=True
    )
    now, mid, flux, coeffs = pl.pallas_call(
        early_kernel,
        out_shape=(
            jax.ShapeDtypeStruct((2, rows) + plane, f32),
            jax.ShapeDtypeStruct((2, ext) + plane, f32),
            jax.ShapeDtypeStruct((3, rows) + plane, f32),
            jax.ShapeDtypeStruct((5, ext) + plane, f32),
        ),
        in_specs=[vmem] * 11,
        out_specs=(vmem,) * 4,
        scratch_shapes=wave_scratch + [pltpu.VMEM((2, ext) + plane, f32)] + steps_scratch,
        compiler_params=pltpu.CompilerParams(vmem_limit_bytes=limit(26 * wide)),
        cost_estimate=pl.CostEstimate(flops=600 * cells, bytes_accessed=120 * cells, transcendentals=0),
        name="early",
    )(
        wave_now,
        wave_prev,
        *medium,
        on_chip,
        off_chip,
        receiver_row,
        receiver_column,
        receiver_traces,
    )

    def sides(x, tail):
        if rows == HALO:
            return x
        return lax.dynamic_slice_in_dim(x, jnp.where(tail, rows - HALO, 0), HALO, axis=1)

    off_chip = lax.ppermute(sides(now, odd == 1), "gx", off_chip_pairs)
    on_chip = lax.ppermute(sides(now, odd == 0), "gx", on_chip_pairs)
    return pl.pallas_call(
        late_kernel,
        out_shape=(
            jax.ShapeDtypeStruct((NBIN, rows) + plane, jnp.bfloat16),
            jax.ShapeDtypeStruct((2, rows) + plane, f32),
        ),
        in_specs=[vmem] * 10 + [smem],
        out_specs=(vmem, vmem),
        scratch_shapes=wave_scratch + steps_scratch,
        compiler_params=pltpu.CompilerParams(vmem_limit_bytes=limit(26 * wide)),
        cost_estimate=pl.CostEstimate(flops=700 * cells, bytes_accessed=120 * cells, transcendentals=0),
        name="late",
    )(
        now,
        mid,
        flux,
        coeffs,
        on_chip,
        off_chip,
        receiver_row,
        receiver_column,
        receiver_traces,
        arrived,
        angle_table,
    )


def solution(mesh):
    placed = (
        P("shot", "gx", None, None),
        P("shot", "gx", None, None),
        P("gx", None, None),
        P("gx", None, None),
        P("gx", None, None),
        P("gx", None, None),
        P("shot", None, None, "gx", None),
        P("shot"),
        P("shot"),
        P("shot", None),
        P(),
    )
    return jax.shard_map(
        local,
        mesh=mesh,
        in_specs=placed,
        out_specs=(P("shot", "gx", None, None), P("shot", "gx", None, None)),
        check_vma=False,
    )
```

```python
import jax
import jax.numpy as jnp
import numpy as np
from jax import lax
from jax.experimental import pallas as pl
from jax.experimental.pallas import tpu as pltpu
from jax.sharding import PartitionSpec as P


STEPS = 4
NBIN = 8
REC_DEPTH = 2
REACH = 4
HALO = 2 * REACH
YPAD = 8

SECOND = (-205.0 / 72.0, 8.0 / 5.0, -1.0 / 5.0, 8.0 / 315.0, -1.0 / 560.0)
FIRST = (4.0 / 5.0, -1.0 / 5.0, 4.0 / 105.0, -1.0 / 280.0)


def each_row(count, width, body):
    if width <= 16:
        for row in range(count):
            body(row)
    else:
        lax.fori_loop(0, count, lambda row, carry: (body(row), carry)[1], 0)


def each_chunk(count, width, body):
    size = max(1, min(count, 512 // width))
    while count % size:
        size -= 1
    if count // size <= 2:
        for start in range(0, count, size):
            body(start, size)
    else:
        lax.fori_loop(0, count // size, lambda i, carry: (body(i * size, size), carry)[1], 0)


def second(centre, pairs):
    total = SECOND[0] * centre
    for k in range(1, 5):
        plus, minus = pairs(k)
        total = total + SECOND[k] * (plus + minus)
    return total


def first(pairs):
    total = None
    for k in range(1, 5):
        plus, minus = pairs(k)
        term = FIRST[k - 1] * (plus - minus)
        total = term if total is None else total + term
    return total


def depth_matrices(depth):
    eye = [np.eye(depth, k=k, dtype=np.float64) for k in range(-4, 5)]
    slope = sum(np.float32(FIRST[k - 1]) * (eye[4 - k] - eye[4 + k]) for k in range(1, 5))
    curve = np.float32(SECOND[0]) * eye[4] + sum(
        np.float32(SECOND[k]) * (eye[4 - k] + eye[4 + k]) for k in range(1, 5)
    )
    rest = np.concatenate([slope, curve], axis=1).astype(np.float32)
    parts = []
    for _ in range(3):
        parts.append(rest.astype(jnp.bfloat16))
        rest = rest - parts[-1].astype(np.float32)
    return np.stack(parts)


def depth_diffs(field, matrices):
    depth = field.shape[1]
    high = field.astype(jnp.bfloat16)
    rest = field - high.astype(jnp.float32)
    middle = rest.astype(jnp.bfloat16)
    low = (rest - middle.astype(jnp.float32)).astype(jnp.bfloat16)
    m_high, m_middle, m_low = matrices[0], matrices[1], matrices[2]

    def product(left, top, bottom):
        return jnp.dot(
            left, jnp.concatenate([top, bottom], axis=0), preferred_element_type=jnp.float32
        )

    upper = jnp.concatenate([high, middle], axis=1)
    lower = jnp.concatenate([high, low], axis=1)
    both = (
        product(lower, m_low, m_high)
        + product(upper, m_middle, m_middle)
        + product(upper, m_high, m_high)
    )
    return both[:, :depth], both[:, depth:]


def depth_rows(read, slope, curve, begin, count, width, matrices, shift=0):
    def chunk(start, size):
        field = read(begin + start, size)
        depth = field.shape[-1]
        s, c = depth_diffs(field.reshape(size * width, depth), matrices)
        slope[pl.ds(begin + shift + start, size)] = s.reshape(size, width, depth)
        curve[pl.ds(begin + shift + start, size)] = c.reshape(size, width, depth)

    each_chunk(count, width, chunk)


def sine_terms(angle):
    half = 0.5 * angle
    sq = half * half
    s = 1.0
    for n in (12 * 13, 10 * 11, 8 * 9, 6 * 7, 4 * 5, 2 * 3):
        s = 1.0 - sq * s * (1.0 / n)
    s = s * half
    c = 1.0
    for n in (13 * 14, 11 * 12, 9 * 10, 7 * 8, 5 * 6, 3 * 4, 1 * 2):
        c = 1.0 - sq * c * (1.0 / n)
    sine = 2.0 * s * c
    cosine = 1.0 - 2.0 * s * s
    return sine * sine, 2.0 * sine * cosine


def derive(coeffs, at, s, e, d, a):
    coeffs[0, at] = s
    coeffs[1, at] = s * (1.0 + 2.0 * e)
    coeffs[2, at] = s * jnp.sqrt(1.0 + 2.0 * d)
    coeffs[3, at], coeffs[4, at] = sine_terms(a)


def receivers(row_ref, column_ref, rows, width):
    begin = lax.axis_index("gx") * rows - REACH
    count = row_ref.shape[0]
    local_row = row_ref[...].reshape(1, count) - begin
    inside = (local_row >= 0) & (local_row < rows + 2 * REACH)
    return jnp.where(inside, local_row * width + column_ref[...].reshape(1, count), -1)


def time_step(rows, width, fields, earlier, coeffs, slopes, curves, inject, emit):
    p, q = fields
    slope_p, slope_q = slopes
    curve_p, curve_q = curves
    inner = slice(YPAD, YPAD + width)

    def update(row):
        at = row + REACH
        now_p = p[at, inner, :]
        now_q = q[at]
        xx_p = second(now_p, lambda k: (p[at + k, inner, :], p[at - k, inner, :]))
        xx_q = second(now_q, lambda k: (q[at + k], q[at - k]))
        xz_p = first(lambda k: (slope_p[at + k], slope_p[at - k]))
        xz_q = first(lambda k: (slope_q[at + k], slope_q[at - k]))
        yy_p = second(
            now_p,
            lambda k: (
                p[at, YPAD + k : YPAD + k + width, :],
                p[at, YPAD - k : YPAD - k + width, :],
            ),
        )
        speed, gain, mixed, sine_sq, sine_double = coeffs(row)
        tilt_p = sine_sq * (xx_p - curve_p[at]) + sine_double * xz_p
        tilt_q = sine_sq * (xx_q - curve_q[at]) + sine_double * xz_q
        across = xx_p + yy_p - tilt_p
        rotated = curve_q[at] + tilt_q
        prev_p, prev_q = earlier(row)
        next_p = 2.0 * now_p - prev_p + (gain * across + mixed * rotated)
        next_q = 2.0 * now_q - prev_q + (mixed * across + speed * rotated)
        emit(row, next_p + inject(row), next_q)

    each_row(rows, width, update)


def flux_row(row, width, p, slope_z, before):
    at = row + REACH
    now = p[at, YPAD : YPAD + width, :]
    back = before - now
    slope_x = first(
        lambda k: (p[at + k, YPAD : YPAD + width, :], p[at - k, YPAD : YPAD + width, :])
    )
    slope_y = first(
        lambda k: (p[at, YPAD + k : YPAD + k + width, :], p[at, YPAD - k : YPAD - k + width, :])
    )
    return now, (back * slope_x, back * slope_y, back * slope_z)


def image_terms(source, n, row, field, flux, offsets, emit):
    fx, fy, fz = flux
    s0, s1, s2, s3 = [source[n, c, row].astype(jnp.float32) for c in range(4)]
    dot = s1 * fx + s2 * fy + s3 * fz
    lengths = jnp.sqrt(s1 * s1 + s2 * s2 + s3 * s3) * jnp.sqrt(fx * fx + fy * fy + fz * fz)
    cosine = dot / jnp.maximum(lengths, 1.0)
    scaled = (cosine + 1.0) * offsets[NBIN + 1 : NBIN + 2, :]
    strength = s0 * field
    ramps = [
        jnp.clip(scaled - offsets[b : b + 1, :], 0.0, 1.0) * strength for b in range(NBIN + 1)
    ]
    for b in range(NBIN):
        emit(b, ramps[b] - ramps[b + 1])


def clear_pads(ref, width):
    rows, _, depth = ref.shape
    zeros = jnp.zeros((rows, YPAD, depth), jnp.float32)
    ref[:, :YPAD, :] = zeros
    ref[:, YPAD + width :, :] = zeros


def place(dst_p, dst_q, centre, sides, width):
    rows = centre.shape[1]
    inner = pl.ds(YPAD, width)
    dst_p[pl.ds(HALO, rows), inner, :] = centre[0]
    dst_q[pl.ds(HALO, rows)] = centre[1]
    for at, read in sides:
        dst_p[pl.ds(at, HALO), inner, :] = read(0, HALO)
        dst_q[pl.ds(at, HALO)] = read(HALO, HALO)


def side_starts(rows, reach):
    odd = lax.rem(lax.axis_index("gx"), 2)
    on_chip = jnp.where(odd == 1, 0, rows + reach)
    off_chip = jnp.where(odd == 1, rows + reach, 0)
    return on_chip, off_chip


def two_steps(
    t, rows, width, waves, own, first_prev, coeffs, inject, matrices, scratch, mid_emit, emit, second_prev
):
    p, q = waves
    slope_p, slope_q, curve_p, curve_q, p1, q1 = scratch
    inner = slice(YPAD, YPAD + width)
    clear_pads(p1, width)
    for dst, src in zip((slope_p, slope_q, curve_p, curve_q), own):
        dst[pl.ds(HALO, rows)] = src

    def read_p(start, size):
        return p[pl.ds(start, size), inner, :]

    def read_q(start, size):
        return q[pl.ds(start, size)]

    for begin in (0, rows + HALO):
        depth_rows(read_p, slope_p, curve_p, begin, HALO, width, matrices)
        depth_rows(read_q, slope_q, curve_q, begin, HALO, width, matrices)

    def keep(row, next_p, next_q):
        p1[row, inner, :] = next_p
        q1[row] = next_q
        mid_emit(row, next_p, next_q)

    ext = rows + 2 * REACH
    time_step(
        ext,
        width,
        waves,
        first_prev,
        lambda row: [coeffs[c, row] for c in range(5)],
        (slope_p, slope_q),
        (curve_p, curve_q),
        lambda row: inject[t, row],
        keep,
    )
    depth_rows(lambda b, n: p1[pl.ds(b, n), inner, :], slope_p, curve_p, 0, ext, width, matrices)
    depth_rows(lambda b, n: q1[pl.ds(b, n)], slope_q, curve_q, 0, ext, width, matrices)
    time_step(
        rows,
        width,
        (p1, q1),
        second_prev,
        lambda row: [coeffs[c, row + REACH] for c in range(5)],
        (slope_p, slope_q),
        (curve_p, curve_q),
        lambda row: inject[t + 1, row + REACH],
        emit,
    )


def pack_kernel(now, prev, speed, epsilon, delta, tilt, far, near, sems):
    rows = now.shape[1]
    odd = lax.rem(lax.axis_index("gx"), 2)
    copies = []

    def copy(src, dst):
        copies.append(pltpu.make_async_copy(src, dst, sems.at[len(copies)]))
        copies[-1].start()

    for out, tail in ((far, odd), (near, 1 - odd)):
        wave_at = tail * (rows - HALO)
        edge_at = tail * (rows - REACH)
        for f in range(2):
            copy(now.at[f, pl.ds(wave_at, HALO)], out.at[pl.ds(f * HALO, HALO)])
        for f in range(2):
            copy(
                prev.at[f, pl.ds(edge_at, REACH)],
                out.at[pl.ds(2 * HALO + f * REACH, REACH)],
            )
        for m, field in enumerate((speed, epsilon, delta, tilt)):
            copy(
                field.at[pl.ds(edge_at, REACH)],
                out.at[pl.ds(2 * HALO + (2 + m) * REACH, REACH)],
            )
    for one in copies:
        one.wait()


def prep_kernel(
    now,
    speed,
    epsilon,
    delta,
    tilt,
    receiver_row,
    receiver_column,
    traces,
    table,
    matrices,
    coeffs,
    inject,
    slopes,
    curves,
    offsets,
):
    rows, width, depth = speed.shape
    each_row(
        rows,
        width,
        lambda r: derive(coeffs, r, speed[r], epsilon[r], delta[r], tilt[r]),
    )
    for f in range(2):
        depth_rows(
            lambda b, n: now[f, pl.ds(b, n)], slopes.at[f], curves.at[f], 0, rows, width, matrices
        )
    flat = receivers(receiver_row, receiver_column, rows, width)

    def samples(row):
        cell = lax.broadcasted_iota(jnp.int32, (width, flat.shape[1]), 0) + row * width
        lane = lax.broadcasted_iota(jnp.int32, (width, depth), 1)
        hit = cell == flat
        for t in range(STEPS):
            column = jnp.sum(jnp.where(hit, traces[t : t + 1, :], 0.0), axis=1, keepdims=True)
            inject[t, row] = jnp.where(lane == REC_DEPTH, column, 0.0)

    each_row(rows + 2 * REACH, width, samples)
    fine = table.shape[0]
    starts = [jnp.int32(0)] * NBIN
    for f in range(fine):
        named = table[f]
        for b in range(1, NBIN):
            starts[b] = starts[b] + (named < b).astype(jnp.int32)
    values = [s.astype(jnp.float32) - 1.0 for s in starts]
    values = values + [jnp.float32(fine - 1), jnp.float32(0.5 * (fine - 1))]
    for b, value in enumerate(values):
        offsets[b : b + 1, :] = jnp.full((1, depth), value, jnp.float32)


def early_kernel(
    now,
    prev,
    on_chip,
    off_chip,
    own_coeffs,
    inject,
    slopes,
    curves,
    matrices,
    out,
    mid,
    coeffs,
    slope_out,
    p,
    q,
    prev_ext,
    *scratch,
):
    rows, width = now.shape[1], now.shape[2]
    near, far = side_starts(rows, HALO)
    clear_pads(p, width)
    place(
        p,
        q,
        now,
        (
            (near, lambda a, n: on_chip[pl.ds(a, n)]),
            (far, lambda a, n: off_chip[pl.ds(a, n)]),
        ),
        width,
    )
    near, far = side_starts(rows, REACH)
    base = 2 * HALO
    for c in range(5):
        coeffs[c, pl.ds(REACH, rows)] = own_coeffs[c]
    for f in range(2):
        prev_ext[f, pl.ds(REACH, rows)] = prev[f]
    for at, part in ((near, on_chip), (far, off_chip)):
        for f in range(2):
            prev_ext[f, pl.ds(at, REACH)] = part[pl.ds(base + f * REACH, REACH)]
        for r in range(REACH):
            derive(coeffs, at + r, *[part[base + (2 + m) * REACH + r] for m in range(4)])

    def mid_emit(row, next_p, next_q):
        mid[0, row] = next_p
        mid[1, row] = next_q

    def emit(row, next_p, next_q):
        out[0, row] = next_p
        out[1, row] = next_q

    two_steps(
        0,
        rows,
        width,
        (p, q),
        (slopes[0], slopes[1], curves[0], curves[1]),
        lambda row: (prev_ext[0, row], prev_ext[1, row]),
        coeffs,
        inject,
        matrices,
        scratch,
        mid_emit,
        emit,
        lambda row: (now[0, row], now[1, row]),
    )
    slope_out[...] = scratch[0][pl.ds(REACH, rows)]


def side_kernel(before, mid, slope_z, now, matrices, flux, slopes, curves, p1):
    rows, width = before.shape[1], before.shape[2]
    clear_pads(p1, width)
    p1[:, YPAD : YPAD + width, :] = mid[0]

    def fluxes(row):
        _, parts = flux_row(row, width, p1, slope_z[row], before[0, row])
        for a in range(3):
            flux[a, row] = parts[a]

    each_row(rows, width, fluxes)
    for f in range(2):
        depth_rows(
            lambda b, n: now[f, pl.ds(b, n)], slopes.at[f], curves.at[f], 0, rows, width, matrices
        )


def first_image_kernel(source, mid, flux, offsets, images):
    rows, width = flux.shape[1], flux.shape[2]

    def image_row(row):
        def emit(b, term):
            images[b, row] = term

        image_terms(
            source, 0, row, mid[0, row + REACH], [flux[a, row] for a in range(3)], offsets, emit
        )

    each_row(rows, width, image_row)


def late_kernel(
    now,
    mid,
    coeffs,
    on_chip,
    off_chip,
    inject,
    slopes,
    curves,
    matrices,
    source,
    offsets,
    partial_images,
    images,
    out,
    p,
    q,
    *scratch,
):
    rows, width = now.shape[1], now.shape[2]
    near, far = side_starts(rows, HALO)
    clear_pads(p, width)
    place(
        p,
        q,
        now,
        (
            (near, lambda a, n: on_chip[a // HALO]),
            (far, lambda a, n: off_chip[a // HALO]),
        ),
        width,
    )

    def emit(row, next_p, next_q):
        out[0, row] = next_p
        out[1, row] = next_q

    two_steps(
        2,
        rows,
        width,
        (p, q),
        (slopes[0], slopes[1], curves[0], curves[1]),
        lambda row: (mid[0, row], mid[1, row]),
        coeffs,
        inject,
        matrices,
        scratch,
        lambda row, next_p, next_q: None,
        emit,
        lambda row: (now[0, row], now[1, row]),
    )
    slope_z, p1 = scratch[0], scratch[4]

    def image_row(row):
        field, flux = flux_row(row, width, p1, slope_z[row + REACH], now[0, row])

        def finish(b, term):
            images[b, row] = (partial_images[b, row] + term).astype(images.dtype)

        image_terms(source, 1, row, field, flux, offsets, finish)

    each_row(rows, width, image_row)


def local(
    wave_now,
    wave_prev,
    speed_term,
    thomsen_epsilon,
    thomsen_delta,
    tilt_angle,
    source_store,
    receiver_row,
    receiver_column,
    receiver_traces,
    angle_table,
):
    _, rows, width, depth = wave_now.shape
    count = lax.axis_size("gx")
    odd = lax.rem(lax.axis_index("gx"), 2)
    on_chip_pairs = [(i, i ^ 1) for i in range(count)]
    off_chip_pairs = [(i, i + 1) for i in range(1, count - 1, 2)]
    off_chip_pairs = off_chip_pairs + [(b, a) for a, b in off_chip_pairs]

    f32 = jnp.float32
    ext, wide = rows + 2 * REACH, rows + 2 * HALO
    vmem = pl.BlockSpec(memory_space=pltpu.VMEM)
    smem = pl.BlockSpec(memory_space=pltpu.SMEM)
    in_hbm = pl.BlockSpec(memory_space=pltpu.HBM)
    plane = (width, depth)
    padded = (width + 2 * YPAD, depth)
    plane_bytes = 4 * width * depth
    line_flops = width * depth

    def planes(*lead):
        return jax.ShapeDtypeStruct(lead + plane, f32)

    def call(kernel, outs, ins, in_specs, scratch, grant, cost):
        return pl.pallas_call(
            kernel,
            out_shape=outs,
            in_specs=in_specs,
            out_specs=jax.tree.map(lambda _: vmem, outs),
            scratch_shapes=scratch,
            compiler_params=pltpu.CompilerParams(
                vmem_limit_bytes=4 * 1024 * 1024 + grant * plane_bytes
            ),
            cost_estimate=pl.CostEstimate(
                flops=cost * line_flops, bytes_accessed=cost * line_flops // 4, transcendentals=0
            ),
        )(*ins)

    step_scratch = [
        pltpu.VMEM((wide,) + plane, f32),
        pltpu.VMEM((wide,) + plane, f32),
        pltpu.VMEM((wide,) + plane, f32),
        pltpu.VMEM((wide,) + plane, f32),
        pltpu.VMEM((ext,) + padded, f32),
        pltpu.VMEM((ext,) + plane, f32),
    ]
    wave_scratch = [pltpu.VMEM((wide,) + padded, f32), pltpu.VMEM((wide,) + plane, f32)]
    medium = (speed_term, thomsen_epsilon, thomsen_delta, tilt_angle)
    matrices = jnp.asarray(depth_matrices(depth))

    packed = planes(2 * HALO + 6 * REACH)
    far_pack, near_pack = call(
        pack_kernel,
        (packed, packed),
        [
            pltpu.with_memory_space_constraint(x, pltpu.HBM)
            for x in (wave_now, wave_prev, *medium)
        ],
        [in_hbm] * 6,
        [pltpu.SemaphoreType.DMA((16,))],
        80,
        200,
    )
    off_chip = lax.ppermute(far_pack, "gx", off_chip_pairs)
    on_chip = lax.ppermute(near_pack, "gx", on_chip_pairs)
    arrived = lax.all_to_all(source_store, "gx", split_axis=2, concat_axis=3, tiled=True)
    own_coeffs, inject, slopes, curves, offsets = call(
        prep_kernel,
        (
            planes(5, rows),
            planes(STEPS, ext),
            planes(2, rows),
            planes(2, rows),
            jax.ShapeDtypeStruct((16, depth), f32),
        ),
        (wave_now, *medium, receiver_row, receiver_column, receiver_traces, angle_table, matrices),
        [vmem] * 8 + [smem, vmem],
        [],
        20 * wide,
        60 * rows,
    )
    now, mid, coeffs, slope_z = call(
        early_kernel,
        (planes(2, rows), planes(2, ext), planes(5, ext), planes(rows)),
        (wave_now, wave_prev, on_chip, off_chip, own_coeffs, inject, slopes, curves, matrices),
        [vmem] * 9,
        wave_scratch + [pltpu.VMEM((2, ext) + plane, f32)] + step_scratch,
        30 * wide,
        400 * rows,
    )

    def side(tail):
        if rows == HALO:
            return now
        return lax.dynamic_slice_in_dim(now, jnp.where(tail, rows - HALO, 0), HALO, axis=1)

    off_chip = lax.ppermute(side(odd == 1), "gx", off_chip_pairs)
    on_chip = lax.ppermute(side(odd == 0), "gx", on_chip_pairs)
    flux, slopes, curves = call(
        side_kernel,
        (planes(3, rows), planes(2, rows), planes(2, rows)),
        (wave_now, mid, slope_z, now, matrices),
        [vmem] * 5,
        [pltpu.VMEM((ext,) + padded, f32)],
        12 * wide,
        60 * rows,
    )
    partial_images = call(
        first_image_kernel,
        planes(NBIN, rows),
        (arrived, mid, flux, offsets),
        [vmem] * 4,
        [],
        16 * wide,
        60 * rows,
    )
    images, final = call(
        late_kernel,
        (jax.ShapeDtypeStruct((NBIN, rows) + plane, jnp.bfloat16), planes(2, rows)),
        (
            now,
            mid,
            coeffs,
            on_chip,
            off_chip,
            inject,
            slopes,
            curves,
            matrices,
            arrived,
            offsets,
            partial_images,
        ),
        [vmem] * 12,
        wave_scratch + step_scratch,
        34 * wide,
        500 * rows,
    )
    return images, final


def solution(mesh):
    placed = (
        P("shot", "gx", None, None),
        P("shot", "gx", None, None),
        P("gx", None, None),
        P("gx", None, None),
        P("gx", None, None),
        P("gx", None, None),
        P("shot", None, None, "gx", None),
        P("shot"),
        P("shot"),
        P("shot", None),
        P(),
    )
    return jax.shard_map(
        local,
        mesh=mesh,
        in_specs=placed,
        out_specs=(P("shot", "gx", None, None), P("shot", "gx", None, None)),
        check_vma=False,
    )
```

```python
import jax
import jax.numpy as jnp
import numpy as np
from jax import lax
from jax.experimental import pallas as pl
from jax.experimental.pallas import tpu as pltpu
from jax.sharding import PartitionSpec as P


STEPS = 4
NBIN = 8
REC_DEPTH = 2
REACH = 4
HALO = 2 * REACH
YPAD = 8

SECOND = (-205.0 / 72.0, 8.0 / 5.0, -1.0 / 5.0, 8.0 / 315.0, -1.0 / 560.0)
FIRST = (4.0 / 5.0, -1.0 / 5.0, 4.0 / 105.0, -1.0 / 280.0)


def each_row(count, width, body):
    if width <= 16:
        for row in range(count):
            body(row)
    else:
        lax.fori_loop(0, count, lambda row, carry: (body(row), carry)[1], 0)


def each_chunk(count, width, body):
    size = max(1, min(count, 512 // width))
    while count % size:
        size -= 1
    if count // size <= 2:
        for start in range(0, count, size):
            body(start, size)
    else:
        lax.fori_loop(0, count // size, lambda i, carry: (body(i * size, size), carry)[1], 0)


def second(centre, pairs):
    total = SECOND[0] * centre
    for k in range(1, 5):
        plus, minus = pairs(k)
        total = total + SECOND[k] * (plus + minus)
    return total


def first(pairs):
    total = None
    for k in range(1, 5):
        plus, minus = pairs(k)
        term = FIRST[k - 1] * (plus - minus)
        total = term if total is None else total + term
    return total


def depth_matrices(depth):
    eye = [np.eye(depth, k=k, dtype=np.float64) for k in range(-4, 5)]
    slope = sum(np.float32(FIRST[k - 1]) * (eye[4 - k] - eye[4 + k]) for k in range(1, 5))
    curve = np.float32(SECOND[0]) * eye[4] + sum(
        np.float32(SECOND[k]) * (eye[4 - k] + eye[4 + k]) for k in range(1, 5)
    )
    rest = np.concatenate([slope, curve], axis=1).astype(np.float32)
    parts = []
    for _ in range(3):
        parts.append(rest.astype(jnp.bfloat16))
        rest = rest - parts[-1].astype(np.float32)
    return np.stack(parts)


def depth_diffs(field, matrices):
    depth = field.shape[1]
    high = field.astype(jnp.bfloat16)
    rest = field - high.astype(jnp.float32)
    middle = rest.astype(jnp.bfloat16)
    low = (rest - middle.astype(jnp.float32)).astype(jnp.bfloat16)
    m_high, m_middle, m_low = matrices[0], matrices[1], matrices[2]

    def product(left, top, bottom):
        return jnp.dot(
            left, jnp.concatenate([top, bottom], axis=0), preferred_element_type=jnp.float32
        )

    upper = jnp.concatenate([high, middle], axis=1)
    lower = jnp.concatenate([high, low], axis=1)
    both = (
        product(lower, m_low, m_high)
        + product(upper, m_middle, m_middle)
        + product(upper, m_high, m_high)
    )
    return both[:, :depth], both[:, depth:]


def depth_rows(read, slope, curve, begin, count, width, matrices, shift=0):
    def chunk(start, size):
        field = read(begin + start, size)
        depth = field.shape[-1]
        s, c = depth_diffs(field.reshape(size * width, depth), matrices)
        slope[pl.ds(begin + shift + start, size)] = s.reshape(size, width, depth)
        curve[pl.ds(begin + shift + start, size)] = c.reshape(size, width, depth)

    each_chunk(count, width, chunk)


def sine_terms(angle):
    half = 0.5 * angle
    sq = half * half
    s = 1.0
    for n in (12 * 13, 10 * 11, 8 * 9, 6 * 7, 4 * 5, 2 * 3):
        s = 1.0 - sq * s * (1.0 / n)
    s = s * half
    c = 1.0
    for n in (13 * 14, 11 * 12, 9 * 10, 7 * 8, 5 * 6, 3 * 4, 1 * 2):
        c = 1.0 - sq * c * (1.0 / n)
    sine = 2.0 * s * c
    cosine = 1.0 - 2.0 * s * s
    return sine * sine, 2.0 * sine * cosine


def derive(coeffs, at, s, e, d, a):
    coeffs[0, at] = s
    coeffs[1, at] = s * (1.0 + 2.0 * e)
    coeffs[2, at] = s * jnp.sqrt(1.0 + 2.0 * d)
    coeffs[3, at], coeffs[4, at] = sine_terms(a)


def receivers(row_ref, column_ref, rows, width):
    begin = lax.axis_index("gx") * rows - REACH
    count = row_ref.shape[0]
    local_row = row_ref[...].reshape(1, count) - begin
    inside = (local_row >= 0) & (local_row < rows + 2 * REACH)
    return jnp.where(inside, local_row * width + column_ref[...].reshape(1, count), -1)


def time_step(rows, width, fields, earlier, coeffs, slopes, curves, inject, emit):
    p, q = fields
    slope_p, slope_q = slopes
    curve_p, curve_q = curves
    inner = slice(YPAD, YPAD + width)

    def update(row):
        at = row + REACH
        now_p = p[at, inner, :]
        now_q = q[at]
        xx_p = second(now_p, lambda k: (p[at + k, inner, :], p[at - k, inner, :]))
        xx_q = second(now_q, lambda k: (q[at + k], q[at - k]))
        xz_p = first(lambda k: (slope_p[at + k], slope_p[at - k]))
        xz_q = first(lambda k: (slope_q[at + k], slope_q[at - k]))
        yy_p = second(
            now_p,
            lambda k: (
                p[at, YPAD + k : YPAD + k + width, :],
                p[at, YPAD - k : YPAD - k + width, :],
            ),
        )
        speed, gain, mixed, sine_sq, sine_double = coeffs(row)
        tilt_p = sine_sq * (xx_p - curve_p[at]) + sine_double * xz_p
        tilt_q = sine_sq * (xx_q - curve_q[at]) + sine_double * xz_q
        across = xx_p + yy_p - tilt_p
        rotated = curve_q[at] + tilt_q
        prev_p, prev_q = earlier(row)
        next_p = 2.0 * now_p - prev_p + (gain * across + mixed * rotated)
        next_q = 2.0 * now_q - prev_q + (mixed * across + speed * rotated)
        emit(row, next_p + inject(row), next_q)

    each_row(rows, width, update)


def flux_row(row, width, p, slope_z, before):
    at = row + REACH
    now = p[at, YPAD : YPAD + width, :]
    back = before - now
    slope_x = first(
        lambda k: (p[at + k, YPAD : YPAD + width, :], p[at - k, YPAD : YPAD + width, :])
    )
    slope_y = first(
        lambda k: (p[at, YPAD + k : YPAD + k + width, :], p[at, YPAD - k : YPAD - k + width, :])
    )
    return now, (back * slope_x, back * slope_y, back * slope_z)


def image_terms(source, n, row, field, flux, offsets, emit):
    fx, fy, fz = flux
    s0, s1, s2, s3 = [source[n, c, row].astype(jnp.float32) for c in range(4)]
    dot = s1 * fx + s2 * fy + s3 * fz
    lengths = jnp.sqrt(s1 * s1 + s2 * s2 + s3 * s3) * jnp.sqrt(fx * fx + fy * fy + fz * fz)
    cosine = dot / jnp.maximum(lengths, 1.0)
    scaled = (cosine + 1.0) * offsets[NBIN + 1 : NBIN + 2, :]
    strength = s0 * field
    ramps = [
        jnp.clip(scaled - offsets[b : b + 1, :], 0.0, 1.0) * strength for b in range(NBIN + 1)
    ]
    for b in range(NBIN):
        emit(b, ramps[b] - ramps[b + 1])


def clear_pads(ref, width):
    rows, _, depth = ref.shape
    zeros = jnp.zeros((rows, YPAD, depth), jnp.float32)
    ref[:, :YPAD, :] = zeros
    ref[:, YPAD + width :, :] = zeros


def place(dst_p, dst_q, centre, sides, width):
    rows = centre.shape[1]
    inner = pl.ds(YPAD, width)
    dst_p[pl.ds(HALO, rows), inner, :] = centre[0]
    dst_q[pl.ds(HALO, rows)] = centre[1]
    for at, read in sides:
        dst_p[pl.ds(at, HALO), inner, :] = read(0, HALO)
        dst_q[pl.ds(at, HALO)] = read(HALO, HALO)


def side_starts(rows, reach):
    odd = lax.rem(lax.axis_index("gx"), 2)
    on_chip = jnp.where(odd == 1, 0, rows + reach)
    off_chip = jnp.where(odd == 1, rows + reach, 0)
    return on_chip, off_chip


def has_far_side():
    at = lax.axis_index("gx")
    return (at > 0) & (at < lax.axis_size("gx") - 1)


def two_steps(
    t, rows, width, waves, own, first_prev, coeffs, inject, matrices, scratch, mid_emit, emit, second_prev
):
    p, q = waves
    slope_p, slope_q, curve_p, curve_q, p1, q1 = scratch
    inner = slice(YPAD, YPAD + width)
    clear_pads(p1, width)
    for dst, src in zip((slope_p, slope_q, curve_p, curve_q), own):
        dst[pl.ds(HALO, rows)] = src

    def read_p(start, size):
        return p[pl.ds(start, size), inner, :]

    def read_q(start, size):
        return q[pl.ds(start, size)]

    for begin in (0, rows + HALO):
        depth_rows(read_p, slope_p, curve_p, begin, HALO, width, matrices)
        depth_rows(read_q, slope_q, curve_q, begin, HALO, width, matrices)

    def keep(row, next_p, next_q):
        p1[row, inner, :] = next_p
        q1[row] = next_q
        mid_emit(row, next_p, next_q)

    ext = rows + 2 * REACH
    time_step(
        ext,
        width,
        waves,
        first_prev,
        lambda row: [coeffs[c, row] for c in range(5)],
        (slope_p, slope_q),
        (curve_p, curve_q),
        lambda row: inject[t, row],
        keep,
    )
    depth_rows(lambda b, n: p1[pl.ds(b, n), inner, :], slope_p, curve_p, 0, ext, width, matrices)
    depth_rows(lambda b, n: q1[pl.ds(b, n)], slope_q, curve_q, 0, ext, width, matrices)
    time_step(
        rows,
        width,
        (p1, q1),
        second_prev,
        lambda row: [coeffs[c, row + REACH] for c in range(5)],
        (slope_p, slope_q),
        (curve_p, curve_q),
        lambda row: inject[t + 1, row + REACH],
        emit,
    )


def pack_kernel(now, prev, speed, epsilon, delta, tilt, far, near, sems):
    rows = now.shape[1]
    odd = lax.rem(lax.axis_index("gx"), 2)
    copies = []

    def copy(src, dst):
        copies.append(pltpu.make_async_copy(src, dst, sems.at[len(copies)]))
        copies[-1].start()

    for out, tail in ((far, odd), (near, 1 - odd)):
        wave_at = tail * (rows - HALO)
        edge_at = tail * (rows - REACH)
        for f in range(2):
            copy(now.at[f, pl.ds(wave_at, HALO)], out.at[pl.ds(f * HALO, HALO)])
        for f in range(2):
            copy(
                prev.at[f, pl.ds(edge_at, REACH)],
                out.at[pl.ds(2 * HALO + f * REACH, REACH)],
            )
        for m, field in enumerate((speed, epsilon, delta, tilt)):
            copy(
                field.at[pl.ds(edge_at, REACH)],
                out.at[pl.ds(2 * HALO + (2 + m) * REACH, REACH)],
            )
    for one in copies:
        one.wait()


def prep_kernel(
    now,
    speed,
    epsilon,
    delta,
    tilt,
    receiver_row,
    receiver_column,
    traces,
    table,
    matrices,
    coeffs,
    inject,
    slopes,
    curves,
    offsets,
):
    rows, width, depth = speed.shape
    each_row(
        rows,
        width,
        lambda r: derive(coeffs, r, speed[r], epsilon[r], delta[r], tilt[r]),
    )
    for f in range(2):
        depth_rows(
            lambda b, n: now[f, pl.ds(b, n)], slopes.at[f], curves.at[f], 0, rows, width, matrices
        )
    flat = receivers(receiver_row, receiver_column, rows, width)

    def samples(row):
        cell = lax.broadcasted_iota(jnp.int32, (width, flat.shape[1]), 0) + row * width
        lane = lax.broadcasted_iota(jnp.int32, (width, depth), 1)
        hit = cell == flat
        for t in range(STEPS):
            column = jnp.sum(jnp.where(hit, traces[t : t + 1, :], 0.0), axis=1, keepdims=True)
            inject[t, row] = jnp.where(lane == REC_DEPTH, column, 0.0)

    each_row(rows + 2 * REACH, width, samples)
    fine = table.shape[0]
    starts = [jnp.int32(0)] * NBIN
    for f in range(fine):
        named = table[f]
        for b in range(1, NBIN):
            starts[b] = starts[b] + (named < b).astype(jnp.int32)
    values = [s.astype(jnp.float32) - 1.0 for s in starts]
    values = values + [jnp.float32(fine - 1), jnp.float32(0.5 * (fine - 1))]
    for b, value in enumerate(values):
        offsets[b : b + 1, :] = jnp.full((1, depth), value, jnp.float32)


def early_kernel(
    now,
    prev,
    on_chip,
    off_chip,
    own_coeffs,
    inject,
    slopes,
    curves,
    matrices,
    out,
    mid,
    coeffs,
    slope_out,
    p,
    q,
    prev_ext,
    *scratch,
):
    rows, width = now.shape[1], now.shape[2]
    near, far = side_starts(rows, HALO)
    inside = has_far_side()
    clear_pads(p, width)
    place(
        p,
        q,
        now,
        (
            (near, lambda a, n: on_chip[pl.ds(a, n)]),
            (far, lambda a, n: jnp.where(inside, off_chip[pl.ds(a, n)], 0.0)),
        ),
        width,
    )
    near, far = side_starts(rows, REACH)
    base = 2 * HALO
    for c in range(5):
        coeffs[c, pl.ds(REACH, rows)] = own_coeffs[c]
    for f in range(2):
        prev_ext[f, pl.ds(REACH, rows)] = prev[f]
    for at, part, real in ((near, on_chip, True), (far, off_chip, inside)):

        def only_real(value, real=real):
            return value if real is True else jnp.where(real, value, 0.0)

        for f in range(2):
            prev_ext[f, pl.ds(at, REACH)] = only_real(part[pl.ds(base + f * REACH, REACH)])
        for r in range(REACH):
            fields = [part[base + (2 + m) * REACH + r] for m in range(4)]
            derive(coeffs, at + r, only_real(fields[0]), *fields[1:])

    def mid_emit(row, next_p, next_q):
        mid[0, row] = next_p
        mid[1, row] = next_q

    def emit(row, next_p, next_q):
        out[0, row] = next_p
        out[1, row] = next_q

    two_steps(
        0,
        rows,
        width,
        (p, q),
        (slopes[0], slopes[1], curves[0], curves[1]),
        lambda row: (prev_ext[0, row], prev_ext[1, row]),
        coeffs,
        inject,
        matrices,
        scratch,
        mid_emit,
        emit,
        lambda row: (now[0, row], now[1, row]),
    )
    slope_out[...] = scratch[0][pl.ds(REACH, rows)]


def side_kernel(before, mid, slope_z, now, matrices, flux, slopes, curves, p1):
    rows, width = before.shape[1], before.shape[2]
    clear_pads(p1, width)
    p1[:, YPAD : YPAD + width, :] = mid[0]

    def fluxes(row):
        _, parts = flux_row(row, width, p1, slope_z[row], before[0, row])
        for a in range(3):
            flux[a, row] = parts[a]

    each_row(rows, width, fluxes)
    for f in range(2):
        depth_rows(
            lambda b, n: now[f, pl.ds(b, n)], slopes.at[f], curves.at[f], 0, rows, width, matrices
        )


def first_image_kernel(source, mid, flux, offsets, images):
    rows, width = flux.shape[1], flux.shape[2]

    def image_row(row):
        def emit(b, term):
            images[b, row] = term

        image_terms(
            source, 0, row, mid[0, row + REACH], [flux[a, row] for a in range(3)], offsets, emit
        )

    each_row(rows, width, image_row)


def late_kernel(
    now,
    mid,
    coeffs,
    on_chip,
    off_chip,
    inject,
    slopes,
    curves,
    matrices,
    source,
    offsets,
    partial_images,
    images,
    out,
    p,
    q,
    *scratch,
):
    rows, width = now.shape[1], now.shape[2]
    near, far = side_starts(rows, HALO)
    inside = has_far_side()
    clear_pads(p, width)
    place(
        p,
        q,
        now,
        (
            (near, lambda a, n: on_chip[a // HALO]),
            (far, lambda a, n: jnp.where(inside, off_chip[a // HALO], 0.0)),
        ),
        width,
    )

    def emit(row, next_p, next_q):
        out[0, row] = next_p
        out[1, row] = next_q

    two_steps(
        2,
        rows,
        width,
        (p, q),
        (slopes[0], slopes[1], curves[0], curves[1]),
        lambda row: (mid[0, row], mid[1, row]),
        coeffs,
        inject,
        matrices,
        scratch,
        lambda row, next_p, next_q: None,
        emit,
        lambda row: (now[0, row], now[1, row]),
    )
    slope_z, p1 = scratch[0], scratch[4]

    def image_row(row):
        field, flux = flux_row(row, width, p1, slope_z[row + REACH], now[0, row])

        def finish(b, term):
            images[b, row] = (partial_images[b, row] + term).astype(images.dtype)

        image_terms(source, 1, row, field, flux, offsets, finish)

    each_row(rows, width, image_row)


def local(
    wave_now,
    wave_prev,
    speed_term,
    thomsen_epsilon,
    thomsen_delta,
    tilt_angle,
    source_store,
    receiver_row,
    receiver_column,
    receiver_traces,
    angle_table,
):
    _, rows, width, depth = wave_now.shape
    count = lax.axis_size("gx")
    odd = lax.rem(lax.axis_index("gx"), 2)
    on_chip_pairs = [(i, i ^ 1) for i in range(count)]
    both_axes = ("shot", "gx")
    shots = lax.axis_size("shot")
    off_chip_pairs = []
    for shot in range(shots):
        at = shot * count
        for i in range(1, count - 1, 2):
            off_chip_pairs += [(at + i, at + i + 1), (at + i + 1, at + i)]
        other = ((shot + 1) % shots) * count
        if shots > 1:
            off_chip_pairs += [(at, other), (at + count - 1, other + count - 1)]

    f32 = jnp.float32
    ext, wide = rows + 2 * REACH, rows + 2 * HALO
    vmem = pl.BlockSpec(memory_space=pltpu.VMEM)
    smem = pl.BlockSpec(memory_space=pltpu.SMEM)
    in_hbm = pl.BlockSpec(memory_space=pltpu.HBM)
    plane = (width, depth)
    padded = (width + 2 * YPAD, depth)
    plane_bytes = 4 * width * depth
    line_flops = width * depth

    def planes(*lead):
        return jax.ShapeDtypeStruct(lead + plane, f32)

    def call(kernel, outs, ins, in_specs, scratch, grant, cost):
        return pl.pallas_call(
            kernel,
            out_shape=outs,
            in_specs=in_specs,
            out_specs=jax.tree.map(lambda _: vmem, outs),
            scratch_shapes=scratch,
            compiler_params=pltpu.CompilerParams(
                vmem_limit_bytes=4 * 1024 * 1024 + grant * plane_bytes
            ),
            cost_estimate=pl.CostEstimate(
                flops=cost * line_flops, bytes_accessed=cost * line_flops // 4, transcendentals=0
            ),
        )(*ins)

    step_scratch = [
        pltpu.VMEM((wide,) + plane, f32),
        pltpu.VMEM((wide,) + plane, f32),
        pltpu.VMEM((wide,) + plane, f32),
        pltpu.VMEM((wide,) + plane, f32),
        pltpu.VMEM((ext,) + padded, f32),
        pltpu.VMEM((ext,) + plane, f32),
    ]
    wave_scratch = [pltpu.VMEM((wide,) + padded, f32), pltpu.VMEM((wide,) + plane, f32)]
    medium = (speed_term, thomsen_epsilon, thomsen_delta, tilt_angle)
    matrices = jnp.asarray(depth_matrices(depth))

    packed = planes(2 * HALO + 6 * REACH)
    far_pack, near_pack = call(
        pack_kernel,
        (packed, packed),
        [
            pltpu.with_memory_space_constraint(x, pltpu.HBM)
            for x in (wave_now, wave_prev, *medium)
        ],
        [in_hbm] * 6,
        [pltpu.SemaphoreType.DMA((16,))],
        80,
        200,
    )
    off_chip = lax.ppermute(far_pack, both_axes, off_chip_pairs)
    on_chip = lax.ppermute(near_pack, "gx", on_chip_pairs)
    arrived = lax.all_to_all(source_store, "gx", split_axis=2, concat_axis=3, tiled=True)
    own_coeffs, inject, slopes, curves, offsets = call(
        prep_kernel,
        (
            planes(5, rows),
            planes(STEPS, ext),
            planes(2, rows),
            planes(2, rows),
            jax.ShapeDtypeStruct((16, depth), f32),
        ),
        (wave_now, *medium, receiver_row, receiver_column, receiver_traces, angle_table, matrices),
        [vmem] * 8 + [smem, vmem],
        [],
        20 * wide,
        60 * rows,
    )
    now, mid, coeffs, slope_z = call(
        early_kernel,
        (planes(2, rows), planes(2, ext), planes(5, ext), planes(rows)),
        (wave_now, wave_prev, on_chip, off_chip, own_coeffs, inject, slopes, curves, matrices),
        [vmem] * 9,
        wave_scratch + [pltpu.VMEM((2, ext) + plane, f32)] + step_scratch,
        30 * wide,
        400 * rows,
    )

    def side(tail):
        if rows == HALO:
            return now
        return lax.dynamic_slice_in_dim(now, jnp.where(tail, rows - HALO, 0), HALO, axis=1)

    off_chip = lax.ppermute(side(odd == 1), both_axes, off_chip_pairs)
    on_chip = lax.ppermute(side(odd == 0), "gx", on_chip_pairs)
    flux, slopes, curves = call(
        side_kernel,
        (planes(3, rows), planes(2, rows), planes(2, rows)),
        (wave_now, mid, slope_z, now, matrices),
        [vmem] * 5,
        [pltpu.VMEM((ext,) + padded, f32)],
        12 * wide,
        60 * rows,
    )
    partial_images = call(
        first_image_kernel,
        planes(NBIN, rows),
        (arrived, mid, flux, offsets),
        [vmem] * 4,
        [],
        16 * wide,
        60 * rows,
    )
    images, final = call(
        late_kernel,
        (jax.ShapeDtypeStruct((NBIN, rows) + plane, jnp.bfloat16), planes(2, rows)),
        (
            now,
            mid,
            coeffs,
            on_chip,
            off_chip,
            inject,
            slopes,
            curves,
            matrices,
            arrived,
            offsets,
            partial_images,
        ),
        [vmem] * 12,
        wave_scratch + step_scratch,
        34 * wide,
        500 * rows,
    )
    return images, final


def solution(mesh):
    placed = (
        P("shot", "gx", None, None),
        P("shot", "gx", None, None),
        P("gx", None, None),
        P("gx", None, None),
        P("gx", None, None),
        P("gx", None, None),
        P("shot", None, None, "gx", None),
        P("shot"),
        P("shot"),
        P("shot", None),
        P(),
    )
    return jax.shard_map(
        local,
        mesh=mesh,
        in_specs=placed,
        out_specs=(P("shot", "gx", None, None), P("shot", "gx", None, None)),
        check_vma=False,
    )
```

```python
import jax
import jax.numpy as jnp
import numpy as np
from jax import lax
from jax.experimental import pallas as pl
from jax.experimental.pallas import tpu as pltpu
from jax.sharding import PartitionSpec as P


STEPS = 4
NBIN = 8
REC_DEPTH = 2
REACH = 4
HALO = 2 * REACH
YPAD = 8

SECOND = (-205.0 / 72.0, 8.0 / 5.0, -1.0 / 5.0, 8.0 / 315.0, -1.0 / 560.0)
FIRST = (4.0 / 5.0, -1.0 / 5.0, 4.0 / 105.0, -1.0 / 280.0)


def each_row(count, width, body):
    if width <= 16:
        for row in range(count):
            body(row)
    else:
        lax.fori_loop(0, count, lambda row, carry: (body(row), carry)[1], 0)


def each_chunk(count, width, body):
    size = max(1, min(count, 512 // width))
    while count % size:
        size -= 1
    if count // size <= 2:
        for start in range(0, count, size):
            body(start, size)
    else:
        lax.fori_loop(0, count // size, lambda i, carry: (body(i * size, size), carry)[1], 0)


def second(centre, pairs):
    total = SECOND[0] * centre
    for k in range(1, 5):
        plus, minus = pairs(k)
        total = total + SECOND[k] * (plus + minus)
    return total


def first(pairs):
    total = None
    for k in range(1, 5):
        plus, minus = pairs(k)
        term = FIRST[k - 1] * (plus - minus)
        total = term if total is None else total + term
    return total


def depth_matrices(depth):
    eye = [np.eye(depth, k=k, dtype=np.float64) for k in range(-4, 5)]
    slope = sum(np.float32(FIRST[k - 1]) * (eye[4 - k] - eye[4 + k]) for k in range(1, 5))
    curve = np.float32(SECOND[0]) * eye[4] + sum(
        np.float32(SECOND[k]) * (eye[4 - k] + eye[4 + k]) for k in range(1, 5)
    )
    rest = np.concatenate([slope, curve], axis=1).astype(np.float32)
    parts = []
    for _ in range(3):
        parts.append(rest.astype(jnp.bfloat16))
        rest = rest - parts[-1].astype(np.float32)
    return np.stack(parts)


def depth_diffs(field, matrices):
    depth = field.shape[1]
    high = field.astype(jnp.bfloat16)
    rest = field - high.astype(jnp.float32)
    middle = rest.astype(jnp.bfloat16)
    low = (rest - middle.astype(jnp.float32)).astype(jnp.bfloat16)
    m_high, m_middle, m_low = matrices[0], matrices[1], matrices[2]

    def product(left, top, bottom):
        return jnp.dot(
            left, jnp.concatenate([top, bottom], axis=0), preferred_element_type=jnp.float32
        )

    upper = jnp.concatenate([high, middle], axis=1)
    lower = jnp.concatenate([high, low], axis=1)
    both = (
        product(lower, m_low, m_high)
        + product(upper, m_middle, m_middle)
        + product(upper, m_high, m_high)
    )
    return both[:, :depth], both[:, depth:]


def depth_rows(read, slope, curve, begin, count, width, matrices, shift=0):
    def chunk(start, size):
        field = read(begin + start, size)
        depth = field.shape[-1]
        s, c = depth_diffs(field.reshape(size * width, depth), matrices)
        slope[pl.ds(begin + shift + start, size)] = s.reshape(size, width, depth)
        curve[pl.ds(begin + shift + start, size)] = c.reshape(size, width, depth)

    each_chunk(count, width, chunk)


def sine_terms(angle):
    half = 0.5 * angle
    sq = half * half
    s = 1.0
    for n in (12 * 13, 10 * 11, 8 * 9, 6 * 7, 4 * 5, 2 * 3):
        s = 1.0 - sq * s * (1.0 / n)
    s = s * half
    c = 1.0
    for n in (13 * 14, 11 * 12, 9 * 10, 7 * 8, 5 * 6, 3 * 4, 1 * 2):
        c = 1.0 - sq * c * (1.0 / n)
    sine = 2.0 * s * c
    cosine = 1.0 - 2.0 * s * s
    return sine * sine, 2.0 * sine * cosine


def derive(coeffs, at, s, e, d, a):
    coeffs[0, at] = s
    coeffs[1, at] = s * (1.0 + 2.0 * e)
    coeffs[2, at] = s * jnp.sqrt(1.0 + 2.0 * d)
    coeffs[3, at], coeffs[4, at] = sine_terms(a)


def receivers(row_ref, column_ref, rows, width):
    begin = lax.axis_index("gx") * rows - REACH
    count = row_ref.shape[0]
    local_row = row_ref[...].reshape(1, count) - begin
    inside = (local_row >= 0) & (local_row < rows + 2 * REACH)
    return jnp.where(inside, local_row * width + column_ref[...].reshape(1, count), -1)


def time_step(rows, width, fields, earlier, coeffs, slopes, curves, inject, emit):
    p, q = fields
    slope_p, slope_q = slopes
    curve_p, curve_q = curves
    inner = slice(YPAD, YPAD + width)

    def update(row):
        at = row + REACH
        now_p = p[at, inner, :]
        now_q = q[at]
        xx_p = second(now_p, lambda k: (p[at + k, inner, :], p[at - k, inner, :]))
        xx_q = second(now_q, lambda k: (q[at + k], q[at - k]))
        xz_p = first(lambda k: (slope_p[at + k], slope_p[at - k]))
        xz_q = first(lambda k: (slope_q[at + k], slope_q[at - k]))
        yy_p = second(
            now_p,
            lambda k: (
                p[at, YPAD + k : YPAD + k + width, :],
                p[at, YPAD - k : YPAD - k + width, :],
            ),
        )
        speed, gain, mixed, sine_sq, sine_double = coeffs(row)
        tilt_p = sine_sq * (xx_p - curve_p[at]) + sine_double * xz_p
        tilt_q = sine_sq * (xx_q - curve_q[at]) + sine_double * xz_q
        across = xx_p + yy_p - tilt_p
        rotated = curve_q[at] + tilt_q
        prev_p, prev_q = earlier(row)
        next_p = 2.0 * now_p - prev_p + (gain * across + mixed * rotated)
        next_q = 2.0 * now_q - prev_q + (mixed * across + speed * rotated)
        emit(row, next_p + inject(row), next_q)

    each_row(rows, width, update)


def flux_row(row, width, p, slope_z, before):
    at = row + REACH
    now = p[at, YPAD : YPAD + width, :]
    back = before - now
    slope_x = first(
        lambda k: (p[at + k, YPAD : YPAD + width, :], p[at - k, YPAD : YPAD + width, :])
    )
    slope_y = first(
        lambda k: (p[at, YPAD + k : YPAD + k + width, :], p[at, YPAD - k : YPAD - k + width, :])
    )
    return now, (back * slope_x, back * slope_y, back * slope_z)


def image_terms(source, n, row, field, flux, offsets, emit):
    fx, fy, fz = flux
    s0, s1, s2, s3 = [source[n, c, row].astype(jnp.float32) for c in range(4)]
    dot = s1 * fx + s2 * fy + s3 * fz
    lengths = jnp.sqrt(s1 * s1 + s2 * s2 + s3 * s3) * jnp.sqrt(fx * fx + fy * fy + fz * fz)
    cosine = dot / jnp.maximum(lengths, 1.0)
    scaled = (cosine + 1.0) * offsets[NBIN + 1 : NBIN + 2, :]
    strength = s0 * field
    ramps = [
        jnp.clip(scaled - offsets[b : b + 1, :], 0.0, 1.0) * strength for b in range(NBIN + 1)
    ]
    for b in range(NBIN):
        emit(b, ramps[b] - ramps[b + 1])


def clear_pads(ref, width):
    rows, _, depth = ref.shape
    zeros = jnp.zeros((rows, YPAD, depth), jnp.float32)
    ref[:, :YPAD, :] = zeros
    ref[:, YPAD + width :, :] = zeros


def place(dst_p, dst_q, centre, sides, width):
    rows = centre.shape[1]
    inner = pl.ds(YPAD, width)
    dst_p[pl.ds(HALO, rows), inner, :] = centre[0]
    dst_q[pl.ds(HALO, rows)] = centre[1]
    for at, read in sides:
        dst_p[pl.ds(at, HALO), inner, :] = read(0, HALO)
        dst_q[pl.ds(at, HALO)] = read(HALO, HALO)


def side_starts(rows, reach):
    odd = lax.rem(lax.axis_index("gx"), 2)
    on_chip = jnp.where(odd == 1, 0, rows + reach)
    off_chip = jnp.where(odd == 1, rows + reach, 0)
    return on_chip, off_chip


def has_far_side():
    at = lax.axis_index("gx")
    return (at > 0) & (at < lax.axis_size("gx") - 1)


def two_steps(
    t, rows, width, waves, own, first_prev, coeffs, inject, matrices, scratch, mid_emit, emit, second_prev
):
    p, q = waves
    slope_p, slope_q, curve_p, curve_q, p1, q1 = scratch
    inner = slice(YPAD, YPAD + width)
    clear_pads(p1, width)
    for dst, src in zip((slope_p, slope_q, curve_p, curve_q), own):
        dst[pl.ds(HALO, rows)] = src

    def read_p(start, size):
        return p[pl.ds(start, size), inner, :]

    def read_q(start, size):
        return q[pl.ds(start, size)]

    for begin in (0, rows + HALO):
        depth_rows(read_p, slope_p, curve_p, begin, HALO, width, matrices)
        depth_rows(read_q, slope_q, curve_q, begin, HALO, width, matrices)

    def keep(row, next_p, next_q):
        p1[row, inner, :] = next_p
        q1[row] = next_q
        mid_emit(row, next_p, next_q)

    ext = rows + 2 * REACH
    time_step(
        ext,
        width,
        waves,
        first_prev,
        lambda row: [coeffs[c, row] for c in range(5)],
        (slope_p, slope_q),
        (curve_p, curve_q),
        lambda row: inject[t, row],
        keep,
    )
    depth_rows(lambda b, n: p1[pl.ds(b, n), inner, :], slope_p, curve_p, 0, ext, width, matrices)
    depth_rows(lambda b, n: q1[pl.ds(b, n)], slope_q, curve_q, 0, ext, width, matrices)
    time_step(
        rows,
        width,
        (p1, q1),
        second_prev,
        lambda row: [coeffs[c, row + REACH] for c in range(5)],
        (slope_p, slope_q),
        (curve_p, curve_q),
        lambda row: inject[t + 1, row + REACH],
        emit,
    )


def pack_kernel(now, prev, speed, epsilon, delta, tilt, source, far, near, sorted_source, sems):
    rows = now.shape[1]
    odd = lax.rem(lax.axis_index("gx"), 2)
    copies = []

    def copy(src, dst):
        copies.append(pltpu.make_async_copy(src, dst, sems.at[len(copies)]))
        copies[-1].start()

    for out, tail in ((far, odd), (near, 1 - odd)):
        wave_at = tail * (rows - HALO)
        edge_at = tail * (rows - REACH)
        for f in range(2):
            copy(now.at[f, pl.ds(wave_at, HALO)], out.at[pl.ds(f * HALO, HALO)])
        for f in range(2):
            copy(
                prev.at[f, pl.ds(edge_at, REACH)],
                out.at[pl.ds(2 * HALO + f * REACH, REACH)],
            )
        for m, field in enumerate((speed, epsilon, delta, tilt)):
            copy(
                field.at[pl.ds(edge_at, REACH)],
                out.at[pl.ds(2 * HALO + (2 + m) * REACH, REACH)],
            )
    for n in range(source.shape[0]):
        for c in range(source.shape[1]):
            copy(source.at[n, c], sorted_source.at[:, n, c])
    for one in copies:
        one.wait()


def prep_kernel(
    now,
    speed,
    epsilon,
    delta,
    tilt,
    receiver_row,
    receiver_column,
    traces,
    table,
    matrices,
    coeffs,
    inject,
    slopes,
    curves,
    offsets,
):
    rows, width, depth = speed.shape
    each_row(
        rows,
        width,
        lambda r: derive(coeffs, r, speed[r], epsilon[r], delta[r], tilt[r]),
    )
    for f in range(2):
        depth_rows(
            lambda b, n: now[f, pl.ds(b, n)], slopes.at[f], curves.at[f], 0, rows, width, matrices
        )
    flat = receivers(receiver_row, receiver_column, rows, width)

    def samples(row):
        cell = lax.broadcasted_iota(jnp.int32, (width, flat.shape[1]), 0) + row * width
        lane = lax.broadcasted_iota(jnp.int32, (width, depth), 1)
        hit = cell == flat
        for t in range(STEPS):
            column = jnp.sum(jnp.where(hit, traces[t : t + 1, :], 0.0), axis=1, keepdims=True)
            inject[t, row] = jnp.where(lane == REC_DEPTH, column, 0.0)

    each_row(rows + 2 * REACH, width, samples)
    fine = table.shape[0]
    starts = [jnp.int32(0)] * NBIN
    for f in range(fine):
        named = table[f]
        for b in range(1, NBIN):
            starts[b] = starts[b] + (named < b).astype(jnp.int32)
    values = [s.astype(jnp.float32) - 1.0 for s in starts]
    values = values + [jnp.float32(fine - 1), jnp.float32(0.5 * (fine - 1))]
    for b, value in enumerate(values):
        offsets[b : b + 1, :] = jnp.full((1, depth), value, jnp.float32)


def early_kernel(
    now,
    prev,
    on_chip,
    off_chip,
    own_coeffs,
    inject,
    slopes,
    curves,
    matrices,
    out,
    mid,
    coeffs,
    slope_out,
    p,
    q,
    prev_ext,
    *scratch,
):
    rows, width = now.shape[1], now.shape[2]
    near, far = side_starts(rows, HALO)
    inside = has_far_side()
    clear_pads(p, width)
    place(
        p,
        q,
        now,
        (
            (near, lambda a, n: on_chip[pl.ds(a, n)]),
            (far, lambda a, n: jnp.where(inside, off_chip[pl.ds(a, n)], 0.0)),
        ),
        width,
    )
    near, far = side_starts(rows, REACH)
    base = 2 * HALO
    for c in range(5):
        coeffs[c, pl.ds(REACH, rows)] = own_coeffs[c]
    for f in range(2):
        prev_ext[f, pl.ds(REACH, rows)] = prev[f]
    for at, part, real in ((near, on_chip, True), (far, off_chip, inside)):

        def only_real(value, real=real):
            return value if real is True else jnp.where(real, value, 0.0)

        for f in range(2):
            prev_ext[f, pl.ds(at, REACH)] = only_real(part[pl.ds(base + f * REACH, REACH)])
        for r in range(REACH):
            fields = [part[base + (2 + m) * REACH + r] for m in range(4)]
            derive(coeffs, at + r, only_real(fields[0]), *fields[1:])

    def mid_emit(row, next_p, next_q):
        mid[0, row] = next_p
        mid[1, row] = next_q

    def emit(row, next_p, next_q):
        out[0, row] = next_p
        out[1, row] = next_q

    two_steps(
        0,
        rows,
        width,
        (p, q),
        (slopes[0], slopes[1], curves[0], curves[1]),
        lambda row: (prev_ext[0, row], prev_ext[1, row]),
        coeffs,
        inject,
        matrices,
        scratch,
        mid_emit,
        emit,
        lambda row: (now[0, row], now[1, row]),
    )
    slope_out[...] = scratch[0][pl.ds(REACH, rows)]


def side_kernel(before, mid, slope_z, now, matrices, flux, slopes, curves, p1):
    rows, width = before.shape[1], before.shape[2]
    clear_pads(p1, width)
    p1[:, YPAD : YPAD + width, :] = mid[0]

    def fluxes(row):
        _, parts = flux_row(row, width, p1, slope_z[row], before[0, row])
        for a in range(3):
            flux[a, row] = parts[a]

    each_row(rows, width, fluxes)
    for f in range(2):
        depth_rows(
            lambda b, n: now[f, pl.ds(b, n)], slopes.at[f], curves.at[f], 0, rows, width, matrices
        )


def late_kernel(
    now,
    mid,
    coeffs,
    on_chip,
    off_chip,
    inject,
    slopes,
    curves,
    matrices,
    out,
    imaged,
    p,
    q,
    *scratch,
):
    rows, width = now.shape[1], now.shape[2]
    near, far = side_starts(rows, HALO)
    inside = has_far_side()
    clear_pads(p, width)
    place(
        p,
        q,
        now,
        (
            (near, lambda a, n: on_chip[a // HALO]),
            (far, lambda a, n: jnp.where(inside, off_chip[a // HALO], 0.0)),
        ),
        width,
    )

    def emit(row, next_p, next_q):
        out[0, row] = next_p
        out[1, row] = next_q

    two_steps(
        2,
        rows,
        width,
        (p, q),
        (slopes[0], slopes[1], curves[0], curves[1]),
        lambda row: (mid[0, row], mid[1, row]),
        coeffs,
        inject,
        matrices,
        scratch,
        lambda row, next_p, next_q: None,
        emit,
        lambda row: (now[0, row], now[1, row]),
    )
    slope_z, p1 = scratch[0], scratch[4]

    def fluxes(row):
        field, parts = flux_row(row, width, p1, slope_z[row + REACH], now[0, row])
        for a, value in enumerate((field, *parts)):
            imaged[a, row] = value

    each_row(rows, width, fluxes)


def image_kernel(source, mid, flux, imaged, offsets, images):
    rows, width = flux.shape[1], flux.shape[2]

    def image_row(row):
        totals = [None] * NBIN

        def keep(b, term):
            totals[b] = term

        def finish(b, term):
            images[b, row] = (totals[b] + term).astype(images.dtype)

        early = [flux[a, row] for a in range(3)]
        image_terms(source, 0, row, mid[0, row + REACH], early, offsets, keep)
        late = [imaged[a, row] for a in range(1, 4)]
        image_terms(source, 1, row, imaged[0, row], late, offsets, finish)

    each_row(rows, width, image_row)


def local(
    wave_now,
    wave_prev,
    speed_term,
    thomsen_epsilon,
    thomsen_delta,
    tilt_angle,
    source_store,
    receiver_row,
    receiver_column,
    receiver_traces,
    angle_table,
):
    _, rows, width, depth = wave_now.shape
    count = lax.axis_size("gx")
    odd = lax.rem(lax.axis_index("gx"), 2)
    on_chip_pairs = [(i, i ^ 1) for i in range(count)]
    both_axes = ("shot", "gx")
    shots = lax.axis_size("shot")
    off_chip_pairs = []
    for shot in range(shots):
        at = shot * count
        for i in range(1, count - 1, 2):
            off_chip_pairs += [(at + i, at + i + 1), (at + i + 1, at + i)]
        other = ((shot + 1) % shots) * count
        if shots > 1:
            off_chip_pairs += [(at, other), (at + count - 1, other + count - 1)]

    f32 = jnp.float32
    ext, wide = rows + 2 * REACH, rows + 2 * HALO
    vmem = pl.BlockSpec(memory_space=pltpu.VMEM)
    smem = pl.BlockSpec(memory_space=pltpu.SMEM)
    in_hbm = pl.BlockSpec(memory_space=pltpu.HBM)
    plane = (width, depth)
    padded = (width + 2 * YPAD, depth)
    plane_bytes = 4 * width * depth
    line_flops = width * depth

    def planes(*lead):
        return jax.ShapeDtypeStruct(lead + plane, f32)

    def call(kernel, outs, ins, in_specs, scratch, grant, cost):
        return pl.pallas_call(
            kernel,
            out_shape=outs,
            in_specs=in_specs,
            out_specs=jax.tree.map(lambda _: vmem, outs),
            scratch_shapes=scratch,
            compiler_params=pltpu.CompilerParams(
                vmem_limit_bytes=4 * 1024 * 1024 + grant * plane_bytes
            ),
            cost_estimate=pl.CostEstimate(
                flops=cost * line_flops, bytes_accessed=cost * line_flops // 4, transcendentals=0
            ),
        )(*ins)

    step_scratch = [
        pltpu.VMEM((wide,) + plane, f32),
        pltpu.VMEM((wide,) + plane, f32),
        pltpu.VMEM((wide,) + plane, f32),
        pltpu.VMEM((wide,) + plane, f32),
        pltpu.VMEM((ext,) + padded, f32),
        pltpu.VMEM((ext,) + plane, f32),
    ]
    wave_scratch = [pltpu.VMEM((wide,) + padded, f32), pltpu.VMEM((wide,) + plane, f32)]
    medium = (speed_term, thomsen_epsilon, thomsen_delta, tilt_angle)
    matrices = jnp.asarray(depth_matrices(depth))

    packed = planes(2 * HALO + 6 * REACH)
    snaps, parts = source_store.shape[:2]
    by_owner = source_store.reshape(snaps, parts, count, rows, depth)
    far_pack, near_pack, sorted_source = call(
        pack_kernel,
        (
            packed,
            packed,
            jax.ShapeDtypeStruct((count, snaps, parts, rows, depth), source_store.dtype),
        ),
        [
            pltpu.with_memory_space_constraint(x, pltpu.HBM)
            for x in (wave_now, wave_prev, *medium, by_owner)
        ],
        [in_hbm] * 7,
        [pltpu.SemaphoreType.DMA((16 + snaps * parts,))],
        120,
        200,
    )
    off_chip = lax.ppermute(far_pack, both_axes, off_chip_pairs)
    on_chip = lax.ppermute(near_pack, "gx", on_chip_pairs)
    arrived = lax.all_to_all(sorted_source, "gx", split_axis=0, concat_axis=0, tiled=True)
    own_coeffs, inject, slopes, curves, offsets = call(
        prep_kernel,
        (
            planes(5, rows),
            planes(STEPS, ext),
            planes(2, rows),
            planes(2, rows),
            jax.ShapeDtypeStruct((16, depth), f32),
        ),
        (wave_now, *medium, receiver_row, receiver_column, receiver_traces, angle_table, matrices),
        [vmem] * 8 + [smem, vmem],
        [],
        20 * wide,
        60 * rows,
    )
    now, mid, coeffs, slope_z = call(
        early_kernel,
        (planes(2, rows), planes(2, ext), planes(5, ext), planes(rows)),
        (wave_now, wave_prev, on_chip, off_chip, own_coeffs, inject, slopes, curves, matrices),
        [vmem] * 9,
        wave_scratch + [pltpu.VMEM((2, ext) + plane, f32)] + step_scratch,
        30 * wide,
        400 * rows,
    )

    def side(tail):
        if rows == HALO:
            return now
        return lax.dynamic_slice_in_dim(now, jnp.where(tail, rows - HALO, 0), HALO, axis=1)

    off_chip = lax.ppermute(side(odd == 1), both_axes, off_chip_pairs)
    on_chip = lax.ppermute(side(odd == 0), "gx", on_chip_pairs)
    flux, slopes, curves = call(
        side_kernel,
        (planes(3, rows), planes(2, rows), planes(2, rows)),
        (wave_now, mid, slope_z, now, matrices),
        [vmem] * 5,
        [pltpu.VMEM((ext,) + padded, f32)],
        12 * wide,
        60 * rows,
    )
    final, imaged = call(
        late_kernel,
        (planes(2, rows), planes(4, rows)),
        (now, mid, coeffs, on_chip, off_chip, inject, slopes, curves, matrices),
        [vmem] * 9,
        wave_scratch + step_scratch,
        30 * wide,
        400 * rows,
    )
    images = call(
        image_kernel,
        jax.ShapeDtypeStruct((NBIN, rows) + plane, jnp.bfloat16),
        (jnp.transpose(arrived, (1, 2, 3, 0, 4)), mid, flux, imaged, offsets),
        [vmem] * 5,
        [],
        16 * wide,
        60 * rows,
    )
    return images, final


def solution(mesh):
    placed = (
        P("shot", "gx", None, None),
        P("shot", "gx", None, None),
        P("gx", None, None),
        P("gx", None, None),
        P("gx", None, None),
        P("gx", None, None),
        P("shot", None, None, "gx", None),
        P("shot"),
        P("shot"),
        P("shot", None),
        P(),
    )
    return jax.shard_map(
        local,
        mesh=mesh,
        in_specs=placed,
        out_specs=(P("shot", "gx", None, None), P("shot", "gx", None, None)),
        check_vma=False,
    )
```

```python
import jax
import jax.numpy as jnp
import numpy as np
from jax import lax
from jax.experimental import pallas as pl
from jax.experimental.pallas import tpu as pltpu
from jax.sharding import PartitionSpec as P


STEPS = 4
NBIN = 8
REC_DEPTH = 2
REACH = 4
HALO = 2 * REACH
YPAD = 8
OUT_PIECES = 4

SECOND = (-205.0 / 72.0, 8.0 / 5.0, -1.0 / 5.0, 8.0 / 315.0, -1.0 / 560.0)
FIRST = (4.0 / 5.0, -1.0 / 5.0, 4.0 / 105.0, -1.0 / 280.0)


def each_row(count, width, body):
    if width <= 16:
        for row in range(count):
            body(row)
    else:
        lax.fori_loop(0, count, lambda row, carry: (body(row), carry)[1], 0)


def each_chunk(count, width, body):
    size = max(1, min(count, 512 // width))
    while count % size:
        size -= 1
    if count // size <= 2:
        for start in range(0, count, size):
            body(start, size)
    else:
        lax.fori_loop(0, count // size, lambda i, carry: (body(i * size, size), carry)[1], 0)


def second(centre, pairs):
    total = SECOND[0] * centre
    for k in range(1, 5):
        plus, minus = pairs(k)
        total = total + SECOND[k] * (plus + minus)
    return total


def first(pairs):
    total = None
    for k in range(1, 5):
        plus, minus = pairs(k)
        term = FIRST[k - 1] * (plus - minus)
        total = term if total is None else total + term
    return total


def depth_matrices(depth):
    eye = [np.eye(depth, k=k, dtype=np.float64) for k in range(-4, 5)]
    slope = sum(np.float32(FIRST[k - 1]) * (eye[4 - k] - eye[4 + k]) for k in range(1, 5))
    curve = np.float32(SECOND[0]) * eye[4] + sum(
        np.float32(SECOND[k]) * (eye[4 - k] + eye[4 + k]) for k in range(1, 5)
    )
    rest = np.concatenate([slope, curve], axis=1).astype(np.float32)
    parts = []
    for _ in range(3):
        parts.append(rest.astype(jnp.bfloat16))
        rest = rest - parts[-1].astype(np.float32)
    return np.stack(parts)


def depth_diffs(field, matrices):
    depth = field.shape[1]
    high = field.astype(jnp.bfloat16)
    rest = field - high.astype(jnp.float32)
    middle = rest.astype(jnp.bfloat16)
    low = (rest - middle.astype(jnp.float32)).astype(jnp.bfloat16)
    m_high, m_middle, m_low = matrices[0], matrices[1], matrices[2]

    def product(left, top, bottom):
        return jnp.dot(
            left, jnp.concatenate([top, bottom], axis=0), preferred_element_type=jnp.float32
        )

    upper = jnp.concatenate([high, middle], axis=1)
    lower = jnp.concatenate([high, low], axis=1)
    both = (
        product(lower, m_low, m_high)
        + product(upper, m_middle, m_middle)
        + product(upper, m_high, m_high)
    )
    return both[:, :depth], both[:, depth:]


def depth_rows(read, slope, curve, begin, count, width, matrices, shift=0):
    def chunk(start, size):
        field = read(begin + start, size)
        depth = field.shape[-1]
        s, c = depth_diffs(field.reshape(size * width, depth), matrices)
        slope[pl.ds(begin + shift + start, size)] = s.reshape(size, width, depth)
        curve[pl.ds(begin + shift + start, size)] = c.reshape(size, width, depth)

    each_chunk(count, width, chunk)


def sine_terms(angle):
    half = 0.5 * angle
    sq = half * half
    s = 1.0
    for n in (12 * 13, 10 * 11, 8 * 9, 6 * 7, 4 * 5, 2 * 3):
        s = 1.0 - sq * s * (1.0 / n)
    s = s * half
    c = 1.0
    for n in (13 * 14, 11 * 12, 9 * 10, 7 * 8, 5 * 6, 3 * 4, 1 * 2):
        c = 1.0 - sq * c * (1.0 / n)
    sine = 2.0 * s * c
    cosine = 1.0 - 2.0 * s * s
    return sine * sine, 2.0 * sine * cosine


def derive(coeffs, at, s, e, d, a):
    coeffs[0, at] = s
    coeffs[1, at] = s * (1.0 + 2.0 * e)
    coeffs[2, at] = s * jnp.sqrt(1.0 + 2.0 * d)
    coeffs[3, at], coeffs[4, at] = sine_terms(a)


def receivers(row_ref, column_ref, rows, width):
    begin = lax.axis_index("gx") * rows - REACH
    count = row_ref.shape[0]
    local_row = row_ref[...].reshape(1, count) - begin
    inside = (local_row >= 0) & (local_row < rows + 2 * REACH)
    return jnp.where(inside, local_row * width + column_ref[...].reshape(1, count), -1)


def time_step(rows, width, fields, earlier, coeffs, slopes, curves, inject, emit):
    p, q = fields
    slope_p, slope_q = slopes
    curve_p, curve_q = curves
    inner = slice(YPAD, YPAD + width)

    def update(row):
        at = row + REACH
        now_p = p[at, inner, :]
        now_q = q[at]
        xx_p = second(now_p, lambda k: (p[at + k, inner, :], p[at - k, inner, :]))
        xx_q = second(now_q, lambda k: (q[at + k], q[at - k]))
        xz_p = first(lambda k: (slope_p[at + k], slope_p[at - k]))
        xz_q = first(lambda k: (slope_q[at + k], slope_q[at - k]))
        yy_p = second(
            now_p,
            lambda k: (
                p[at, YPAD + k : YPAD + k + width, :],
                p[at, YPAD - k : YPAD - k + width, :],
            ),
        )
        speed, gain, mixed, sine_sq, sine_double = coeffs(row)
        tilt_p = sine_sq * (xx_p - curve_p[at]) + sine_double * xz_p
        tilt_q = sine_sq * (xx_q - curve_q[at]) + sine_double * xz_q
        across = xx_p + yy_p - tilt_p
        rotated = curve_q[at] + tilt_q
        prev_p, prev_q = earlier(row)
        next_p = 2.0 * now_p - prev_p + (gain * across + mixed * rotated)
        next_q = 2.0 * now_q - prev_q + (mixed * across + speed * rotated)
        emit(row, next_p + inject(row), next_q)

    each_row(rows, width, update)


def flux_row(row, width, p, slope_z, before):
    at = row + REACH
    now = p[at, YPAD : YPAD + width, :]
    back = before - now
    slope_x = first(
        lambda k: (p[at + k, YPAD : YPAD + width, :], p[at - k, YPAD : YPAD + width, :])
    )
    slope_y = first(
        lambda k: (p[at, YPAD + k : YPAD + k + width, :], p[at, YPAD - k : YPAD - k + width, :])
    )
    return now, (back * slope_x, back * slope_y, back * slope_z)


def image_terms(source, field, flux, offsets, emit):
    fx, fy, fz = flux
    s0, s1, s2, s3 = source
    dot = s1 * fx + s2 * fy + s3 * fz
    lengths = jnp.sqrt(s1 * s1 + s2 * s2 + s3 * s3) * jnp.sqrt(fx * fx + fy * fy + fz * fz)
    cosine = dot / jnp.maximum(lengths, 1.0)
    scaled = (cosine + 1.0) * offsets[NBIN + 1 : NBIN + 2, :]
    strength = s0 * field
    ramps = [
        jnp.clip(scaled - offsets[b : b + 1, :], 0.0, 1.0) * strength for b in range(NBIN + 1)
    ]
    for b in range(NBIN):
        emit(b, ramps[b] - ramps[b + 1])


def clear_pads(ref, width):
    rows, _, depth = ref.shape
    zeros = jnp.zeros((rows, YPAD, depth), jnp.float32)
    ref[:, :YPAD, :] = zeros
    ref[:, YPAD + width :, :] = zeros


def place(dst_p, dst_q, centre, sides, width):
    rows = centre.shape[1]
    inner = pl.ds(YPAD, width)
    dst_p[pl.ds(HALO, rows), inner, :] = centre[0]
    dst_q[pl.ds(HALO, rows)] = centre[1]
    for at, read in sides:
        dst_p[pl.ds(at, HALO), inner, :] = read(0, HALO)
        dst_q[pl.ds(at, HALO)] = read(HALO, HALO)


def side_starts(rows, reach):
    odd = lax.rem(lax.axis_index("gx"), 2)
    on_chip = jnp.where(odd == 1, 0, rows + reach)
    off_chip = jnp.where(odd == 1, rows + reach, 0)
    return on_chip, off_chip


def has_far_side():
    at = lax.axis_index("gx")
    return (at > 0) & (at < lax.axis_size("gx") - 1)


def two_steps(
    t, rows, width, waves, own, first_prev, coeffs, inject, matrices, scratch, mid_emit, emit, second_prev
):
    p, q = waves
    slope_p, slope_q, curve_p, curve_q, p1, q1 = scratch
    inner = slice(YPAD, YPAD + width)
    clear_pads(p1, width)
    for dst, src in zip((slope_p, slope_q, curve_p, curve_q), own):
        dst[pl.ds(HALO, rows)] = src

    def read_p(start, size):
        return p[pl.ds(start, size), inner, :]

    def read_q(start, size):
        return q[pl.ds(start, size)]

    for begin in (0, rows + HALO):
        depth_rows(read_p, slope_p, curve_p, begin, HALO, width, matrices)
        depth_rows(read_q, slope_q, curve_q, begin, HALO, width, matrices)

    def keep(row, next_p, next_q):
        p1[row, inner, :] = next_p
        q1[row] = next_q
        mid_emit(row, next_p, next_q)

    ext = rows + 2 * REACH
    time_step(
        ext,
        width,
        waves,
        first_prev,
        lambda row: [coeffs[c, row] for c in range(5)],
        (slope_p, slope_q),
        (curve_p, curve_q),
        lambda row: inject[t, row],
        keep,
    )
    depth_rows(lambda b, n: p1[pl.ds(b, n), inner, :], slope_p, curve_p, 0, ext, width, matrices)
    depth_rows(lambda b, n: q1[pl.ds(b, n)], slope_q, curve_q, 0, ext, width, matrices)
    time_step(
        rows,
        width,
        (p1, q1),
        second_prev,
        lambda row: [coeffs[c, row + REACH] for c in range(5)],
        (slope_p, slope_q),
        (curve_p, curve_q),
        lambda row: inject[t + 1, row + REACH],
        emit,
    )


def pack_kernel(
    now, prev, speed, epsilon, delta, tilt, source, far, near, sorted_source, staged, sems
):
    rows = now.shape[1]
    odd = lax.rem(lax.axis_index("gx"), 2)
    copies = []

    def copy(src, dst):
        copies.append(pltpu.make_async_copy(src, dst, sems.at[len(copies)]))
        copies[-1].start()

    for n in range(source.shape[0]):
        for c in range(source.shape[1]):
            copy(source.at[n, c], staged.at[:, n, c])
    sources = len(copies)
    for out, tail in ((far, odd), (near, 1 - odd)):
        wave_at = tail * (rows - HALO)
        edge_at = tail * (rows - REACH)
        for f in range(2):
            copy(now.at[f, pl.ds(wave_at, HALO)], out.at[pl.ds(f * HALO, HALO)])
        for f in range(2):
            copy(
                prev.at[f, pl.ds(edge_at, REACH)],
                out.at[pl.ds(2 * HALO + f * REACH, REACH)],
            )
        for m, field in enumerate((speed, epsilon, delta, tilt)):
            copy(
                field.at[pl.ds(edge_at, REACH)],
                out.at[pl.ds(2 * HALO + (2 + m) * REACH, REACH)],
            )
    for one in copies[:sources]:
        one.wait()
    copy(staged, sorted_source)
    for one in copies[sources:]:
        one.wait()


def prep_kernel(
    now,
    speed,
    epsilon,
    delta,
    tilt,
    receiver_row,
    receiver_column,
    traces,
    table,
    matrices,
    coeffs,
    inject,
    slopes,
    curves,
    offsets,
):
    rows, width, depth = speed.shape
    each_row(
        rows,
        width,
        lambda r: derive(coeffs, r, speed[r], epsilon[r], delta[r], tilt[r]),
    )
    for f in range(2):
        depth_rows(
            lambda b, n: now[f, pl.ds(b, n)], slopes.at[f], curves.at[f], 0, rows, width, matrices
        )
    flat = receivers(receiver_row, receiver_column, rows, width)

    def samples(row):
        cell = lax.broadcasted_iota(jnp.int32, (width, flat.shape[1]), 0) + row * width
        lane = lax.broadcasted_iota(jnp.int32, (width, depth), 1)
        hit = cell == flat
        for t in range(STEPS):
            column = jnp.sum(jnp.where(hit, traces[t : t + 1, :], 0.0), axis=1, keepdims=True)
            inject[t, row] = jnp.where(lane == REC_DEPTH, column, 0.0)

    each_row(rows + 2 * REACH, width, samples)
    fine = table.shape[0]
    starts = [jnp.int32(0)] * NBIN
    for f in range(fine):
        named = table[f]
        for b in range(1, NBIN):
            starts[b] = starts[b] + (named < b).astype(jnp.int32)
    values = [s.astype(jnp.float32) - 1.0 for s in starts]
    values = values + [jnp.float32(fine - 1), jnp.float32(0.5 * (fine - 1))]
    for b, value in enumerate(values):
        offsets[b : b + 1, :] = jnp.full((1, depth), value, jnp.float32)


def early_kernel(
    now,
    prev,
    on_chip,
    off_chip,
    own_coeffs,
    inject,
    slopes,
    curves,
    matrices,
    out,
    mid,
    coeffs,
    slope_out,
    p,
    q,
    prev_ext,
    *scratch,
):
    rows, width = now.shape[1], now.shape[2]
    near, far = side_starts(rows, HALO)
    inside = has_far_side()
    clear_pads(p, width)
    place(
        p,
        q,
        now,
        (
            (near, lambda a, n: on_chip[pl.ds(a, n)]),
            (far, lambda a, n: jnp.where(inside, off_chip[pl.ds(a, n)], 0.0)),
        ),
        width,
    )
    near, far = side_starts(rows, REACH)
    base = 2 * HALO
    for c in range(5):
        coeffs[c, pl.ds(REACH, rows)] = own_coeffs[c]
    for f in range(2):
        prev_ext[f, pl.ds(REACH, rows)] = prev[f]
    for at, part, real in ((near, on_chip, True), (far, off_chip, inside)):

        def only_real(value, real=real):
            return value if real is True else jnp.where(real, value, 0.0)

        for f in range(2):
            prev_ext[f, pl.ds(at, REACH)] = only_real(part[pl.ds(base + f * REACH, REACH)])
        for r in range(REACH):
            fields = [part[base + (2 + m) * REACH + r] for m in range(4)]
            derive(coeffs, at + r, only_real(fields[0]), *fields[1:])

    def mid_emit(row, next_p, next_q):
        mid[0, row] = next_p
        mid[1, row] = next_q

    def emit(row, next_p, next_q):
        out[0, row] = next_p
        out[1, row] = next_q

    two_steps(
        0,
        rows,
        width,
        (p, q),
        (slopes[0], slopes[1], curves[0], curves[1]),
        lambda row: (prev_ext[0, row], prev_ext[1, row]),
        coeffs,
        inject,
        matrices,
        scratch,
        mid_emit,
        emit,
        lambda row: (now[0, row], now[1, row]),
    )
    slope_out[...] = scratch[0][pl.ds(REACH, rows)]


def side_kernel(before, mid, slope_z, now, matrices, flux, slopes, curves, p1):
    rows, width = before.shape[1], before.shape[2]
    clear_pads(p1, width)
    p1[:, YPAD : YPAD + width, :] = mid[0]

    def fluxes(row):
        _, parts = flux_row(row, width, p1, slope_z[row], before[0, row])
        for a in range(3):
            flux[a, row] = parts[a]

    each_row(rows, width, fluxes)
    for f in range(2):
        depth_rows(
            lambda b, n: now[f, pl.ds(b, n)], slopes.at[f], curves.at[f], 0, rows, width, matrices
        )


def late_kernel(
    now,
    mid,
    coeffs,
    on_chip,
    off_chip,
    inject,
    slopes,
    curves,
    matrices,
    out,
    imaged,
    p,
    q,
    *scratch,
):
    rows, width = now.shape[1], now.shape[2]
    near, far = side_starts(rows, HALO)
    inside = has_far_side()
    clear_pads(p, width)
    place(
        p,
        q,
        now,
        (
            (near, lambda a, n: on_chip[a // HALO]),
            (far, lambda a, n: jnp.where(inside, off_chip[a // HALO], 0.0)),
        ),
        width,
    )

    def emit(row, next_p, next_q):
        out[0, row] = next_p
        out[1, row] = next_q

    two_steps(
        2,
        rows,
        width,
        (p, q),
        (slopes[0], slopes[1], curves[0], curves[1]),
        lambda row: (mid[0, row], mid[1, row]),
        coeffs,
        inject,
        matrices,
        scratch,
        lambda row, next_p, next_q: None,
        emit,
        lambda row: (now[0, row], now[1, row]),
    )
    slope_z, p1 = scratch[0], scratch[4]

    def fluxes(row):
        field, parts = flux_row(row, width, p1, slope_z[row + REACH], now[0, row])
        for a, value in enumerate((field, *parts)):
            imaged[a, row] = value

    each_row(rows, width, fluxes)


def image_kernel(
    arrived, mid, flux, imaged, offsets, wave, images, wave_out, block, lines, sems
):
    rows, width, _ = flux.shape[1:]
    whole = pltpu.make_async_copy(wave, wave_out, sems.at[0])
    whole.start()
    lines[...] = arrived[...].astype(jnp.float32).reshape(lines.shape)
    parts = arrived.shape[2]
    stride = lines.shape[0] // width

    def source(n, row):
        begin = n * parts * rows + row
        return [lines[pl.ds(begin + c * rows, width, stride=stride), :] for c in range(parts)]

    def image_row(row):
        totals = [None] * NBIN

        def keep(b, term):
            totals[b] = term

        def finish(b, term):
            block[b, row] = (totals[b] + term).astype(block.dtype)

        early = [flux[a, row] for a in range(3)]
        image_terms(source(0, row), mid[0, row + REACH], early, offsets, keep)
        late = [imaged[a, row] for a in range(1, 4)]
        image_terms(source(1, row), imaged[0, row], late, offsets, finish)

    pieces = []
    size = rows // OUT_PIECES
    for piece in range(OUT_PIECES):
        each_row(size, width, lambda row: image_row(row + piece * size))
        part = pl.ds(piece * size, size)
        pieces.append(
            pltpu.make_async_copy(block.at[:, part], images.at[:, part], sems.at[1 + piece])
        )
        pieces[-1].start()
    for piece in pieces:
        piece.wait()
    whole.wait()


def local(
    wave_now,
    wave_prev,
    speed_term,
    thomsen_epsilon,
    thomsen_delta,
    tilt_angle,
    source_store,
    receiver_row,
    receiver_column,
    receiver_traces,
    angle_table,
):
    _, rows, width, depth = wave_now.shape
    count = lax.axis_size("gx")
    odd = lax.rem(lax.axis_index("gx"), 2)
    on_chip_pairs = [(i, i ^ 1) for i in range(count)]
    both_axes = ("shot", "gx")
    shots = lax.axis_size("shot")
    off_chip_pairs = []
    for shot in range(shots):
        at = shot * count
        for i in range(1, count - 1, 2):
            off_chip_pairs += [(at + i, at + i + 1), (at + i + 1, at + i)]
        other = ((shot + 1) % shots) * count
        if shots > 1:
            off_chip_pairs += [(at, other), (at + count - 1, other + count - 1)]

    f32 = jnp.float32
    ext, wide = rows + 2 * REACH, rows + 2 * HALO
    vmem = pl.BlockSpec(memory_space=pltpu.VMEM)
    smem = pl.BlockSpec(memory_space=pltpu.SMEM)
    in_hbm = pl.BlockSpec(memory_space=pltpu.HBM)
    plane = (width, depth)
    padded = (width + 2 * YPAD, depth)
    plane_bytes = 4 * width * depth
    line_flops = width * depth

    def planes(*lead):
        return jax.ShapeDtypeStruct(lead + plane, f32)

    def call(kernel, outs, ins, in_specs, scratch, grant, cost, out_specs=None):
        return pl.pallas_call(
            kernel,
            out_shape=outs,
            in_specs=in_specs,
            out_specs=out_specs or jax.tree.map(lambda _: vmem, outs),
            scratch_shapes=scratch,
            compiler_params=pltpu.CompilerParams(
                vmem_limit_bytes=4 * 1024 * 1024 + grant * plane_bytes
            ),
            cost_estimate=pl.CostEstimate(
                flops=cost * line_flops, bytes_accessed=cost * line_flops // 4, transcendentals=0
            ),
        )(*ins)

    step_scratch = [
        pltpu.VMEM((wide,) + plane, f32),
        pltpu.VMEM((wide,) + plane, f32),
        pltpu.VMEM((wide,) + plane, f32),
        pltpu.VMEM((wide,) + plane, f32),
        pltpu.VMEM((ext,) + padded, f32),
        pltpu.VMEM((ext,) + plane, f32),
    ]
    wave_scratch = [pltpu.VMEM((wide,) + padded, f32), pltpu.VMEM((wide,) + plane, f32)]
    medium = (speed_term, thomsen_epsilon, thomsen_delta, tilt_angle)
    matrices = jnp.asarray(depth_matrices(depth))

    packed = planes(2 * HALO + 6 * REACH)
    snaps, parts = source_store.shape[:2]
    by_owner = source_store.reshape(snaps, parts, count, rows, depth)
    far_pack, near_pack, sorted_source = call(
        pack_kernel,
        (
            packed,
            packed,
            jax.ShapeDtypeStruct((count, snaps, parts, rows, depth), source_store.dtype),
        ),
        [
            pltpu.with_memory_space_constraint(x, pltpu.HBM)
            for x in (wave_now, wave_prev, *medium, by_owner)
        ],
        [in_hbm] * 7,
        [
            pltpu.VMEM((count, snaps, parts, rows, depth), source_store.dtype),
            pltpu.SemaphoreType.DMA((17 + snaps * parts,)),
        ],
        120,
        200,
        (vmem, vmem, in_hbm),
    )
    off_chip = lax.ppermute(far_pack, both_axes, off_chip_pairs)
    on_chip = lax.ppermute(near_pack, "gx", on_chip_pairs)
    arrived = lax.all_to_all(sorted_source, "gx", split_axis=0, concat_axis=0, tiled=True)
    own_coeffs, inject, slopes, curves, offsets = call(
        prep_kernel,
        (
            planes(5, rows),
            planes(STEPS, ext),
            planes(2, rows),
            planes(2, rows),
            jax.ShapeDtypeStruct((16, depth), f32),
        ),
        (wave_now, *medium, receiver_row, receiver_column, receiver_traces, angle_table, matrices),
        [vmem] * 8 + [smem, vmem],
        [],
        20 * wide,
        60 * rows,
    )
    now, mid, coeffs, slope_z = call(
        early_kernel,
        (planes(2, rows), planes(2, ext), planes(5, ext), planes(rows)),
        (wave_now, wave_prev, on_chip, off_chip, own_coeffs, inject, slopes, curves, matrices),
        [vmem] * 9,
        wave_scratch + [pltpu.VMEM((2, ext) + plane, f32)] + step_scratch,
        30 * wide,
        400 * rows,
    )

    def side(tail):
        if rows == HALO:
            return now
        return lax.dynamic_slice_in_dim(now, jnp.where(tail, rows - HALO, 0), HALO, axis=1)

    off_chip = lax.ppermute(side(odd == 1), both_axes, off_chip_pairs)
    on_chip = lax.ppermute(side(odd == 0), "gx", on_chip_pairs)
    flux, slopes, curves = call(
        side_kernel,
        (planes(3, rows), planes(2, rows), planes(2, rows)),
        (wave_now, mid, slope_z, now, matrices),
        [vmem] * 5,
        [pltpu.VMEM((ext,) + padded, f32)],
        12 * wide,
        60 * rows,
    )
    final, imaged = call(
        late_kernel,
        (planes(2, rows), planes(4, rows)),
        (now, mid, coeffs, on_chip, off_chip, inject, slopes, curves, matrices),
        [vmem] * 9,
        wave_scratch + step_scratch,
        30 * wide,
        400 * rows,
    )
    return call(
        image_kernel,
        (jax.ShapeDtypeStruct((NBIN, rows) + plane, jnp.bfloat16), planes(2, rows)),
        (arrived, mid, flux, imaged, offsets, final),
        [vmem] * 6,
        [
            pltpu.VMEM((NBIN, rows) + plane, jnp.bfloat16),
            pltpu.VMEM((sorted_source.size // depth, depth), f32),
            pltpu.SemaphoreType.DMA((1 + OUT_PIECES,)),
        ],
        16 * wide,
        60 * rows,
        (in_hbm, in_hbm),
    )


def solution(mesh):
    placed = (
        P("shot", "gx", None, None),
        P("shot", "gx", None, None),
        P("gx", None, None),
        P("gx", None, None),
        P("gx", None, None),
        P("gx", None, None),
        P("shot", None, None, "gx", None),
        P("shot"),
        P("shot"),
        P("shot", None),
        P(),
    )
    return jax.shard_map(
        local,
        mesh=mesh,
        in_specs=placed,
        out_specs=(P("shot", "gx", None, None), P("shot", "gx", None, None)),
        check_vma=False,
    )
```

```python
import jax
import jax.numpy as jnp
import numpy as np
from jax import lax
from jax.experimental import pallas as pl
from jax.experimental.pallas import tpu as pltpu
from jax.sharding import PartitionSpec as P


STEPS = 4
NBIN = 8
REC_DEPTH = 2
REACH = 4
HALO = 2 * REACH
YPAD = 8
OUT_PIECES = 4

SECOND = (-205.0 / 72.0, 8.0 / 5.0, -1.0 / 5.0, 8.0 / 315.0, -1.0 / 560.0)
FIRST = (4.0 / 5.0, -1.0 / 5.0, 4.0 / 105.0, -1.0 / 280.0)


def each_row(count, width, body):
    if width <= 16:
        for row in range(count):
            body(row)
    else:
        lax.fori_loop(0, count, lambda row, carry: (body(row), carry)[1], 0)


def each_chunk(count, width, body):
    size = max(1, min(count, 512 // width))
    while count % size:
        size -= 1
    if count // size <= 2:
        for start in range(0, count, size):
            body(start, size)
    else:
        lax.fori_loop(0, count // size, lambda i, carry: (body(i * size, size), carry)[1], 0)


def second(centre, pairs):
    total = SECOND[0] * centre
    for k in range(1, 5):
        plus, minus = pairs(k)
        total = total + SECOND[k] * (plus + minus)
    return total


def first(pairs):
    total = None
    for k in range(1, 5):
        plus, minus = pairs(k)
        term = FIRST[k - 1] * (plus - minus)
        total = term if total is None else total + term
    return total


def depth_matrices(depth):
    eye = [np.eye(depth, k=k, dtype=np.float64) for k in range(-4, 5)]
    slope = sum(np.float32(FIRST[k - 1]) * (eye[4 - k] - eye[4 + k]) for k in range(1, 5))
    curve = np.float32(SECOND[0]) * eye[4] + sum(
        np.float32(SECOND[k]) * (eye[4 - k] + eye[4 + k]) for k in range(1, 5)
    )
    rest = np.concatenate([slope, curve], axis=1).astype(np.float32)
    parts = []
    for _ in range(3):
        parts.append(rest.astype(jnp.bfloat16))
        rest = rest - parts[-1].astype(np.float32)
    return np.stack(parts)


def depth_diffs(field, matrices):
    depth = field.shape[1]
    high = field.astype(jnp.bfloat16)
    rest = field - high.astype(jnp.float32)
    middle = rest.astype(jnp.bfloat16)
    low = (rest - middle.astype(jnp.float32)).astype(jnp.bfloat16)
    m_high, m_middle, m_low = matrices[0], matrices[1], matrices[2]

    def product(left, top, bottom):
        return jnp.dot(
            left, jnp.concatenate([top, bottom], axis=0), preferred_element_type=jnp.float32
        )

    upper = jnp.concatenate([high, middle], axis=1)
    lower = jnp.concatenate([high, low], axis=1)
    both = (
        product(lower, m_low, m_high)
        + product(upper, m_middle, m_middle)
        + product(upper, m_high, m_high)
    )
    return both[:, :depth], both[:, depth:]


def depth_rows(read, slope, curve, begin, count, width, matrices, shift=0):
    def chunk(start, size):
        field = read(begin + start, size)
        depth = field.shape[-1]
        s, c = depth_diffs(field.reshape(size * width, depth), matrices)
        slope[pl.ds(begin + shift + start, size)] = s.reshape(size, width, depth)
        curve[pl.ds(begin + shift + start, size)] = c.reshape(size, width, depth)

    each_chunk(count, width, chunk)


def sine_terms(angle):
    half = 0.5 * angle
    sq = half * half
    s = 1.0
    for n in (12 * 13, 10 * 11, 8 * 9, 6 * 7, 4 * 5, 2 * 3):
        s = 1.0 - sq * s * (1.0 / n)
    s = s * half
    c = 1.0
    for n in (13 * 14, 11 * 12, 9 * 10, 7 * 8, 5 * 6, 3 * 4, 1 * 2):
        c = 1.0 - sq * c * (1.0 / n)
    sine = 2.0 * s * c
    cosine = 1.0 - 2.0 * s * s
    return sine * sine, 2.0 * sine * cosine


def derive(coeffs, at, s, e, d, a):
    coeffs[0, at] = s
    coeffs[1, at] = s * (1.0 + 2.0 * e)
    coeffs[2, at] = s * jnp.sqrt(1.0 + 2.0 * d)
    coeffs[3, at], coeffs[4, at] = sine_terms(a)


def receivers(row_ref, column_ref, rows, width):
    begin = lax.axis_index("gx") * rows - REACH
    count = row_ref.shape[0]
    local_row = row_ref[...].reshape(1, count) - begin
    inside = (local_row >= 0) & (local_row < rows + 2 * REACH)
    return jnp.where(inside, local_row * width + column_ref[...].reshape(1, count), -1)


def time_step(begin, rows, width, fields, earlier, coeffs, slopes, curves, emit):
    p, q = fields
    slope_p, slope_q = slopes
    curve_p, curve_q = curves
    inner = slice(YPAD, YPAD + width)

    def update(row):
        at = row + REACH
        now_p = p[at, inner, :]
        now_q = q[at]
        xx_p = second(now_p, lambda k: (p[at + k, inner, :], p[at - k, inner, :]))
        xx_q = second(now_q, lambda k: (q[at + k], q[at - k]))
        xz_p = first(lambda k: (slope_p[at + k], slope_p[at - k]))
        xz_q = first(lambda k: (slope_q[at + k], slope_q[at - k]))
        yy_p = second(
            now_p,
            lambda k: (
                p[at, YPAD + k : YPAD + k + width, :],
                p[at, YPAD - k : YPAD - k + width, :],
            ),
        )
        speed, gain, mixed, sine_sq, sine_double = coeffs(row)
        tilt_p = sine_sq * (xx_p - curve_p[at]) + sine_double * xz_p
        tilt_q = sine_sq * (xx_q - curve_q[at]) + sine_double * xz_q
        across = xx_p + yy_p - tilt_p
        rotated = curve_q[at] + tilt_q
        prev_p, prev_q = earlier(row)
        next_p = 2.0 * now_p - prev_p + (gain * across + mixed * rotated)
        next_q = 2.0 * now_q - prev_q + (mixed * across + speed * rotated)
        emit(row, next_p, next_q)

    each_row(rows, width, lambda row: update(begin + row))


def border_terms(row, rows, read, slope):
    curve, mixed = None, None
    for border in (REACH, rows + REACH):
        for k in range(1, 5):
            for other, sign in ((row + k, 1.0), (row - k, -1.0)):
                low, high = min(row, other), max(row, other)
                if low < border <= high:
                    c = SECOND[k] * read(other)
                    m = (sign * FIRST[k - 1]) * slope(other)
                    curve = c if curve is None else curve + c
                    mixed = m if mixed is None else mixed + m
    return curve, mixed


def add_border(row, rows, reads, slopes, coeffs, base):
    next_p, next_q = base
    xx_p, xz_p = border_terms(row, rows, reads[0], slopes[0])
    if xx_p is None:
        return next_p, next_q
    xx_q, xz_q = border_terms(row, rows, reads[1], slopes[1])
    speed, gain, mixed, sine_sq, sine_double = coeffs
    across = xx_p - (sine_sq * xx_p + sine_double * xz_p)
    rotated = sine_sq * xx_q + sine_double * xz_q
    return (
        next_p + (gain * across + mixed * rotated),
        next_q + (mixed * across + speed * rotated),
    )


def block_step(rows, width, fields, slopes, curves, matrices, earlier, coeffs, emit):
    p, q = fields
    inner = slice(YPAD, YPAD + width)
    for field, slope, curve in (
        (lambda b, n: p[pl.ds(b, n), inner, :], slopes[0], curves[0]),
        (lambda b, n: q[pl.ds(b, n)], slopes[1], curves[1]),
    ):
        depth_rows(field, slope, curve, REACH, rows, width, matrices)
    time_step(0, rows, width, fields, earlier, coeffs, slopes, curves, emit)


def clear_sides(rows, *refs):
    for ref in refs:
        zeros = jnp.zeros((REACH,) + ref.shape[1:], jnp.float32)
        ref[pl.ds(0, REACH)] = zeros
        ref[pl.ds(rows + REACH, REACH)] = zeros


def flux_row(row, width, p, slope_z, before):
    at = row + REACH
    now = p[at, YPAD : YPAD + width, :]
    back = before - now
    slope_x = first(
        lambda k: (p[at + k, YPAD : YPAD + width, :], p[at - k, YPAD : YPAD + width, :])
    )
    slope_y = first(
        lambda k: (p[at, YPAD + k : YPAD + k + width, :], p[at, YPAD - k : YPAD - k + width, :])
    )
    return now, (back * slope_x, back * slope_y, back * slope_z)


def image_terms(source, field, flux, offsets, emit):
    fx, fy, fz = flux
    s0, s1, s2, s3 = source
    dot = s1 * fx + s2 * fy + s3 * fz
    squares = (s1 * s1 + s2 * s2 + s3 * s3) * (fx * fx + fy * fy + fz * fz)
    cosine = dot * jnp.minimum(lax.rsqrt(squares), 1.0)
    scaled = (cosine + 1.0) * offsets[NBIN : NBIN + 1, :]
    strength = s0 * field
    above = strength
    for b in range(NBIN - 1):
        beyond = jnp.clip(scaled - offsets[b + 1 : b + 2, :], 0.0, 1.0) * strength
        emit(b, above - beyond)
        above = beyond
    emit(NBIN - 1, above)


def clear_pads(ref, width):
    rows, _, depth = ref.shape
    zeros = jnp.zeros((rows, YPAD, depth), jnp.float32)
    ref[:, :YPAD, :] = zeros
    ref[:, YPAD + width :, :] = zeros


def place(dst_p, dst_q, centre, sides, width):
    rows = centre.shape[1]
    inner = pl.ds(YPAD, width)
    dst_p[pl.ds(HALO, rows), inner, :] = centre[0]
    dst_q[pl.ds(HALO, rows)] = centre[1]
    for at, read in sides:
        dst_p[pl.ds(at, HALO), inner, :] = read(0, HALO)
        dst_q[pl.ds(at, HALO)] = read(HALO, HALO)


def side_starts(rows, reach):
    odd = lax.rem(lax.axis_index("gx"), 2)
    on_chip = jnp.where(odd == 1, 0, rows + reach)
    off_chip = jnp.where(odd == 1, rows + reach, 0)
    return on_chip, off_chip


def has_far_side():
    at = lax.axis_index("gx")
    return (at > 0) & (at < lax.axis_size("gx") - 1)


def second_step(rows, width, p1, q1, slopes, curves, earlier, coeffs, inject, matrices, emit):
    inner = slice(YPAD, YPAD + width)
    ext = rows + 2 * REACH
    depth_rows(
        lambda b, n: p1[pl.ds(b, n), inner, :], slopes[0], curves[0], 0, ext, width, matrices
    )
    depth_rows(lambda b, n: q1[pl.ds(b, n)], slopes[1], curves[1], 0, ext, width, matrices)

    def finish(row, next_p, next_q):
        emit(row, next_p + inject[row + REACH], next_q)

    time_step(
        0,
        rows,
        width,
        (p1, q1),
        earlier,
        lambda row: [coeffs[c, row + REACH] for c in range(5)],
        slopes,
        curves,
        finish,
    )


def pack_kernel(
    now,
    prev,
    speed,
    epsilon,
    delta,
    tilt,
    source,
    matrices,
    far,
    near,
    sorted_source,
    coeffs,
    base,
    slopes,
    staged,
    p,
    q,
    before,
    medium,
    slope_p,
    slope_q,
    curve_p,
    curve_q,
    weights,
    sems,
):
    rows, width = now.shape[1], now.shape[2]
    odd = lax.rem(lax.axis_index("gx"), 2)
    ends = ((far, odd), (near, 1 - odd))
    copies = []
    clear_pads(p, width)
    clear_sides(rows, p, q, slope_p, slope_q)

    def copy(src, dst):
        copies.append(pltpu.make_async_copy(src, dst, sems.at[len(copies)]))
        copies[-1].start()
        return copies[-1]

    own = pl.ds(REACH, rows)
    local = [copy(matrices, weights)]
    local.append(copy(now.at[0], p.at[own, pl.ds(YPAD, width)]))
    local.append(copy(now.at[1], q.at[own]))
    fields = (speed, epsilon, delta, tilt)
    for m, field in enumerate(fields):
        local.append(copy(field, medium.at[m]))
    local.append(copy(prev, before))
    arriving = []
    for n in range(source.shape[0]):
        for c in range(source.shape[1]):
            arriving.append(copy(source.at[n, c], staged.at[:, n, c]))
    edges = []
    for out, tail in ends:
        edge = pl.ds(tail * (rows - REACH), REACH)
        for f in range(2):
            edges.append(copy(now.at[f, edge], out.at[pl.ds(f * REACH, REACH)]))
        for m, field in enumerate(fields):
            edges.append(copy(field.at[edge], out.at[pl.ds((4 + m) * REACH, REACH)]))
    for one in local + arriving:
        one.wait()
    leaving = copy(staged, sorted_source)
    each_row(rows, width, lambda r: derive(coeffs, r, *[medium[m, r] for m in range(4)]))

    def emit(row, next_p, next_q):
        base[0, row] = next_p
        base[1, row] = next_q

    block_step(
        rows,
        width,
        (p, q),
        (slope_p, slope_q),
        (curve_p, curve_q),
        weights,
        lambda row: (before[0, row], before[1, row]),
        lambda row: [coeffs[c, row] for c in range(5)],
        emit,
    )
    slopes[0] = slope_p[own]
    slopes[1] = slope_q[own]
    for out, tail in ends:
        for f in range(2):
            out[pl.ds((2 + f) * REACH, REACH)] = base[f, pl.ds(tail * (rows - REACH), REACH)]
    for one in edges:
        one.wait()
    leaving.wait()


def prep_kernel(receiver_row, receiver_column, traces, table, inject, offsets):
    _, ext, width, depth = inject.shape
    flat = receivers(receiver_row, receiver_column, ext - 2 * REACH, width)

    def samples(row):
        cell = lax.broadcasted_iota(jnp.int32, (width, flat.shape[1]), 0) + row * width
        lane = lax.broadcasted_iota(jnp.int32, (width, depth), 1)
        hit = cell == flat
        for t in range(STEPS):
            column = jnp.sum(jnp.where(hit, traces[t : t + 1, :], 0.0), axis=1, keepdims=True)
            inject[t, row] = jnp.where(lane == REC_DEPTH, column, 0.0)

    each_row(ext, width, samples)
    fine = table.shape[0]
    starts = [jnp.int32(0)] * NBIN
    for f in range(fine):
        named = table[f]
        for b in range(1, NBIN):
            starts[b] = starts[b] + (named < b).astype(jnp.int32)
    values = [s.astype(jnp.float32) - 1.0 for s in starts]
    values.append(jnp.float32(0.5 * (fine - 1)))
    for b, value in enumerate(values):
        offsets[b : b + 1, :] = jnp.full((1, depth), value, jnp.float32)


def early_kernel(
    now,
    on_chip,
    off_chip,
    own_coeffs,
    base,
    own_slopes,
    inject,
    matrices,
    out,
    mid,
    coeffs,
    slope_out,
    p,
    q,
    ext_base,
    slope_p,
    slope_q,
    curve_p,
    curve_q,
    p1,
):
    rows, width = now.shape[1], now.shape[2]
    inner = slice(YPAD, YPAD + width)
    near, far = side_starts(rows, REACH)
    inside = has_far_side()
    clear_pads(p1, width)
    own = pl.ds(REACH, rows)
    p[own], q[own] = now[0], now[1]
    slope_p[own], slope_q[own] = own_slopes[0], own_slopes[1]
    for f in range(2):
        ext_base[f, own] = base[f]
    for c in range(5):
        coeffs[c, own] = own_coeffs[c]
    for at, part, real in ((near, on_chip, None), (far, off_chip, inside)):

        def take(index, real=real, part=part):
            value = part[pl.ds(index * REACH, REACH)]
            return value if real is None else jnp.where(real, value, 0.0)

        side = pl.ds(at, REACH)
        p[side], q[side] = take(0), take(1)
        ext_base[0, side], ext_base[1, side] = take(2), take(3)
        medium = [take(4)] + [part[pl.ds((5 + m) * REACH, REACH)] for m in range(3)]
        for r in range(REACH):
            derive(coeffs, at + r, *[m[r] for m in medium])
    for begin in (0, rows + REACH):
        depth_rows(lambda b, n: p[pl.ds(b, n)], slope_p, curve_p, begin, REACH, width, matrices)
        depth_rows(lambda b, n: q[pl.ds(b, n)], slope_q, curve_q, begin, REACH, width, matrices)
    q1 = mid.at[1]
    for row in range(rows + 2 * REACH):
        next_p, next_q = add_border(
            row,
            rows,
            (lambda i: p[i], lambda i: q[i]),
            (lambda i: slope_p[i], lambda i: slope_q[i]),
            [coeffs[c, row] for c in range(5)],
            (ext_base[0, row], ext_base[1, row]),
        )
        next_p = next_p + inject[0, row]
        p1[row, inner, :] = next_p
        mid[0, row] = next_p
        mid[1, row] = next_q

    def emit(row, next_p, next_q):
        out[0, row] = next_p
        out[1, row] = next_q

    second_step(
        rows,
        width,
        p1,
        q1,
        (slope_p, slope_q),
        (curve_p, curve_q),
        lambda row: (now[0, row], now[1, row]),
        coeffs,
        inject.at[1],
        matrices,
        emit,
    )
    slope_out[...] = slope_p[own]


def side_kernel(
    before,
    mid,
    slope_z,
    now,
    coeffs,
    matrices,
    flux,
    base,
    slopes,
    p1,
    p,
    q,
    slope_p,
    slope_q,
    curve_p,
    curve_q,
):
    rows, width = before.shape[1], before.shape[2]
    own = pl.ds(REACH, rows)
    clear_pads(p1, width)
    p1[:, YPAD : YPAD + width, :] = mid[0]

    def fluxes(row):
        _, parts = flux_row(row, width, p1, slope_z[row], before[0, row])
        for a in range(3):
            flux[a, row] = parts[a]

    each_row(rows, width, fluxes)
    clear_pads(p, width)
    clear_sides(rows, p, q, slope_p, slope_q)
    p[own, YPAD : YPAD + width, :] = now[0]
    q[own] = now[1]

    def emit(row, next_p, next_q):
        base[0, row] = next_p
        base[1, row] = next_q

    block_step(
        rows,
        width,
        (p, q),
        (slope_p, slope_q),
        (curve_p, curve_q),
        matrices,
        lambda row: (mid[0, row + REACH], mid[1, row + REACH]),
        lambda row: [coeffs[c, row + REACH] for c in range(5)],
        emit,
    )
    slopes[0] = slope_p[own]
    slopes[1] = slope_q[own]


def late_kernel(
    now,
    mid,
    coeffs,
    on_chip,
    off_chip,
    base,
    own_slopes,
    inject,
    matrices,
    out,
    imaged,
    p,
    q,
    slope_p,
    slope_q,
    curve_p,
    curve_q,
    p1,
    q1,
):
    rows, width = now.shape[1], now.shape[2]
    inner = slice(YPAD, YPAD + width)
    near, far = side_starts(rows, HALO)
    inside = has_far_side()
    clear_pads(p, width)
    clear_pads(p1, width)
    place(
        p,
        q,
        now,
        (
            (near, lambda a, n: on_chip[a // HALO]),
            (far, lambda a, n: jnp.where(inside, off_chip[a // HALO], 0.0)),
        ),
        width,
    )
    own = pl.ds(HALO, rows)
    slope_p[own], slope_q[own] = own_slopes[0], own_slopes[1]
    for begin in (0, rows + HALO):
        depth_rows(
            lambda b, n: p[pl.ds(b, n), inner, :], slope_p, curve_p, begin, HALO, width, matrices
        )
        depth_rows(lambda b, n: q[pl.ds(b, n)], slope_q, curve_q, begin, HALO, width, matrices)

    def keep(row, next_p, next_q):
        p1[row, inner, :] = next_p + inject[2, row]
        q1[row] = next_q

    for begin in (0, rows + REACH):
        time_step(
            begin,
            REACH,
            width,
            (p, q),
            lambda row: (mid[0, row], mid[1, row]),
            lambda row: [coeffs[c, row] for c in range(5)],
            (slope_p, slope_q),
            (curve_p, curve_q),
            keep,
        )
    for row in range(REACH, rows + REACH):
        result = add_border(
            row,
            rows,
            (lambda i: p[i + REACH, inner, :], lambda i: q[i + REACH]),
            (lambda i: slope_p[i + REACH], lambda i: slope_q[i + REACH]),
            [coeffs[c, row] for c in range(5)],
            (base[0, row - REACH], base[1, row - REACH]),
        )
        keep(row, *result)

    def emit(row, next_p, next_q):
        out[0, row] = next_p
        out[1, row] = next_q

    second_step(
        rows,
        width,
        p1,
        q1,
        (slope_p, slope_q),
        (curve_p, curve_q),
        lambda row: (now[0, row], now[1, row]),
        coeffs,
        inject.at[3],
        matrices,
        emit,
    )

    def fluxes(row):
        field, parts = flux_row(row, width, p1, slope_p[row + REACH], now[0, row])
        for a, value in enumerate((field, *parts)):
            imaged[a, row] = value

    each_row(rows, width, fluxes)


def image_kernel(
    arrived, mid, flux, imaged, offsets, wave, images, wave_out, block, lines, sems
):
    rows, width, _ = flux.shape[1:]
    whole = pltpu.make_async_copy(wave, wave_out, sems.at[0])
    whole.start()
    lines[...] = arrived[...].astype(jnp.float32).reshape(lines.shape)
    parts = arrived.shape[2]
    stride = lines.shape[0] // width

    def source(n, row):
        begin = n * parts * rows + row
        return [lines[pl.ds(begin + c * rows, width, stride=stride), :] for c in range(parts)]

    def image_row(row):
        totals = [None] * NBIN

        def keep(b, term):
            totals[b] = term

        def finish(b, term):
            block[b, row] = (totals[b] + term).astype(block.dtype)

        early = [flux[a, row] for a in range(3)]
        image_terms(source(0, row), mid[0, row + REACH], early, offsets, keep)
        late = [imaged[a, row] for a in range(1, 4)]
        image_terms(source(1, row), imaged[0, row], late, offsets, finish)

    pieces = []
    size = rows // OUT_PIECES
    for piece in range(OUT_PIECES):
        each_row(size, width, lambda row: image_row(row + piece * size))
        part = pl.ds(piece * size, size)
        pieces.append(
            pltpu.make_async_copy(block.at[:, part], images.at[:, part], sems.at[1 + piece])
        )
        pieces[-1].start()
    for piece in pieces:
        piece.wait()
    whole.wait()


def local(
    wave_now,
    wave_prev,
    speed_term,
    thomsen_epsilon,
    thomsen_delta,
    tilt_angle,
    source_store,
    receiver_row,
    receiver_column,
    receiver_traces,
    angle_table,
):
    _, rows, width, depth = wave_now.shape
    count = lax.axis_size("gx")
    odd = lax.rem(lax.axis_index("gx"), 2)
    on_chip_pairs = [(i, i ^ 1) for i in range(count)]
    both_axes = ("shot", "gx")
    shots = lax.axis_size("shot")
    off_chip_pairs = []
    for shot in range(shots):
        at = shot * count
        for i in range(1, count - 1, 2):
            off_chip_pairs += [(at + i, at + i + 1), (at + i + 1, at + i)]
        other = ((shot + 1) % shots) * count
        if shots > 1:
            off_chip_pairs += [(at, other), (at + count - 1, other + count - 1)]

    f32 = jnp.float32
    ext, wide = rows + 2 * REACH, rows + 2 * HALO
    vmem = pl.BlockSpec(memory_space=pltpu.VMEM)
    smem = pl.BlockSpec(memory_space=pltpu.SMEM)
    in_hbm = pl.BlockSpec(memory_space=pltpu.HBM)
    plane = (width, depth)
    padded = (width + 2 * YPAD, depth)
    plane_bytes = 4 * width * depth
    line_flops = width * depth

    def planes(*lead):
        return jax.ShapeDtypeStruct(lead + plane, f32)

    def call(kernel, outs, ins, in_specs, scratch, grant, cost, out_specs=None):
        return pl.pallas_call(
            kernel,
            out_shape=outs,
            in_specs=in_specs,
            out_specs=out_specs or jax.tree.map(lambda _: vmem, outs),
            scratch_shapes=scratch,
            compiler_params=pltpu.CompilerParams(
                vmem_limit_bytes=4 * 1024 * 1024 + grant * plane_bytes
            ),
            cost_estimate=pl.CostEstimate(
                flops=cost * line_flops, bytes_accessed=cost * line_flops // 4, transcendentals=0
            ),
        )(*ins)

    def room(count, lines=plane):
        return pltpu.VMEM((count,) + lines, f32)

    medium = (speed_term, thomsen_epsilon, thomsen_delta, tilt_angle)
    matrices = jnp.asarray(depth_matrices(depth))
    snaps, parts = source_store.shape[:2]
    by_owner = source_store.reshape(snaps, parts, count, rows, depth)
    sorted_shape = (count, snaps, parts, rows, depth)
    packed = planes(8 * REACH)
    far_pack, near_pack, sorted_source, own_coeffs, base, slopes = call(
        pack_kernel,
        (
            packed,
            packed,
            jax.ShapeDtypeStruct(sorted_shape, source_store.dtype),
            planes(5, rows),
            planes(2, rows),
            planes(2, rows),
        ),
        [
            pltpu.with_memory_space_constraint(x, pltpu.HBM)
            for x in (wave_now, wave_prev, *medium, by_owner, matrices)
        ],
        [in_hbm] * 8,
        [
            pltpu.VMEM(sorted_shape, source_store.dtype),
            room(ext, padded),
            room(ext),
            pltpu.VMEM((2, rows) + plane, f32),
            pltpu.VMEM((4, rows) + plane, f32),
            *[room(ext)] * 4,
            pltpu.VMEM(matrices.shape, matrices.dtype),
            pltpu.SemaphoreType.DMA((21 + snaps * parts,)),
        ],
        16 * wide,
        200,
        (vmem, vmem, in_hbm, vmem, vmem, vmem),
    )
    off_chip = lax.ppermute(far_pack, both_axes, off_chip_pairs)
    on_chip = lax.ppermute(near_pack, "gx", on_chip_pairs)
    arrived = lax.all_to_all(sorted_source, "gx", split_axis=0, concat_axis=0, tiled=True)
    inject, offsets = call(
        prep_kernel,
        (planes(STEPS, ext), jax.ShapeDtypeStruct((16, depth), f32)),
        (receiver_row, receiver_column, receiver_traces, angle_table),
        [vmem] * 3 + [smem],
        [],
        8 * wide,
        60 * rows,
    )
    now, mid, coeffs, slope_z = call(
        early_kernel,
        (planes(2, rows), planes(2, ext), planes(5, ext), planes(rows)),
        (wave_now, on_chip, off_chip, own_coeffs, base, slopes, inject, matrices),
        [vmem] * 8,
        [
            room(ext),
            room(ext),
            pltpu.VMEM((2, ext) + plane, f32),
            *[room(ext)] * 4,
            room(ext, padded),
        ],
        26 * wide,
        400 * rows,
    )

    def side(tail):
        if rows == HALO:
            return now
        return lax.dynamic_slice_in_dim(now, jnp.where(tail, rows - HALO, 0), HALO, axis=1)

    off_chip = lax.ppermute(side(odd == 1), both_axes, off_chip_pairs)
    on_chip = lax.ppermute(side(odd == 0), "gx", on_chip_pairs)
    flux, base, slopes = call(
        side_kernel,
        (planes(3, rows), planes(2, rows), planes(2, rows)),
        (wave_now, mid, slope_z, now, coeffs, matrices),
        [vmem] * 6,
        [room(ext, padded), room(ext, padded), *[room(ext)] * 5],
        18 * wide,
        60 * rows,
    )
    final, imaged = call(
        late_kernel,
        (planes(2, rows), planes(4, rows)),
        (now, mid, coeffs, on_chip, off_chip, base, slopes, inject, matrices),
        [vmem] * 9,
        [room(wide, padded), *[room(wide)] * 5, room(ext, padded), room(ext)],
        28 * wide,
        400 * rows,
    )
    return call(
        image_kernel,
        (jax.ShapeDtypeStruct((NBIN, rows) + plane, jnp.bfloat16), planes(2, rows)),
        (arrived, mid, flux, imaged, offsets, final),
        [vmem] * 6,
        [
            pltpu.VMEM((NBIN, rows) + plane, jnp.bfloat16),
            pltpu.VMEM((sorted_source.size // depth, depth), f32),
            pltpu.SemaphoreType.DMA((1 + OUT_PIECES,)),
        ],
        16 * wide,
        60 * rows,
        (in_hbm, in_hbm),
    )


def solution(mesh):
    placed = (
        P("shot", "gx", None, None),
        P("shot", "gx", None, None),
        P("gx", None, None),
        P("gx", None, None),
        P("gx", None, None),
        P("gx", None, None),
        P("shot", None, None, "gx", None),
        P("shot"),
        P("shot"),
        P("shot", None),
        P(),
    )
    return jax.shard_map(
        local,
        mesh=mesh,
        in_specs=placed,
        out_specs=(P("shot", "gx", None, None), P("shot", "gx", None, None)),
        check_vma=False,
    )
```

```python
import math

import jax
import jax.numpy as jnp
import numpy as np
from jax import lax
from jax.experimental import pallas as pl
from jax.experimental.pallas import tpu as pltpu
from jax.sharding import PartitionSpec as P


STEPS = 4
NBIN = 8
REC_DEPTH = 2
REACH = 4
HALO = 2 * REACH
YPAD = 8
OUT_PIECES = 4

SECOND = (-205.0 / 72.0, 8.0 / 5.0, -1.0 / 5.0, 8.0 / 315.0, -1.0 / 560.0)
FIRST = (4.0 / 5.0, -1.0 / 5.0, 4.0 / 105.0, -1.0 / 280.0)


def exchange_order(count):
    step = next(n for n in (5, 7, 3, 1) if math.gcd(n, count) == 1)
    return [(count // 2 - 1 + step * j) % count for j in range(count)]


def each_row(count, width, body):
    if width <= 16:
        for row in range(count):
            body(row)
    else:
        lax.fori_loop(0, count, lambda row, carry: (body(row), carry)[1], 0)


def each_chunk(count, width, body):
    size = max(1, min(count, 512 // width))
    while count % size:
        size -= 1
    if count // size <= 2:
        for start in range(0, count, size):
            body(start, size)
    else:
        lax.fori_loop(0, count // size, lambda i, carry: (body(i * size, size), carry)[1], 0)


def second(centre, pairs):
    total = SECOND[0] * centre
    for k in range(1, 5):
        plus, minus = pairs(k)
        total = total + SECOND[k] * (plus + minus)
    return total


def first(pairs):
    total = None
    for k in range(1, 5):
        plus, minus = pairs(k)
        term = FIRST[k - 1] * (plus - minus)
        total = term if total is None else total + term
    return total


def build_matrices(out):
    depth = out.shape[1]
    slope = {k: -FIRST[k - 1] for k in range(1, 5)}
    slope = {d: c for k, v in slope.items() for d, c in ((-k, v), (k, -v))}
    curve = {d: SECOND[abs(d)] for d in range(-4, 5)}
    line = lax.broadcasted_iota(jnp.int32, (depth, depth), 0)
    apart = line - lax.broadcasted_iota(jnp.int32, (depth, depth), 1)
    hits = {d: apart == d for d in range(-4, 5)}
    for side, coefficients in enumerate((slope, curve)):
        rest = {d: np.float32(c) for d, c in coefficients.items()}
        for part in range(3):
            rounded = {d: c.astype(jnp.bfloat16).astype(np.float32) for d, c in rest.items()}
            rest = {d: c - rounded[d] for d, c in rest.items()}
            values = jnp.zeros((depth, depth), jnp.float32)
            for d, c in rounded.items():
                values = jnp.where(hits[d], float(c), values)
            out[part, :, side * depth : (side + 1) * depth] = values.astype(jnp.bfloat16)


def depth_diffs(field, matrices):
    depth = field.shape[1]
    high = field.astype(jnp.bfloat16)
    rest = field - high.astype(jnp.float32)
    middle = rest.astype(jnp.bfloat16)
    low = (rest - middle.astype(jnp.float32)).astype(jnp.bfloat16)
    m_high, m_middle, m_low = matrices[0], matrices[1], matrices[2]

    def product(left, top, bottom):
        return jnp.dot(
            left, jnp.concatenate([top, bottom], axis=0), preferred_element_type=jnp.float32
        )

    upper = jnp.concatenate([high, middle], axis=1)
    lower = jnp.concatenate([high, low], axis=1)
    both = (
        product(lower, m_low, m_high)
        + product(upper, m_middle, m_middle)
        + product(upper, m_high, m_high)
    )
    return both[:, :depth], both[:, depth:]


def depth_rows(read, slope, curve, begin, count, width, matrices, shift=0):
    def chunk(start, size):
        field = read(begin + start, size)
        depth = field.shape[-1]
        s, c = depth_diffs(field.reshape(size * width, depth), matrices)
        slope[pl.ds(begin + shift + start, size)] = s.reshape(size, width, depth)
        curve[pl.ds(begin + shift + start, size)] = c.reshape(size, width, depth)

    each_chunk(count, width, chunk)


def sine_terms(angle):
    half = 0.5 * angle
    sq = half * half
    s = 1.0
    for n in (12 * 13, 10 * 11, 8 * 9, 6 * 7, 4 * 5, 2 * 3):
        s = 1.0 - sq * s * (1.0 / n)
    s = s * half
    c = 1.0
    for n in (13 * 14, 11 * 12, 9 * 10, 7 * 8, 5 * 6, 3 * 4, 1 * 2):
        c = 1.0 - sq * c * (1.0 / n)
    sine = 2.0 * s * c
    cosine = 1.0 - 2.0 * s * s
    return sine * sine, 2.0 * sine * cosine


def derive(coeffs, at, s, e, d, a):
    coeffs[0, at] = s
    coeffs[1, at] = s * (1.0 + 2.0 * e)
    coeffs[2, at] = s * jnp.sqrt(1.0 + 2.0 * d)
    coeffs[3, at], coeffs[4, at] = sine_terms(a)


def receivers(row_ref, column_ref, rows, width):
    begin = lax.axis_index("gx") * rows - REACH
    count = row_ref.shape[0]
    local_row = row_ref[...].reshape(1, count) - begin
    inside = (local_row >= 0) & (local_row < rows + 2 * REACH)
    return jnp.where(inside, local_row * width + column_ref[...].reshape(1, count), -1)


def time_step(begin, rows, width, fields, earlier, coeffs, slopes, curves, emit):
    p, q = fields
    slope_p, slope_q = slopes
    curve_p, curve_q = curves
    inner = slice(YPAD, YPAD + width)

    def update(row):
        at = row + REACH
        now_p = p[at, inner, :]
        now_q = q[at]
        xx_p = second(now_p, lambda k: (p[at + k, inner, :], p[at - k, inner, :]))
        xx_q = second(now_q, lambda k: (q[at + k], q[at - k]))
        xz_p = first(lambda k: (slope_p[at + k], slope_p[at - k]))
        xz_q = first(lambda k: (slope_q[at + k], slope_q[at - k]))
        yy_p = second(
            now_p,
            lambda k: (
                p[at, YPAD + k : YPAD + k + width, :],
                p[at, YPAD - k : YPAD - k + width, :],
            ),
        )
        speed, gain, mixed, sine_sq, sine_double = coeffs(row)
        tilt_p = sine_sq * (xx_p - curve_p[at]) + sine_double * xz_p
        tilt_q = sine_sq * (xx_q - curve_q[at]) + sine_double * xz_q
        across = xx_p + yy_p - tilt_p
        rotated = curve_q[at] + tilt_q
        prev_p, prev_q = earlier(row)
        next_p = 2.0 * now_p - prev_p + (gain * across + mixed * rotated)
        next_q = 2.0 * now_q - prev_q + (mixed * across + speed * rotated)
        emit(row, next_p, next_q)

    each_row(rows, width, lambda row: update(begin + row))


def border_terms(row, rows, read, slope):
    curve, mixed = None, None
    for border in (REACH, rows + REACH):
        for k in range(1, 5):
            for other, sign in ((row + k, 1.0), (row - k, -1.0)):
                low, high = min(row, other), max(row, other)
                if low < border <= high:
                    c = SECOND[k] * read(other)
                    m = (sign * FIRST[k - 1]) * slope(other)
                    curve = c if curve is None else curve + c
                    mixed = m if mixed is None else mixed + m
    return curve, mixed


def add_border(row, rows, reads, slopes, coeffs, base):
    next_p, next_q = base
    xx_p, xz_p = border_terms(row, rows, reads[0], slopes[0])
    if xx_p is None:
        return next_p, next_q
    xx_q, xz_q = border_terms(row, rows, reads[1], slopes[1])
    speed, gain, mixed, sine_sq, sine_double = coeffs
    across = xx_p - (sine_sq * xx_p + sine_double * xz_p)
    rotated = sine_sq * xx_q + sine_double * xz_q
    return (
        next_p + (gain * across + mixed * rotated),
        next_q + (mixed * across + speed * rotated),
    )


def block_step(rows, width, fields, slopes, curves, matrices, earlier, coeffs, emit):
    p, q = fields
    inner = slice(YPAD, YPAD + width)
    for field, slope, curve in (
        (lambda b, n: p[pl.ds(b, n), inner, :], slopes[0], curves[0]),
        (lambda b, n: q[pl.ds(b, n)], slopes[1], curves[1]),
    ):
        depth_rows(field, slope, curve, REACH, rows, width, matrices)
    time_step(0, rows, width, fields, earlier, coeffs, slopes, curves, emit)


def clear_sides(rows, *refs):
    for ref in refs:
        zeros = jnp.zeros((REACH,) + ref.shape[1:], jnp.float32)
        ref[pl.ds(0, REACH)] = zeros
        ref[pl.ds(rows + REACH, REACH)] = zeros


def flux_row(row, width, p, slope_z, before):
    at = row + REACH
    now = p[at, YPAD : YPAD + width, :]
    back = before - now
    slope_x = first(
        lambda k: (p[at + k, YPAD : YPAD + width, :], p[at - k, YPAD : YPAD + width, :])
    )
    slope_y = first(
        lambda k: (p[at, YPAD + k : YPAD + k + width, :], p[at, YPAD - k : YPAD - k + width, :])
    )
    return now, (back * slope_x, back * slope_y, back * slope_z)


def image_terms(source, field, flux, offsets, emit):
    fx, fy, fz = flux
    s0, s1, s2, s3 = source
    dot = s1 * fx + s2 * fy + s3 * fz
    squares = (s1 * s1 + s2 * s2 + s3 * s3) * (fx * fx + fy * fy + fz * fz)
    cosine = dot * jnp.minimum(lax.rsqrt(squares), 1.0)
    scaled = (cosine + 1.0) * offsets[NBIN : NBIN + 1, :]
    strength = s0 * field
    above = strength
    for b in range(NBIN - 1):
        beyond = jnp.clip(scaled - offsets[b + 1 : b + 2, :], 0.0, 1.0) * strength
        emit(b, above - beyond)
        above = beyond
    emit(NBIN - 1, above)


def clear_pads(ref, width):
    rows, _, depth = ref.shape
    zeros = jnp.zeros((rows, YPAD, depth), jnp.float32)
    ref[:, :YPAD, :] = zeros
    ref[:, YPAD + width :, :] = zeros


def place(dst_p, dst_q, centre, sides, width):
    inner = pl.ds(YPAD, width)
    for at, count, read in ((HALO, centre.shape[1], lambda f: centre[f]), *sides):
        dst_p[pl.ds(at, count), inner, :] = read(0)
        dst_q[pl.ds(at, count)] = read(1)


def side_starts(rows, reach):
    odd = lax.rem(lax.axis_index("gx"), 2)
    on_chip = jnp.where(odd == 1, 0, rows + reach)
    off_chip = jnp.where(odd == 1, rows + reach, 0)
    return on_chip, off_chip


def has_far_side():
    at = lax.axis_index("gx")
    return (at > 0) & (at < lax.axis_size("gx") - 1)


def second_step(rows, width, p1, q1, slopes, curves, earlier, coeffs, inject, matrices, emit):
    inner = slice(YPAD, YPAD + width)
    ext = rows + 2 * REACH
    depth_rows(
        lambda b, n: p1[pl.ds(b, n), inner, :], slopes[0], curves[0], 0, ext, width, matrices
    )
    depth_rows(lambda b, n: q1[pl.ds(b, n)], slopes[1], curves[1], 0, ext, width, matrices)

    def finish(row, next_p, next_q):
        emit(row, next_p + inject[row + REACH], next_q)

    time_step(
        0,
        rows,
        width,
        (p1, q1),
        earlier,
        lambda row: [coeffs[c, row + REACH] for c in range(5)],
        slopes,
        curves,
        finish,
    )


def pack_kernel(
    now,
    prev,
    speed,
    epsilon,
    delta,
    tilt,
    source,
    receiver_row,
    receiver_column,
    traces,
    table,
    far,
    near,
    sorted_source,
    coeffs,
    base,
    slopes,
    weights,
    row_out,
    column_out,
    traces_out,
    table_out,
    staged,
    p,
    q,
    before,
    medium,
    slope_p,
    slope_q,
    curve_p,
    curve_q,
    sems,
):
    rows, width = now.shape[1], now.shape[2]
    odd = lax.rem(lax.axis_index("gx"), 2)
    started = []

    def copy(src, dst):
        started.append(pltpu.make_async_copy(src, dst, sems.at[len(started)]))
        started[-1].start()
        return started[-1]

    arriving = []
    for place, owner in enumerate(exchange_order(source.shape[2])):
        arriving.append(copy(source.at[:, :, owner], staged.at[place]))
    clear_pads(p, width)
    clear_sides(rows, p, q, slope_p, slope_q)
    own = pl.ds(REACH, rows)
    inner = slice(YPAD, YPAD + width)
    local = [copy(field, medium.at[m]) for m, field in enumerate((speed, epsilon, delta, tilt))]
    local.append(copy(now.at[0], p.at[own, pl.ds(YPAD, width)]))
    local.append(copy(now.at[1], q.at[own]))
    local.append(copy(prev, before))
    local.append(copy(receiver_row, row_out))
    local.append(copy(receiver_column, column_out))
    local.append(copy(traces, traces_out))
    local.append(copy(table, table_out))
    build_matrices(weights)
    for one in arriving:
        one.wait()
    leaving = copy(staged, sorted_source)
    for one in local:
        one.wait()
    each_row(rows, width, lambda r: derive(coeffs, r, *[medium[m, r] for m in range(4)]))

    def emit(row, next_p, next_q):
        base[0, row] = next_p
        base[1, row] = next_q

    block_step(
        rows,
        width,
        (p, q),
        (slope_p, slope_q),
        (curve_p, curve_q),
        weights,
        lambda row: (before[0, row], before[1, row]),
        lambda row: [coeffs[c, row] for c in range(5)],
        emit,
    )
    slopes[0] = slope_p[own]
    slopes[1] = slope_q[own]
    for out, tail in ((far, odd), (near, 1 - odd)):
        first_row = tail * (rows - REACH)
        edge = pl.ds(first_row, REACH)
        edge_fields = [
            p[pl.ds(REACH + first_row, REACH), inner, :],
            q[pl.ds(REACH + first_row, REACH)],
            base[0, edge],
            base[1, edge],
            *[medium[m, edge] for m in range(4)],
        ]
        for index, value in enumerate(edge_fields):
            out[pl.ds(index * REACH, REACH)] = value
    leaving.wait()


def prep_kernel(receiver_row, receiver_column, traces, table, inject, offsets):
    _, ext, width, depth = inject.shape
    flat = receivers(receiver_row, receiver_column, ext - 2 * REACH, width)
    count = flat.shape[1]
    at_depth = lax.broadcasted_iota(jnp.int32, (depth, count), 0) == REC_DEPTH
    parts = []
    rest = traces[...]
    for _ in range(3):
        parts.append(rest.astype(jnp.bfloat16).astype(jnp.float32))
        rest = rest - parts[-1]
    samples = [
        jnp.concatenate(
            [jnp.where(at_depth, part[t : t + 1, :], 0.0) for t in range(STEPS)], axis=0
        ).astype(jnp.bfloat16)
        for part in reversed(parts)
    ]

    def chunk(start, size):
        lines = size * width
        cell = lax.broadcasted_iota(jnp.int32, (lines, count), 0) + start * width
        hit = jnp.where(cell == flat, 1.0, 0.0).astype(jnp.bfloat16)
        total = None
        for sample in samples:
            term = lax.dot_general(
                hit, sample, (((1,), (1,)), ((), ())), preferred_element_type=jnp.float32
            )
            total = term if total is None else total + term
        for t in range(STEPS):
            part = total[:, t * depth : (t + 1) * depth]
            inject[t, pl.ds(start, size)] = part.reshape(size, width, depth)

    each_chunk(ext, width, chunk)
    fine = table.shape[0]
    names = table[...].reshape(1, fine)
    for b in range(NBIN):
        begin = jnp.sum((names < b).astype(jnp.float32), axis=1, keepdims=True) - 1.0
        offsets[b : b + 1, :] = jnp.broadcast_to(begin, (1, depth))
    offsets[NBIN : NBIN + 1, :] = jnp.full((1, depth), 0.5 * (fine - 1), jnp.float32)


def early_kernel(
    now,
    on_chip,
    off_chip,
    own_coeffs,
    base,
    own_slopes,
    inject,
    matrices,
    out,
    far_near,
    far_outer,
    mid,
    coeffs,
    slope_out,
    p,
    q,
    ext_base,
    slope_p,
    slope_q,
    curve_p,
    curve_q,
    p1,
):
    rows, width = now.shape[1], now.shape[2]
    inner = slice(YPAD, YPAD + width)
    near, far = side_starts(rows, REACH)
    inside = has_far_side()
    clear_pads(p1, width)
    own = pl.ds(REACH, rows)
    p[own], q[own] = now[0], now[1]
    slope_p[own], slope_q[own] = own_slopes[0], own_slopes[1]
    for f in range(2):
        ext_base[f, own] = base[f]
    for c in range(5):
        coeffs[c, own] = own_coeffs[c]
    for at, part, real in ((near, on_chip, None), (far, off_chip, inside)):

        def take(index, real=real, part=part):
            value = part[pl.ds(index * REACH, REACH)]
            return value if real is None else jnp.where(real, value, 0.0)

        side = pl.ds(at, REACH)
        p[side], q[side] = take(0), take(1)
        ext_base[0, side], ext_base[1, side] = take(2), take(3)
        medium = [take(4)] + [part[pl.ds((5 + m) * REACH, REACH)] for m in range(3)]
        for r in range(REACH):
            derive(coeffs, at + r, *[m[r] for m in medium])
    for begin in (0, rows + REACH):
        depth_rows(lambda b, n: p[pl.ds(b, n)], slope_p, curve_p, begin, REACH, width, matrices)
        depth_rows(lambda b, n: q[pl.ds(b, n)], slope_q, curve_q, begin, REACH, width, matrices)
    q1 = mid.at[1]
    for row in range(rows + 2 * REACH):
        next_p, next_q = add_border(
            row,
            rows,
            (lambda i: p[i], lambda i: q[i]),
            (lambda i: slope_p[i], lambda i: slope_q[i]),
            [coeffs[c, row] for c in range(5)],
            (ext_base[0, row], ext_base[1, row]),
        )
        next_p = next_p + inject[0, row]
        p1[row, inner, :] = next_p
        mid[0, row] = next_p
        mid[1, row] = next_q

    def emit(row, next_p, next_q):
        out[0, row] = next_p
        out[1, row] = next_q

    second_step(
        rows,
        width,
        p1,
        q1,
        (slope_p, slope_q),
        (curve_p, curve_q),
        lambda row: (now[0, row], now[1, row]),
        coeffs,
        inject.at[1],
        matrices,
        emit,
    )
    slope_out[...] = slope_p[own]
    tail = lax.rem(lax.axis_index("gx"), 2)
    for f in range(2):
        far_near[f] = out[f, pl.ds(tail * (rows - REACH), REACH)]
        outer = out[f, pl.ds(REACH + tail * (rows - HALO - REACH), REACH)]
        far_outer[f] = outer.astype(far_outer.dtype)


def side_kernel(
    before,
    mid,
    slope_z,
    now,
    coeffs,
    matrices,
    flux,
    base,
    slopes,
    p1,
    p,
    q,
    slope_p,
    slope_q,
    curve_p,
    curve_q,
):
    rows, width = before.shape[1], before.shape[2]
    own = pl.ds(REACH, rows)
    clear_pads(p1, width)
    p1[:, YPAD : YPAD + width, :] = mid[0]

    def fluxes(row):
        _, parts = flux_row(row, width, p1, slope_z[row], before[0, row])
        for a in range(3):
            flux[a, row] = parts[a]

    each_row(rows, width, fluxes)
    clear_pads(p, width)
    clear_sides(rows, p, q, slope_p, slope_q)
    p[own, YPAD : YPAD + width, :] = now[0]
    q[own] = now[1]

    def emit(row, next_p, next_q):
        base[0, row] = next_p
        base[1, row] = next_q

    block_step(
        rows,
        width,
        (p, q),
        (slope_p, slope_q),
        (curve_p, curve_q),
        matrices,
        lambda row: (mid[0, row + REACH], mid[1, row + REACH]),
        lambda row: [coeffs[c, row + REACH] for c in range(5)],
        emit,
    )
    slopes[0] = slope_p[own]
    slopes[1] = slope_q[own]


def late_kernel(
    now,
    mid,
    coeffs,
    on_chip,
    off_near,
    off_outer,
    base,
    own_slopes,
    inject,
    matrices,
    out,
    imaged,
    p,
    q,
    slope_p,
    slope_q,
    curve_p,
    curve_q,
    p1,
    q1,
):
    rows, width = now.shape[1], now.shape[2]
    inner = slice(YPAD, YPAD + width)
    near, far = side_starts(rows, HALO)
    inside = has_far_side()
    odd = lax.rem(lax.axis_index("gx"), 2)
    clear_pads(p, width)
    clear_pads(p1, width)

    def far_rows(part, f):
        return jnp.where(inside, part[f].astype(jnp.float32), 0.0)

    place(
        p,
        q,
        now,
        (
            (near, HALO, lambda f: on_chip[f]),
            (far + (1 - odd) * REACH, REACH, lambda f: far_rows(off_near, f)),
            (far + odd * REACH, REACH, lambda f: far_rows(off_outer, f)),
        ),
        width,
    )
    own = pl.ds(HALO, rows)
    slope_p[own], slope_q[own] = own_slopes[0], own_slopes[1]
    for begin in (0, rows + HALO):
        depth_rows(
            lambda b, n: p[pl.ds(b, n), inner, :], slope_p, curve_p, begin, HALO, width, matrices
        )
        depth_rows(lambda b, n: q[pl.ds(b, n)], slope_q, curve_q, begin, HALO, width, matrices)

    def keep(row, next_p, next_q):
        p1[row, inner, :] = next_p + inject[2, row]
        q1[row] = next_q

    for begin in (0, rows + REACH):
        time_step(
            begin,
            REACH,
            width,
            (p, q),
            lambda row: (mid[0, row], mid[1, row]),
            lambda row: [coeffs[c, row] for c in range(5)],
            (slope_p, slope_q),
            (curve_p, curve_q),
            keep,
        )
    for row in range(REACH, rows + REACH):
        result = add_border(
            row,
            rows,
            (lambda i: p[i + REACH, inner, :], lambda i: q[i + REACH]),
            (lambda i: slope_p[i + REACH], lambda i: slope_q[i + REACH]),
            [coeffs[c, row] for c in range(5)],
            (base[0, row - REACH], base[1, row - REACH]),
        )
        keep(row, *result)

    def emit(row, next_p, next_q):
        out[0, row] = next_p
        out[1, row] = next_q

    second_step(
        rows,
        width,
        p1,
        q1,
        (slope_p, slope_q),
        (curve_p, curve_q),
        lambda row: (now[0, row], now[1, row]),
        coeffs,
        inject.at[3],
        matrices,
        emit,
    )

    def fluxes(row):
        field, parts = flux_row(row, width, p1, slope_p[row + REACH], now[0, row])
        for a, value in enumerate((field, *parts)):
            imaged[a, row] = value

    each_row(rows, width, fluxes)


def image_kernel(
    arrived, mid, flux, imaged, offsets, wave, images, wave_out, block, lines, sems
):
    rows, width, depth = flux.shape[1:]
    whole = pltpu.make_async_copy(wave, wave_out, sems.at[0])
    whole.start()
    parts = arrived.shape[2]
    stride = lines.shape[0] // width
    for place, column in enumerate(exchange_order(width)):
        block_lines = arrived[place].astype(jnp.float32).reshape(stride, depth)
        lines[column * stride : (column + 1) * stride, :] = block_lines

    def source(n, row):
        begin = n * parts * rows + row
        return [lines[pl.ds(begin + c * rows, width, stride=stride), :] for c in range(parts)]

    def image_row(row):
        totals = [None] * NBIN

        def keep(b, term):
            totals[b] = term

        def finish(b, term):
            block[b, row] = (totals[b] + term).astype(block.dtype)

        early = [flux[a, row] for a in range(3)]
        image_terms(source(0, row), mid[0, row + REACH], early, offsets, keep)
        late = [imaged[a, row] for a in range(1, 4)]
        image_terms(source(1, row), imaged[0, row], late, offsets, finish)

    pieces = []
    size = rows // OUT_PIECES
    for piece in range(OUT_PIECES):
        each_row(size, width, lambda row: image_row(row + piece * size))
        part = pl.ds(piece * size, size)
        pieces.append(
            pltpu.make_async_copy(block.at[:, part], images.at[:, part], sems.at[1 + piece])
        )
        pieces[-1].start()
    for piece in pieces:
        piece.wait()
    whole.wait()


def local(
    wave_now,
    wave_prev,
    speed_term,
    thomsen_epsilon,
    thomsen_delta,
    tilt_angle,
    source_store,
    receiver_row,
    receiver_column,
    receiver_traces,
    angle_table,
):
    _, rows, width, depth = wave_now.shape
    count = lax.axis_size("gx")
    odd = lax.rem(lax.axis_index("gx"), 2)
    on_chip_pairs = [(i, i ^ 1) for i in range(count)]
    both_axes = ("shot", "gx")
    shots = lax.axis_size("shot")
    off_chip_pairs = []
    for shot in range(shots):
        at = shot * count
        for i in range(1, count - 1, 2):
            off_chip_pairs += [(at + i, at + i + 1), (at + i + 1, at + i)]
        other = ((shot + 1) % shots) * count
        if shots > 1:
            off_chip_pairs += [(at, other), (at + count - 1, other + count - 1)]

    f32 = jnp.float32
    ext, wide = rows + 2 * REACH, rows + 2 * HALO
    vmem = pl.BlockSpec(memory_space=pltpu.VMEM)
    in_hbm = pl.BlockSpec(memory_space=pltpu.HBM)
    plane = (width, depth)
    padded = (width + 2 * YPAD, depth)
    plane_bytes = 4 * width * depth
    line_flops = width * depth

    def planes(*lead):
        return jax.ShapeDtypeStruct(lead + plane, f32)

    def call(kernel, outs, ins, in_specs, scratch, grant, cost, out_specs=None):
        return pl.pallas_call(
            kernel,
            out_shape=outs,
            in_specs=in_specs,
            out_specs=out_specs or jax.tree.map(lambda _: vmem, outs),
            scratch_shapes=scratch,
            compiler_params=pltpu.CompilerParams(
                vmem_limit_bytes=4 * 1024 * 1024 + grant * plane_bytes
            ),
            cost_estimate=pl.CostEstimate(
                flops=cost * line_flops, bytes_accessed=cost * line_flops // 4, transcendentals=0
            ),
        )(*ins)

    def room(count, lines=plane):
        return pltpu.VMEM((count,) + lines, f32)

    medium = (speed_term, thomsen_epsilon, thomsen_delta, tilt_angle)
    matrices = jax.ShapeDtypeStruct((3, depth, 2 * depth), jnp.bfloat16)
    snaps, parts = source_store.shape[:2]
    by_owner = source_store.reshape(snaps, parts, count, rows, depth)
    sorted_shape = (count, snaps, parts, rows, depth)
    packed = planes(8 * REACH)
    tables = (receiver_row, receiver_column, receiver_traces, angle_table)
    far_pack, near_pack, sorted_source, own_coeffs, base, slopes, matrices, *small = call(
        pack_kernel,
        (
            packed,
            packed,
            jax.ShapeDtypeStruct(sorted_shape, source_store.dtype),
            planes(5, rows),
            planes(2, rows),
            planes(2, rows),
            matrices,
            *[jax.ShapeDtypeStruct(x.shape, x.dtype) for x in tables],
        ),
        [
            pltpu.with_memory_space_constraint(x, pltpu.HBM)
            for x in (wave_now, wave_prev, *medium, by_owner, *tables)
        ],
        [in_hbm] * 11,
        [
            pltpu.VMEM(sorted_shape, source_store.dtype),
            room(ext, padded),
            room(ext),
            pltpu.VMEM((2, rows) + plane, f32),
            pltpu.VMEM((4, rows) + plane, f32),
            *[room(ext)] * 4,
            pltpu.SemaphoreType.DMA((12 + count,)),
        ],
        16 * wide,
        200,
        (vmem, vmem, in_hbm, *[vmem] * 8),
    )
    off_chip = lax.ppermute(far_pack, both_axes, off_chip_pairs)
    on_chip = lax.ppermute(near_pack, "gx", on_chip_pairs)
    arrived = lax.all_to_all(
        sorted_source,
        "gx",
        split_axis=0,
        concat_axis=0,
        tiled=True,
        axis_index_groups=[exchange_order(count)],
    )
    inject, offsets = call(
        prep_kernel,
        (planes(STEPS, ext), jax.ShapeDtypeStruct((16, depth), f32)),
        small,
        [vmem] * 4,
        [],
        8 * wide,
        60 * rows,
    )
    now, far_near, far_outer, mid, coeffs, slope_z = call(
        early_kernel,
        (
            planes(2, rows),
            planes(2, REACH),
            jax.ShapeDtypeStruct((2, REACH) + plane, jnp.bfloat16),
            planes(2, ext),
            planes(5, ext),
            planes(rows),
        ),
        (wave_now, on_chip, off_chip, own_coeffs, base, slopes, inject, matrices),
        [vmem] * 8,
        [
            room(ext),
            room(ext),
            pltpu.VMEM((2, ext) + plane, f32),
            *[room(ext)] * 4,
            room(ext, padded),
        ],
        26 * wide,
        400 * rows,
    )

    def side(tail):
        if rows == HALO:
            return now
        return lax.dynamic_slice_in_dim(now, jnp.where(tail, rows - HALO, 0), HALO, axis=1)

    off_near = lax.ppermute(far_near, both_axes, off_chip_pairs)
    off_outer = lax.ppermute(far_outer, both_axes, off_chip_pairs)
    on_chip = lax.ppermute(side(odd == 0), "gx", on_chip_pairs)
    flux, base, slopes = call(
        side_kernel,
        (planes(3, rows), planes(2, rows), planes(2, rows)),
        (wave_now, mid, slope_z, now, coeffs, matrices),
        [vmem] * 6,
        [room(ext, padded), room(ext, padded), *[room(ext)] * 5],
        18 * wide,
        60 * rows,
    )
    final, imaged = call(
        late_kernel,
        (planes(2, rows), planes(4, rows)),
        (now, mid, coeffs, on_chip, off_near, off_outer, base, slopes, inject, matrices),
        [vmem] * 10,
        [room(wide, padded), *[room(wide)] * 5, room(ext, padded), room(ext)],
        28 * wide,
        400 * rows,
    )
    return call(
        image_kernel,
        (jax.ShapeDtypeStruct((NBIN, rows) + plane, jnp.bfloat16), planes(2, rows)),
        (arrived, mid, flux, imaged, offsets, final),
        [vmem] * 6,
        [
            pltpu.VMEM((NBIN, rows) + plane, jnp.bfloat16),
            pltpu.VMEM((sorted_source.size // depth, depth), f32),
            pltpu.SemaphoreType.DMA((1 + OUT_PIECES,)),
        ],
        16 * wide,
        60 * rows,
        (in_hbm, in_hbm),
    )


def solution(mesh):
    placed = (
        P("shot", "gx", None, None),
        P("shot", "gx", None, None),
        P("gx", None, None),
        P("gx", None, None),
        P("gx", None, None),
        P("gx", None, None),
        P("shot", None, None, "gx", None),
        P("shot"),
        P("shot"),
        P("shot", None),
        P(),
    )
    return jax.shard_map(
        local,
        mesh=mesh,
        in_specs=placed,
        out_specs=(P("shot", "gx", None, None), P("shot", "gx", None, None)),
        check_vma=False,
    )
```

```python
import math

import jax
import jax.numpy as jnp
import numpy as np
from jax import lax
from jax.experimental import pallas as pl
from jax.experimental.pallas import tpu as pltpu
from jax.sharding import PartitionSpec as P


STEPS = 4
NBIN = 8
REC_DEPTH = 2
REACH = 4
HALO = 2 * REACH
YPAD = 8
OUT_PIECES = 4

SECOND = (-205.0 / 72.0, 8.0 / 5.0, -1.0 / 5.0, 8.0 / 315.0, -1.0 / 560.0)
FIRST = (4.0 / 5.0, -1.0 / 5.0, 4.0 / 105.0, -1.0 / 280.0)


def exchange_order(count):
    step = next(n for n in (13, 5, 3, 1) if math.gcd(n, count) == 1)
    return [(count // 2 - 1 + step * j) % count for j in range(count)]


def each_row(count, width, body):
    if width <= 16:
        for row in range(count):
            body(row)
    else:
        lax.fori_loop(0, count, lambda row, carry: (body(row), carry)[1], 0)


def each_chunk(count, width, body):
    size = max(1, min(count, 256 // width))
    while count % size:
        size -= 1
    if count // size <= 2:
        for start in range(0, count, size):
            body(start, size)
    else:
        lax.fori_loop(0, count // size, lambda i, carry: (body(i * size, size), carry)[1], 0)


def second(centre, pairs):
    total = SECOND[0] * centre
    for k in range(1, 5):
        plus, minus = pairs(k)
        total = total + SECOND[k] * (plus + minus)
    return total


def first(pairs):
    total = None
    for k in range(1, 5):
        plus, minus = pairs(k)
        term = FIRST[k - 1] * (plus - minus)
        total = term if total is None else total + term
    return total


def build_matrices(out):
    depth = out.shape[1]
    slope = {k: -FIRST[k - 1] for k in range(1, 5)}
    slope = {d: c for k, v in slope.items() for d, c in ((-k, v), (k, -v))}
    curve = {d: SECOND[abs(d)] for d in range(-4, 5)}
    line = lax.broadcasted_iota(jnp.int32, (depth, depth), 0)
    apart = line - lax.broadcasted_iota(jnp.int32, (depth, depth), 1)
    hits = {d: apart == d for d in range(-4, 5)}
    for side, coefficients in enumerate((slope, curve)):
        rest = {d: np.float32(c) for d, c in coefficients.items()}
        for part in range(3):
            rounded = {d: c.astype(jnp.bfloat16).astype(np.float32) for d, c in rest.items()}
            rest = {d: c - rounded[d] for d, c in rest.items()}
            values = jnp.zeros((depth, depth), jnp.float32)
            for d, c in rounded.items():
                values = jnp.where(hits[d], float(c), values)
            out[part, :, side * depth : (side + 1) * depth] = values.astype(jnp.bfloat16)


def depth_diffs(field, matrices):
    depth = field.shape[1]
    high = field.astype(jnp.bfloat16)
    rest = field - high.astype(jnp.float32)
    middle = rest.astype(jnp.bfloat16)
    low = (rest - middle.astype(jnp.float32)).astype(jnp.bfloat16)
    m_high, m_middle, m_low = matrices[0], matrices[1], matrices[2]

    def product(left, top, bottom):
        return jnp.dot(
            left, jnp.concatenate([top, bottom], axis=0), preferred_element_type=jnp.float32
        )

    upper = jnp.concatenate([high, middle], axis=1)
    lower = jnp.concatenate([high, low], axis=1)
    both = (
        product(lower, m_low, m_high)
        + product(upper, m_middle, m_middle)
        + product(upper, m_high, m_high)
    )
    return both[:, :depth], both[:, depth:]


def depth_rows(items, count, width, matrices):
    def chunk(start, size):
        lines = size * width
        fields = [read(begin + start, size) for read, _, _, begin in items]
        depth = fields[0].shape[-1]
        joined = jnp.concatenate([f.reshape(lines, depth) for f in fields], axis=0)
        slopes, curves = depth_diffs(joined, matrices)
        for i, (_, slope, curve, begin) in enumerate(items):
            part = slice(i * lines, (i + 1) * lines)
            rows = pl.ds(begin + start, size)
            slope[rows] = slopes[part].reshape(size, width, depth)
            if curve is not None:
                curve[rows] = curves[part].reshape(size, width, depth)

    each_chunk(count, width * len(items), chunk)


def sine_terms(angle):
    half = 0.5 * angle
    sq = half * half
    s = 1.0
    for n in (12 * 13, 10 * 11, 8 * 9, 6 * 7, 4 * 5, 2 * 3):
        s = 1.0 - sq * s * (1.0 / n)
    s = s * half
    c = 1.0
    for n in (13 * 14, 11 * 12, 9 * 10, 7 * 8, 5 * 6, 3 * 4, 1 * 2):
        c = 1.0 - sq * c * (1.0 / n)
    sine = 2.0 * s * c
    cosine = 1.0 - 2.0 * s * s
    return sine * sine, 2.0 * sine * cosine


def derive(coeffs, at, s, e, d, a):
    coeffs[0, at] = s
    coeffs[1, at] = s * (1.0 + 2.0 * e)
    coeffs[2, at] = s * jnp.sqrt(1.0 + 2.0 * d)
    coeffs[3, at], coeffs[4, at] = sine_terms(a)


def receivers(row_ref, column_ref, rows, width):
    begin = lax.axis_index("gx") * rows - REACH
    count = row_ref.shape[0]
    local_row = row_ref[...].reshape(1, count) - begin
    inside = (local_row >= 0) & (local_row < rows + 2 * REACH)
    return jnp.where(inside, local_row * width + column_ref[...].reshape(1, count), -1)


def time_step(begin, rows, width, fields, earlier, coeffs, slopes, curves, emit):
    p, q = fields
    slope_p, slope_q = slopes
    curve_p, curve_q = curves
    inner = slice(YPAD, YPAD + width)

    def update(row):
        at = row + REACH
        now_p = p[at, inner, :]
        now_q = q[at]
        xx_p = second(now_p, lambda k: (p[at + k, inner, :], p[at - k, inner, :]))
        xx_q = second(now_q, lambda k: (q[at + k], q[at - k]))
        xz_p = first(lambda k: (slope_p[at + k], slope_p[at - k]))
        xz_q = first(lambda k: (slope_q[at + k], slope_q[at - k]))
        yy_p = second(
            now_p,
            lambda k: (
                p[at, YPAD + k : YPAD + k + width, :],
                p[at, YPAD - k : YPAD - k + width, :],
            ),
        )
        speed, gain, mixed, sine_sq, sine_double = coeffs(row)
        tilt_p = sine_sq * (xx_p - curve_p[at]) + sine_double * xz_p
        tilt_q = sine_sq * (xx_q - curve_q[at]) + sine_double * xz_q
        across = xx_p + yy_p - tilt_p
        rotated = curve_q[at] + tilt_q
        prev_p, prev_q = earlier(row)
        next_p = 2.0 * now_p - prev_p + (gain * across + mixed * rotated)
        next_q = 2.0 * now_q - prev_q + (mixed * across + speed * rotated)
        emit(row, next_p, next_q)

    each_row(rows, width, lambda row: update(begin + row))


def border_terms(row, rows, read, slope):
    curve, mixed = None, None
    for border in (REACH, rows + REACH):
        for k in range(1, 5):
            for other, sign in ((row + k, 1.0), (row - k, -1.0)):
                low, high = min(row, other), max(row, other)
                if low < border <= high:
                    c = SECOND[k] * read(other)
                    m = (sign * FIRST[k - 1]) * slope(other)
                    curve = c if curve is None else curve + c
                    mixed = m if mixed is None else mixed + m
    return curve, mixed


def add_border(row, rows, reads, slopes, coeffs, base):
    next_p, next_q = base
    xx_p, xz_p = border_terms(row, rows, reads[0], slopes[0])
    if xx_p is None:
        return next_p, next_q
    xx_q, xz_q = border_terms(row, rows, reads[1], slopes[1])
    speed, gain, mixed, sine_sq, sine_double = coeffs
    across = xx_p - (sine_sq * xx_p + sine_double * xz_p)
    rotated = sine_sq * xx_q + sine_double * xz_q
    return (
        next_p + (gain * across + mixed * rotated),
        next_q + (mixed * across + speed * rotated),
    )


def block_step(rows, width, fields, slopes, curves, matrices, earlier, coeffs, emit):
    p, q = fields
    inner = slice(YPAD, YPAD + width)
    items = (
        (lambda b, n: p[pl.ds(b, n), inner, :], slopes[0], curves[0], REACH),
        (lambda b, n: q[pl.ds(b, n)], slopes[1], curves[1], REACH),
    )
    depth_rows(items, rows, width, matrices)
    time_step(0, rows, width, fields, earlier, coeffs, slopes, curves, emit)


def clear_sides(rows, *refs):
    for ref in refs:
        zeros = jnp.zeros((REACH,) + ref.shape[1:], jnp.float32)
        ref[pl.ds(0, REACH)] = zeros
        ref[pl.ds(rows + REACH, REACH)] = zeros


def flux_row(row, width, p, slope_z, before):
    at = row + REACH
    now = p[at, YPAD : YPAD + width, :]
    back = before - now
    slope_x = first(
        lambda k: (p[at + k, YPAD : YPAD + width, :], p[at - k, YPAD : YPAD + width, :])
    )
    slope_y = first(
        lambda k: (p[at, YPAD + k : YPAD + k + width, :], p[at, YPAD - k : YPAD - k + width, :])
    )
    return now, (back * slope_x, back * slope_y, back * slope_z)


def image_terms(source, field, flux, offsets, emit):
    fx, fy, fz = flux
    s0, s1, s2, s3 = source
    dot = s1 * fx + s2 * fy + s3 * fz
    squares = (s1 * s1 + s2 * s2 + s3 * s3) * (fx * fx + fy * fy + fz * fz)
    cosine = dot * jnp.minimum(lax.rsqrt(squares), 1.0)
    scaled = (cosine + 1.0) * offsets[NBIN : NBIN + 1, :]
    strength = s0 * field
    above = strength
    for b in range(NBIN - 1):
        beyond = jnp.clip(scaled - offsets[b + 1 : b + 2, :], 0.0, 1.0) * strength
        emit(b, above - beyond)
        above = beyond
    emit(NBIN - 1, above)


def clear_pads(ref, width):
    rows, _, depth = ref.shape
    zeros = jnp.zeros((rows, YPAD, depth), jnp.float32)
    ref[:, :YPAD, :] = zeros
    ref[:, YPAD + width :, :] = zeros


def place(dst_p, dst_q, centre, sides, width):
    inner = pl.ds(YPAD, width)
    for at, count, read in ((HALO, centre.shape[1], lambda f: centre[f]), *sides):
        dst_p[pl.ds(at, count), inner, :] = read(0)
        dst_q[pl.ds(at, count)] = read(1)


def side_starts(rows, reach):
    odd = lax.rem(lax.axis_index("gx"), 2)
    on_chip = jnp.where(odd == 1, 0, rows + reach)
    off_chip = jnp.where(odd == 1, rows + reach, 0)
    return on_chip, off_chip


def has_far_side():
    at = lax.axis_index("gx")
    return (at > 0) & (at < lax.axis_size("gx") - 1)


def second_step(rows, width, p1, q1, slopes, curves, earlier, coeffs, inject, matrices, emit):
    inner = slice(YPAD, YPAD + width)
    ext = rows + 2 * REACH
    items = (
        (lambda b, n: p1[pl.ds(b, n), inner, :], slopes[0], curves[0], 0),
        (lambda b, n: q1[pl.ds(b, n)], slopes[1], curves[1], 0),
    )
    depth_rows(items, ext, width, matrices)

    def finish(row, next_p, next_q):
        emit(row, next_p + inject[row + REACH], next_q)

    time_step(
        0,
        rows,
        width,
        (p1, q1),
        earlier,
        lambda row: [coeffs[c, row + REACH] for c in range(5)],
        slopes,
        curves,
        finish,
    )


def pack_kernel(
    now,
    prev,
    speed,
    epsilon,
    delta,
    tilt,
    source,
    receiver_row,
    receiver_column,
    traces,
    table,
    far,
    near,
    sorted_source,
    coeffs,
    base,
    slopes,
    weights,
    row_out,
    column_out,
    traces_out,
    table_out,
    staged,
    p,
    q,
    before,
    medium,
    slope_p,
    slope_q,
    curve_p,
    curve_q,
    sems,
):
    rows, width = now.shape[1], now.shape[2]
    odd = lax.rem(lax.axis_index("gx"), 2)
    started = []

    def copy(src, dst):
        started.append(pltpu.make_async_copy(src, dst, sems.at[len(started)]))
        started[-1].start()
        return started[-1]

    arriving = []
    for place, owner in enumerate(exchange_order(source.shape[2])):
        arriving.append(copy(source.at[:, :, owner], staged.at[place]))
    clear_pads(p, width)
    clear_sides(rows, p, q, slope_p, slope_q)
    own = pl.ds(REACH, rows)
    inner = slice(YPAD, YPAD + width)
    local = [copy(field, medium.at[m]) for m, field in enumerate((speed, epsilon, delta, tilt))]
    local.append(copy(now.at[0], p.at[own, pl.ds(YPAD, width)]))
    local.append(copy(now.at[1], q.at[own]))
    local.append(copy(prev, before))
    local.append(copy(receiver_row, row_out))
    local.append(copy(receiver_column, column_out))
    local.append(copy(traces, traces_out))
    local.append(copy(table, table_out))
    build_matrices(weights)
    for one in arriving:
        one.wait()
    leaving = copy(staged, sorted_source)
    for one in local:
        one.wait()
    each_row(rows, width, lambda r: derive(coeffs, r, *[medium[m, r] for m in range(4)]))

    def emit(row, next_p, next_q):
        base[0, row] = next_p
        base[1, row] = next_q

    block_step(
        rows,
        width,
        (p, q),
        (slope_p, slope_q),
        (curve_p, curve_q),
        weights,
        lambda row: (before[0, row], before[1, row]),
        lambda row: [coeffs[c, row] for c in range(5)],
        emit,
    )
    slopes[0] = slope_p[own]
    slopes[1] = slope_q[own]
    for out, tail in ((far, odd), (near, 1 - odd)):
        first_row = tail * (rows - REACH)
        edge = pl.ds(first_row, REACH)
        edge_fields = [
            p[pl.ds(REACH + first_row, REACH), inner, :],
            q[pl.ds(REACH + first_row, REACH)],
            base[0, edge],
            base[1, edge],
            *[medium[m, edge] for m in range(4)],
        ]
        for index, value in enumerate(edge_fields):
            out[pl.ds(index * REACH, REACH)] = value
    leaving.wait()


def prep_kernel(receiver_row, receiver_column, traces, table, inject, offsets):
    _, ext, width, depth = inject.shape
    flat = receivers(receiver_row, receiver_column, ext - 2 * REACH, width)
    count = flat.shape[1]
    at_depth = lax.broadcasted_iota(jnp.int32, (depth, count), 0) == REC_DEPTH
    parts = []
    rest = traces[...]
    for _ in range(3):
        parts.append(rest.astype(jnp.bfloat16).astype(jnp.float32))
        rest = rest - parts[-1]
    samples = [
        jnp.concatenate(
            [jnp.where(at_depth, part[t : t + 1, :], 0.0) for t in range(STEPS)], axis=0
        ).astype(jnp.bfloat16)
        for part in reversed(parts)
    ]

    def chunk(start, size):
        lines = size * width
        cell = lax.broadcasted_iota(jnp.int32, (lines, count), 0) + start * width
        hit = jnp.where(cell == flat, 1.0, 0.0).astype(jnp.bfloat16)
        total = None
        for sample in samples:
            term = lax.dot_general(
                hit, sample, (((1,), (1,)), ((), ())), preferred_element_type=jnp.float32
            )
            total = term if total is None else total + term
        for t in range(STEPS):
            part = total[:, t * depth : (t + 1) * depth]
            inject[t, pl.ds(start, size)] = part.reshape(size, width, depth)

    each_chunk(ext, width, chunk)
    fine = table.shape[0]
    names = table[...].reshape(1, fine)
    for b in range(NBIN):
        begin = jnp.sum((names < b).astype(jnp.float32), axis=1, keepdims=True) - 1.0
        offsets[b : b + 1, :] = jnp.broadcast_to(begin, (1, depth))
    offsets[NBIN : NBIN + 1, :] = jnp.full((1, depth), 0.5 * (fine - 1), jnp.float32)


def early_kernel(
    now,
    on_chip,
    off_chip,
    own_coeffs,
    base,
    own_slopes,
    inject,
    matrices,
    out,
    far_near,
    far_outer,
    mid,
    coeffs,
    slope_out,
    p,
    q,
    ext_base,
    slope_p,
    slope_q,
    curve_p,
    curve_q,
    p1,
):
    rows, width = now.shape[1], now.shape[2]
    inner = slice(YPAD, YPAD + width)
    near, far = side_starts(rows, REACH)
    inside = has_far_side()
    clear_pads(p1, width)
    own = pl.ds(REACH, rows)
    p[own], q[own] = now[0], now[1]
    slope_p[own], slope_q[own] = own_slopes[0], own_slopes[1]
    for f in range(2):
        ext_base[f, own] = base[f]
    for c in range(5):
        coeffs[c, own] = own_coeffs[c]
    for at, part, real in ((near, on_chip, None), (far, off_chip, inside)):

        def take(index, real=real, part=part):
            value = part[pl.ds(index * REACH, REACH)]
            return value if real is None else jnp.where(real, value, 0.0)

        side = pl.ds(at, REACH)
        p[side], q[side] = take(0), take(1)
        ext_base[0, side], ext_base[1, side] = take(2), take(3)
        medium = [take(4)] + [part[pl.ds((5 + m) * REACH, REACH)] for m in range(3)]
        for r in range(REACH):
            derive(coeffs, at + r, *[m[r] for m in medium])
    items = []
    for begin in (0, rows + REACH):
        items.append((lambda b, n: p[pl.ds(b, n)], slope_p, None, begin))
        items.append((lambda b, n: q[pl.ds(b, n)], slope_q, None, begin))
    depth_rows(items, REACH, width, matrices)
    q1 = mid.at[1]
    for row in range(rows + 2 * REACH):
        next_p, next_q = add_border(
            row,
            rows,
            (lambda i: p[i], lambda i: q[i]),
            (lambda i: slope_p[i], lambda i: slope_q[i]),
            [coeffs[c, row] for c in range(5)],
            (ext_base[0, row], ext_base[1, row]),
        )
        next_p = next_p + inject[0, row]
        p1[row, inner, :] = next_p
        mid[0, row] = next_p
        mid[1, row] = next_q

    def emit(row, next_p, next_q):
        out[0, row] = next_p
        out[1, row] = next_q

    second_step(
        rows,
        width,
        p1,
        q1,
        (slope_p, slope_q),
        (curve_p, curve_q),
        lambda row: (now[0, row], now[1, row]),
        coeffs,
        inject.at[1],
        matrices,
        emit,
    )
    slope_out[...] = slope_p[own]
    tail = lax.rem(lax.axis_index("gx"), 2)
    for f in range(2):
        far_near[f] = out[f, pl.ds(tail * (rows - REACH), REACH)]
        outer = out[f, pl.ds(REACH + tail * (rows - HALO - REACH), REACH)]
        far_outer[f] = outer.astype(far_outer.dtype)


def side_kernel(
    before,
    mid,
    slope_z,
    now,
    coeffs,
    matrices,
    flux,
    base,
    slopes,
    p1,
    p,
    q,
    slope_p,
    slope_q,
    curve_p,
    curve_q,
):
    rows, width = before.shape[1], before.shape[2]
    own = pl.ds(REACH, rows)
    clear_pads(p1, width)
    p1[:, YPAD : YPAD + width, :] = mid[0]

    def fluxes(row):
        _, parts = flux_row(row, width, p1, slope_z[row], before[0, row])
        for a in range(3):
            flux[a, row] = parts[a]

    each_row(rows, width, fluxes)
    clear_pads(p, width)
    clear_sides(rows, p, q, slope_p, slope_q)
    p[own, YPAD : YPAD + width, :] = now[0]
    q[own] = now[1]

    def emit(row, next_p, next_q):
        base[0, row] = next_p
        base[1, row] = next_q

    block_step(
        rows,
        width,
        (p, q),
        (slope_p, slope_q),
        (curve_p, curve_q),
        matrices,
        lambda row: (mid[0, row + REACH], mid[1, row + REACH]),
        lambda row: [coeffs[c, row + REACH] for c in range(5)],
        emit,
    )
    slopes[0] = slope_p[own]
    slopes[1] = slope_q[own]


def late_kernel(
    now,
    mid,
    coeffs,
    on_chip,
    off_near,
    off_outer,
    base,
    own_slopes,
    inject,
    matrices,
    out,
    imaged,
    p,
    q,
    slope_p,
    slope_q,
    curve_p,
    curve_q,
    p1,
    q1,
):
    rows, width = now.shape[1], now.shape[2]
    inner = slice(YPAD, YPAD + width)
    near, far = side_starts(rows, HALO)
    inside = has_far_side()
    odd = lax.rem(lax.axis_index("gx"), 2)
    clear_pads(p, width)
    clear_pads(p1, width)

    def far_rows(part, f):
        return jnp.where(inside, part[f].astype(jnp.float32), 0.0)

    place(
        p,
        q,
        now,
        (
            (near, HALO, lambda f: on_chip[f]),
            (far + (1 - odd) * REACH, REACH, lambda f: far_rows(off_near, f)),
            (far + odd * REACH, REACH, lambda f: far_rows(off_outer, f)),
        ),
        width,
    )
    own = pl.ds(HALO, rows)
    slope_p[own], slope_q[own] = own_slopes[0], own_slopes[1]
    for begin in (0, rows + HALO):
        item = (lambda b, n: p[pl.ds(b, n), inner, :], slope_p, curve_p, begin)
        depth_rows((item,), HALO, width, matrices)
        item = (lambda b, n: q[pl.ds(b, n)], slope_q, curve_q, begin)
        depth_rows((item,), HALO, width, matrices)

    def keep(row, next_p, next_q):
        p1[row, inner, :] = next_p + inject[2, row]
        q1[row] = next_q

    for begin in (0, rows + REACH):
        time_step(
            begin,
            REACH,
            width,
            (p, q),
            lambda row: (mid[0, row], mid[1, row]),
            lambda row: [coeffs[c, row] for c in range(5)],
            (slope_p, slope_q),
            (curve_p, curve_q),
            keep,
        )
    for row in range(REACH, rows + REACH):
        result = add_border(
            row,
            rows,
            (lambda i: p[i + REACH, inner, :], lambda i: q[i + REACH]),
            (lambda i: slope_p[i + REACH], lambda i: slope_q[i + REACH]),
            [coeffs[c, row] for c in range(5)],
            (base[0, row - REACH], base[1, row - REACH]),
        )
        keep(row, *result)

    def emit(row, next_p, next_q):
        out[0, row] = next_p
        out[1, row] = next_q

    second_step(
        rows,
        width,
        p1,
        q1,
        (slope_p, slope_q),
        (curve_p, curve_q),
        lambda row: (now[0, row], now[1, row]),
        coeffs,
        inject.at[3],
        matrices,
        emit,
    )

    def fluxes(row):
        field, parts = flux_row(row, width, p1, slope_p[row + REACH], now[0, row])
        for a, value in enumerate((field, *parts)):
            imaged[a, row] = value

    each_row(rows, width, fluxes)


def image_kernel(
    arrived, mid, flux, imaged, offsets, wave, images, wave_out, block, lines, sems
):
    rows, width, depth = flux.shape[1:]
    whole = pltpu.make_async_copy(wave, wave_out, sems.at[0])
    whole.start()
    parts = arrived.shape[2]
    stride = lines.shape[0] // width
    for place, column in enumerate(exchange_order(width)):
        block_lines = arrived[place].astype(jnp.float32).reshape(stride, depth)
        lines[column * stride : (column + 1) * stride, :] = block_lines

    def source(n, row):
        begin = n * parts * rows + row
        return [lines[pl.ds(begin + c * rows, width, stride=stride), :] for c in range(parts)]

    def image_row(row):
        totals = [None] * NBIN

        def keep(b, term):
            totals[b] = term

        def finish(b, term):
            block[b, row] = (totals[b] + term).astype(block.dtype)

        early = [flux[a, row] for a in range(3)]
        image_terms(source(0, row), mid[0, row + REACH], early, offsets, keep)
        late = [imaged[a, row] for a in range(1, 4)]
        image_terms(source(1, row), imaged[0, row], late, offsets, finish)

    pieces = []
    size = rows // OUT_PIECES
    for piece in range(OUT_PIECES):
        each_row(size, width, lambda row: image_row(row + piece * size))
        part = pl.ds(piece * size, size)
        pieces.append(
            pltpu.make_async_copy(block.at[:, part], images.at[:, part], sems.at[1 + piece])
        )
        pieces[-1].start()
    for piece in pieces:
        piece.wait()
    whole.wait()


def local(
    wave_now,
    wave_prev,
    speed_term,
    thomsen_epsilon,
    thomsen_delta,
    tilt_angle,
    source_store,
    receiver_row,
    receiver_column,
    receiver_traces,
    angle_table,
):
    _, rows, width, depth = wave_now.shape
    count = lax.axis_size("gx")
    odd = lax.rem(lax.axis_index("gx"), 2)
    on_chip_pairs = [(i, i ^ 1) for i in range(count)]
    both_axes = ("shot", "gx")
    shots = lax.axis_size("shot")
    off_chip_pairs = []
    for shot in range(shots):
        at = shot * count
        for i in range(1, count - 1, 2):
            off_chip_pairs += [(at + i, at + i + 1), (at + i + 1, at + i)]
        other = ((shot + 1) % shots) * count
        if shots > 1:
            off_chip_pairs += [(at, other), (at + count - 1, other + count - 1)]

    f32 = jnp.float32
    ext, wide = rows + 2 * REACH, rows + 2 * HALO
    vmem = pl.BlockSpec(memory_space=pltpu.VMEM)
    in_hbm = pl.BlockSpec(memory_space=pltpu.HBM)
    plane = (width, depth)
    padded = (width + 2 * YPAD, depth)
    plane_bytes = 4 * width * depth
    line_flops = width * depth

    def planes(*lead):
        return jax.ShapeDtypeStruct(lead + plane, f32)

    def call(kernel, outs, ins, in_specs, scratch, grant, cost, out_specs=None):
        return pl.pallas_call(
            kernel,
            out_shape=outs,
            in_specs=in_specs,
            out_specs=out_specs or jax.tree.map(lambda _: vmem, outs),
            scratch_shapes=scratch,
            compiler_params=pltpu.CompilerParams(
                vmem_limit_bytes=4 * 1024 * 1024 + grant * plane_bytes
            ),
            cost_estimate=pl.CostEstimate(
                flops=cost * line_flops, bytes_accessed=cost * line_flops // 4, transcendentals=0
            ),
        )(*ins)

    def room(count, lines=plane):
        return pltpu.VMEM((count,) + lines, f32)

    medium = (speed_term, thomsen_epsilon, thomsen_delta, tilt_angle)
    matrices = jax.ShapeDtypeStruct((3, depth, 2 * depth), jnp.bfloat16)
    snaps, parts = source_store.shape[:2]
    by_owner = source_store.reshape(snaps, parts, count, rows, depth)
    sorted_shape = (count, snaps, parts, rows, depth)
    packed = planes(8 * REACH)
    tables = (receiver_row, receiver_column, receiver_traces, angle_table)
    far_pack, near_pack, sorted_source, own_coeffs, base, slopes, matrices, *small = call(
        pack_kernel,
        (
            packed,
            packed,
            jax.ShapeDtypeStruct(sorted_shape, source_store.dtype),
            planes(5, rows),
            planes(2, rows),
            planes(2, rows),
            matrices,
            *[jax.ShapeDtypeStruct(x.shape, x.dtype) for x in tables],
        ),
        [
            pltpu.with_memory_space_constraint(x, pltpu.HBM)
            for x in (wave_now, wave_prev, *medium, by_owner, *tables)
        ],
        [in_hbm] * 11,
        [
            pltpu.VMEM(sorted_shape, source_store.dtype),
            room(ext, padded),
            room(ext),
            pltpu.VMEM((2, rows) + plane, f32),
            pltpu.VMEM((4, rows) + plane, f32),
            *[room(ext)] * 4,
            pltpu.SemaphoreType.DMA((12 + count,)),
        ],
        16 * wide,
        200,
        (vmem, vmem, in_hbm, *[vmem] * 8),
    )
    off_chip = lax.ppermute(far_pack, both_axes, off_chip_pairs)
    on_chip = lax.ppermute(near_pack, "gx", on_chip_pairs)
    arrived = lax.all_to_all(
        sorted_source,
        "gx",
        split_axis=0,
        concat_axis=0,
        tiled=True,
        axis_index_groups=[exchange_order(count)],
    )
    inject, offsets = call(
        prep_kernel,
        (planes(STEPS, ext), jax.ShapeDtypeStruct((16, depth), f32)),
        small,
        [vmem] * 4,
        [],
        8 * wide,
        60 * rows,
    )
    now, far_near, far_outer, mid, coeffs, slope_z = call(
        early_kernel,
        (
            planes(2, rows),
            planes(2, REACH),
            jax.ShapeDtypeStruct((2, REACH) + plane, jnp.bfloat16),
            planes(2, ext),
            planes(5, ext),
            planes(rows),
        ),
        (wave_now, on_chip, off_chip, own_coeffs, base, slopes, inject, matrices),
        [vmem] * 8,
        [
            room(ext),
            room(ext),
            pltpu.VMEM((2, ext) + plane, f32),
            *[room(ext)] * 4,
            room(ext, padded),
        ],
        26 * wide,
        400 * rows,
    )

    def side(tail):
        if rows == HALO:
            return now
        return lax.dynamic_slice_in_dim(now, jnp.where(tail, rows - HALO, 0), HALO, axis=1)

    off_near = lax.ppermute(far_near, both_axes, off_chip_pairs)
    off_outer = lax.ppermute(far_outer, both_axes, off_chip_pairs)
    on_chip = lax.ppermute(side(odd == 0), "gx", on_chip_pairs)
    flux, base, slopes = call(
        side_kernel,
        (planes(3, rows), planes(2, rows), planes(2, rows)),
        (wave_now, mid, slope_z, now, coeffs, matrices),
        [vmem] * 6,
        [room(ext, padded), room(ext, padded), *[room(ext)] * 5],
        18 * wide,
        60 * rows,
    )
    final, imaged = call(
        late_kernel,
        (planes(2, rows), planes(4, rows)),
        (now, mid, coeffs, on_chip, off_near, off_outer, base, slopes, inject, matrices),
        [vmem] * 10,
        [room(wide, padded), *[room(wide)] * 5, room(ext, padded), room(ext)],
        28 * wide,
        400 * rows,
    )
    return call(
        image_kernel,
        (jax.ShapeDtypeStruct((NBIN, rows) + plane, jnp.bfloat16), planes(2, rows)),
        (arrived, mid, flux, imaged, offsets, final),
        [vmem] * 6,
        [
            pltpu.VMEM((NBIN, rows) + plane, jnp.bfloat16),
            pltpu.VMEM((sorted_source.size // depth, depth), f32),
            pltpu.SemaphoreType.DMA((1 + OUT_PIECES,)),
        ],
        16 * wide,
        60 * rows,
        (in_hbm, in_hbm),
    )


def solution(mesh):
    placed = (
        P("shot", "gx", None, None),
        P("shot", "gx", None, None),
        P("gx", None, None),
        P("gx", None, None),
        P("gx", None, None),
        P("gx", None, None),
        P("shot", None, None, "gx", None),
        P("shot"),
        P("shot"),
        P("shot", None),
        P(),
    )
    return jax.shard_map(
        local,
        mesh=mesh,
        in_specs=placed,
        out_specs=(P("shot", "gx", None, None), P("shot", "gx", None, None)),
        check_vma=False,
    )
```

```python
import math

import jax
import jax.numpy as jnp
import numpy as np
from jax import lax
from jax.experimental import pallas as pl
from jax.experimental.pallas import tpu as pltpu
from jax.sharding import PartitionSpec as P


STEPS = 4
NBIN = 8
REC_DEPTH = 2
REACH = 4
HALO = 2 * REACH
YPAD = 8
OUT_PIECES = 4

SECOND = (-205.0 / 72.0, 8.0 / 5.0, -1.0 / 5.0, 8.0 / 315.0, -1.0 / 560.0)
FIRST = (4.0 / 5.0, -1.0 / 5.0, 4.0 / 105.0, -1.0 / 280.0)


def exchange_order(count):
    step = next(n for n in (13, 5, 3, 1) if math.gcd(n, count) == 1)
    return [(count // 2 - 1 + step * j) % count for j in range(count)]


def each_row(count, width, body):
    if width <= 16:
        for row in range(count):
            body(row)
    else:
        lax.fori_loop(0, count, lambda row, carry: (body(row), carry)[1], 0)


def each_chunk(count, width, body):
    size = max(1, min(count, 256 // width))
    while count % size:
        size -= 1
    if count // size <= 2:
        for start in range(0, count, size):
            body(start, size)
    else:
        lax.fori_loop(0, count // size, lambda i, carry: (body(i * size, size), carry)[1], 0)


def second(centre, pairs):
    total = SECOND[0] * centre
    for k in range(1, 5):
        plus, minus = pairs(k)
        total = total + SECOND[k] * (plus + minus)
    return total


def first(pairs):
    total = None
    for k in range(1, 5):
        plus, minus = pairs(k)
        term = FIRST[k - 1] * (plus - minus)
        total = term if total is None else total + term
    return total


def build_matrices(out):
    depth = out.shape[1]
    slope = {k: -FIRST[k - 1] for k in range(1, 5)}
    slope = {d: c for k, v in slope.items() for d, c in ((-k, v), (k, -v))}
    curve = {d: SECOND[abs(d)] for d in range(-4, 5)}
    line = lax.broadcasted_iota(jnp.int32, (depth, depth), 0)
    apart = line - lax.broadcasted_iota(jnp.int32, (depth, depth), 1)
    hits = {d: apart == d for d in range(-4, 5)}
    for side, coefficients in enumerate((slope, curve)):
        rest = {d: np.float32(c) for d, c in coefficients.items()}
        for part in range(3):
            rounded = {d: c.astype(jnp.bfloat16).astype(np.float32) for d, c in rest.items()}
            rest = {d: c - rounded[d] for d, c in rest.items()}
            values = jnp.zeros((depth, depth), jnp.float32)
            for d, c in rounded.items():
                values = jnp.where(hits[d], float(c), values)
            out[part, :, side * depth : (side + 1) * depth] = values.astype(jnp.bfloat16)


def depth_diffs(field, matrices):
    depth = field.shape[1]
    high = field.astype(jnp.bfloat16)
    rest = field - high.astype(jnp.float32)
    middle = rest.astype(jnp.bfloat16)
    low = (rest - middle.astype(jnp.float32)).astype(jnp.bfloat16)
    m_high, m_middle, m_low = matrices[0], matrices[1], matrices[2]

    def product(left, top, bottom):
        return jnp.dot(
            left, jnp.concatenate([top, bottom], axis=0), preferred_element_type=jnp.float32
        )

    upper = jnp.concatenate([high, middle], axis=1)
    lower = jnp.concatenate([high, low], axis=1)
    both = (
        product(lower, m_low, m_high)
        + product(upper, m_middle, m_middle)
        + product(upper, m_high, m_high)
    )
    return both[:, :depth], both[:, depth:]


def depth_rows(items, count, width, matrices):
    def chunk(start, size):
        lines = size * width
        fields = [read(begin + start, size) for read, _, _, begin in items]
        depth = fields[0].shape[-1]
        joined = jnp.concatenate([f.reshape(lines, depth) for f in fields], axis=0)
        slopes, curves = depth_diffs(joined, matrices)
        for i, (_, slope, curve, begin) in enumerate(items):
            part = slice(i * lines, (i + 1) * lines)
            rows = pl.ds(begin + start, size)
            slope[rows] = slopes[part].reshape(size, width, depth)
            if curve is not None:
                curve[rows] = curves[part].reshape(size, width, depth)

    each_chunk(count, width * len(items), chunk)


def sine_terms(angle):
    half = 0.5 * angle
    sq = half * half
    s = 1.0
    for n in (12 * 13, 10 * 11, 8 * 9, 6 * 7, 4 * 5, 2 * 3):
        s = 1.0 - sq * s * (1.0 / n)
    s = s * half
    c = 1.0
    for n in (13 * 14, 11 * 12, 9 * 10, 7 * 8, 5 * 6, 3 * 4, 1 * 2):
        c = 1.0 - sq * c * (1.0 / n)
    sine = 2.0 * s * c
    cosine = 1.0 - 2.0 * s * s
    return sine * sine, 2.0 * sine * cosine


def derive(coeffs, at, s, e, d, a):
    coeffs[0, at] = s
    coeffs[1, at] = s * (1.0 + 2.0 * e)
    coeffs[2, at] = s * jnp.sqrt(1.0 + 2.0 * d)
    coeffs[3, at], coeffs[4, at] = sine_terms(a)


def receivers(row_ref, column_ref, rows, width):
    begin = lax.axis_index("gx") * rows - REACH
    count = row_ref.shape[0]
    local_row = row_ref[...].reshape(1, count) - begin
    inside = (local_row >= 0) & (local_row < rows + 2 * REACH)
    return jnp.where(inside, local_row * width + column_ref[...].reshape(1, count), -1)


def time_step(begin, rows, width, fields, earlier, coeffs, slopes, curves, emit):
    p, q = fields
    slope_p, slope_q = slopes
    curve_p, curve_q = curves
    inner = slice(YPAD, YPAD + width)

    def update(row):
        at = row + REACH
        now_p = p[at, inner, :]
        now_q = q[at]
        xx_p = second(now_p, lambda k: (p[at + k, inner, :], p[at - k, inner, :]))
        xx_q = second(now_q, lambda k: (q[at + k], q[at - k]))
        xz_p = first(lambda k: (slope_p[at + k], slope_p[at - k]))
        xz_q = first(lambda k: (slope_q[at + k], slope_q[at - k]))
        yy_p = second(
            now_p,
            lambda k: (
                p[at, YPAD + k : YPAD + k + width, :],
                p[at, YPAD - k : YPAD - k + width, :],
            ),
        )
        speed, gain, mixed, sine_sq, sine_double = coeffs(row)
        tilt_p = sine_sq * (xx_p - curve_p[at]) + sine_double * xz_p
        tilt_q = sine_sq * (xx_q - curve_q[at]) + sine_double * xz_q
        across = xx_p + yy_p - tilt_p
        rotated = curve_q[at] + tilt_q
        prev_p, prev_q = earlier(row)
        next_p = 2.0 * now_p - prev_p + (gain * across + mixed * rotated)
        next_q = 2.0 * now_q - prev_q + (mixed * across + speed * rotated)
        emit(row, next_p, next_q)

    each_row(rows, width, lambda row: update(begin + row))


def border_terms(row, rows, read, slope):
    curve, mixed = None, None
    for border in (REACH, rows + REACH):
        for k in range(1, 5):
            for other, sign in ((row + k, 1.0), (row - k, -1.0)):
                low, high = min(row, other), max(row, other)
                if low < border <= high:
                    c = SECOND[k] * read(other)
                    m = (sign * FIRST[k - 1]) * slope(other)
                    curve = c if curve is None else curve + c
                    mixed = m if mixed is None else mixed + m
    return curve, mixed


def add_border(row, rows, reads, slopes, coeffs, base):
    next_p, next_q = base
    xx_p, xz_p = border_terms(row, rows, reads[0], slopes[0])
    if xx_p is None:
        return next_p, next_q
    xx_q, xz_q = border_terms(row, rows, reads[1], slopes[1])
    speed, gain, mixed, sine_sq, sine_double = coeffs
    across = xx_p - (sine_sq * xx_p + sine_double * xz_p)
    rotated = sine_sq * xx_q + sine_double * xz_q
    return (
        next_p + (gain * across + mixed * rotated),
        next_q + (mixed * across + speed * rotated),
    )


def block_step(rows, width, fields, slopes, curves, matrices, earlier, coeffs, emit):
    p, q = fields
    inner = slice(YPAD, YPAD + width)
    items = (
        (lambda b, n: p[pl.ds(b, n), inner, :], slopes[0], curves[0], REACH),
        (lambda b, n: q[pl.ds(b, n)], slopes[1], curves[1], REACH),
    )
    depth_rows(items, rows, width, matrices)
    time_step(0, rows, width, fields, earlier, coeffs, slopes, curves, emit)


def clear_sides(rows, *refs):
    for ref in refs:
        zeros = jnp.zeros((REACH,) + ref.shape[1:], jnp.float32)
        ref[pl.ds(0, REACH)] = zeros
        ref[pl.ds(rows + REACH, REACH)] = zeros


def flux_row(row, width, p, slope_z, before):
    at = row + REACH
    now = p[at, YPAD : YPAD + width, :]
    back = before - now
    slope_x = first(
        lambda k: (p[at + k, YPAD : YPAD + width, :], p[at - k, YPAD : YPAD + width, :])
    )
    slope_y = first(
        lambda k: (p[at, YPAD + k : YPAD + k + width, :], p[at, YPAD - k : YPAD - k + width, :])
    )
    return now, (back * slope_x, back * slope_y, back * slope_z)


def image_terms(source, field, flux, offsets, emit):
    fx, fy, fz = flux
    s0, s1, s2, s3 = source
    dot = s1 * fx + s2 * fy + s3 * fz
    squares = (s1 * s1 + s2 * s2 + s3 * s3) * (fx * fx + fy * fy + fz * fz)
    cosine = dot * jnp.minimum(lax.rsqrt(squares), 1.0)
    scaled = (cosine + 1.0) * offsets[NBIN : NBIN + 1, :]
    strength = s0 * field
    above = strength
    for b in range(NBIN - 1):
        beyond = jnp.clip(scaled - offsets[b + 1 : b + 2, :], 0.0, 1.0) * strength
        emit(b, above - beyond)
        above = beyond
    emit(NBIN - 1, above)


def clear_pads(ref, width, begin, rows):
    zeros = jnp.zeros((rows, YPAD, ref.shape[2]), jnp.float32)
    ref[pl.ds(begin, rows), :YPAD, :] = zeros
    ref[pl.ds(begin, rows), YPAD + width :, :] = zeros


def place(dst_p, dst_q, centre, sides, width):
    inner = pl.ds(YPAD, width)
    for at, count, read in ((HALO, centre.shape[1], lambda f: centre[f]), *sides):
        dst_p[pl.ds(at, count), inner, :] = read(0)
        dst_q[pl.ds(at, count)] = read(1)


def side_starts(rows, reach):
    odd = lax.rem(lax.axis_index("gx"), 2)
    on_chip = jnp.where(odd == 1, 0, rows + reach)
    off_chip = jnp.where(odd == 1, rows + reach, 0)
    return on_chip, off_chip


def has_far_side():
    at = lax.axis_index("gx")
    return (at > 0) & (at < lax.axis_size("gx") - 1)


def second_step(rows, width, p1, q1, slopes, curves, earlier, coeffs, inject, matrices, emit):
    inner = slice(YPAD, YPAD + width)
    ext = rows + 2 * REACH
    items = (
        (lambda b, n: p1[pl.ds(b, n), inner, :], slopes[0], curves[0], 0),
        (lambda b, n: q1[pl.ds(b, n)], slopes[1], curves[1], 0),
    )
    depth_rows(items, ext, width, matrices)

    def finish(row, next_p, next_q):
        emit(row, next_p + inject[row + REACH], next_q)

    time_step(
        0,
        rows,
        width,
        (p1, q1),
        earlier,
        lambda row: [coeffs[c, row + REACH] for c in range(5)],
        slopes,
        curves,
        finish,
    )


def pack_kernel(
    now,
    prev,
    speed,
    epsilon,
    delta,
    tilt,
    source,
    receiver_row,
    receiver_column,
    traces,
    table,
    far,
    near,
    sorted_source,
    coeffs,
    base,
    slopes,
    weights,
    row_out,
    column_out,
    traces_out,
    table_out,
    staged,
    p,
    q,
    before,
    medium,
    slope_p,
    slope_q,
    curve_p,
    curve_q,
    sems,
):
    rows, width = now.shape[1], now.shape[2]
    odd = lax.rem(lax.axis_index("gx"), 2)
    started = []

    def copy(src, dst):
        started.append(pltpu.make_async_copy(src, dst, sems.at[len(started)]))
        started[-1].start()
        return started[-1]

    arriving = []
    for place, owner in enumerate(exchange_order(source.shape[2])):
        arriving.append(copy(source.at[:, :, owner], staged.at[place]))
    clear_pads(p, width, REACH, rows)
    clear_sides(rows, p, q, slope_p, slope_q)
    own = pl.ds(REACH, rows)
    inner = slice(YPAD, YPAD + width)
    local = [copy(field, medium.at[m]) for m, field in enumerate((speed, epsilon, delta, tilt))]
    local.append(copy(now.at[0], p.at[own, pl.ds(YPAD, width)]))
    local.append(copy(now.at[1], q.at[own]))
    local.append(copy(prev, before))
    local.append(copy(receiver_row, row_out))
    local.append(copy(receiver_column, column_out))
    local.append(copy(traces, traces_out))
    local.append(copy(table, table_out))
    build_matrices(weights)
    for one in arriving:
        one.wait()
    leaving = copy(staged, sorted_source)
    for one in local:
        one.wait()
    each_row(rows, width, lambda r: derive(coeffs, r, *[medium[m, r] for m in range(4)]))

    def emit(row, next_p, next_q):
        base[0, row] = next_p
        base[1, row] = next_q

    block_step(
        rows,
        width,
        (p, q),
        (slope_p, slope_q),
        (curve_p, curve_q),
        weights,
        lambda row: (before[0, row], before[1, row]),
        lambda row: [coeffs[c, row] for c in range(5)],
        emit,
    )
    slopes[0] = slope_p[own]
    slopes[1] = slope_q[own]
    for out, tail in ((far, odd), (near, 1 - odd)):
        first_row = tail * (rows - REACH)
        edge = pl.ds(first_row, REACH)
        edge_fields = [
            p[pl.ds(REACH + first_row, REACH), inner, :],
            q[pl.ds(REACH + first_row, REACH)],
            base[0, edge],
            base[1, edge],
            *[medium[m, edge] for m in range(4)],
        ]
        for index, value in enumerate(edge_fields):
            out[pl.ds(index * REACH, REACH)] = value
    leaving.wait()


def prep_kernel(receiver_row, receiver_column, traces, table, inject, offsets):
    _, ext, width, depth = inject.shape
    flat = receivers(receiver_row, receiver_column, ext - 2 * REACH, width)
    count = flat.shape[1]
    at_depth = lax.broadcasted_iota(jnp.int32, (depth, count), 0) == REC_DEPTH
    parts = []
    rest = traces[...]
    for _ in range(3):
        parts.append(rest.astype(jnp.bfloat16).astype(jnp.float32))
        rest = rest - parts[-1]
    samples = [
        jnp.concatenate(
            [jnp.where(at_depth, part[t : t + 1, :], 0.0) for t in range(STEPS)], axis=0
        ).astype(jnp.bfloat16)
        for part in reversed(parts)
    ]

    def chunk(start, size):
        lines = size * width
        cell = lax.broadcasted_iota(jnp.int32, (lines, count), 0) + start * width
        hit = jnp.where(cell == flat, 1.0, 0.0).astype(jnp.bfloat16)
        total = None
        for sample in samples:
            term = lax.dot_general(
                hit, sample, (((1,), (1,)), ((), ())), preferred_element_type=jnp.float32
            )
            total = term if total is None else total + term
        for t in range(STEPS):
            part = total[:, t * depth : (t + 1) * depth]
            inject[t, pl.ds(start, size)] = part.reshape(size, width, depth)

    each_chunk(ext, width, chunk)
    fine = table.shape[0]
    names = table[...].reshape(1, fine)
    for b in range(NBIN):
        begin = jnp.sum((names < b).astype(jnp.float32), axis=1, keepdims=True) - 1.0
        offsets[b : b + 1, :] = jnp.broadcast_to(begin, (1, depth))
    offsets[NBIN : NBIN + 1, :] = jnp.full((1, depth), 0.5 * (fine - 1), jnp.float32)


def early_kernel(
    now,
    on_chip,
    off_chip,
    own_coeffs,
    base,
    own_slopes,
    inject,
    matrices,
    out,
    far_near,
    far_outer,
    mid,
    coeffs,
    slope_out,
    p,
    q,
    ext_base,
    slope_p,
    slope_q,
    curve_p,
    curve_q,
    p1,
):
    rows, width = now.shape[1], now.shape[2]
    inner = slice(YPAD, YPAD + width)
    near, far = side_starts(rows, REACH)
    inside = has_far_side()
    clear_pads(p1, width, REACH, rows)
    own = pl.ds(REACH, rows)
    p[own], q[own] = now[0], now[1]
    slope_p[own], slope_q[own] = own_slopes[0], own_slopes[1]
    for f in range(2):
        ext_base[f, own] = base[f]
    for c in range(5):
        coeffs[c, own] = own_coeffs[c]
    for at, part, real in ((near, on_chip, None), (far, off_chip, inside)):

        def take(index, real=real, part=part):
            value = part[pl.ds(index * REACH, REACH)]
            return value if real is None else jnp.where(real, value, 0.0)

        side = pl.ds(at, REACH)
        p[side], q[side] = take(0), take(1)
        ext_base[0, side], ext_base[1, side] = take(2), take(3)
        medium = [take(4)] + [part[pl.ds((5 + m) * REACH, REACH)] for m in range(3)]
        for r in range(REACH):
            derive(coeffs, at + r, *[m[r] for m in medium])
    items = []
    for begin in (0, rows + REACH):
        items.append((lambda b, n: p[pl.ds(b, n)], slope_p, None, begin))
        items.append((lambda b, n: q[pl.ds(b, n)], slope_q, None, begin))
    depth_rows(items, REACH, width, matrices)
    q1 = mid.at[1]
    for row in range(rows + 2 * REACH):
        next_p, next_q = add_border(
            row,
            rows,
            (lambda i: p[i], lambda i: q[i]),
            (lambda i: slope_p[i], lambda i: slope_q[i]),
            [coeffs[c, row] for c in range(5)],
            (ext_base[0, row], ext_base[1, row]),
        )
        next_p = next_p + inject[0, row]
        p1[row, inner, :] = next_p
        mid[0, row] = next_p
        mid[1, row] = next_q

    def emit(row, next_p, next_q):
        out[0, row] = next_p
        out[1, row] = next_q

    second_step(
        rows,
        width,
        p1,
        q1,
        (slope_p, slope_q),
        (curve_p, curve_q),
        lambda row: (now[0, row], now[1, row]),
        coeffs,
        inject.at[1],
        matrices,
        emit,
    )
    slope_out[...] = slope_p[own]
    tail = lax.rem(lax.axis_index("gx"), 2)
    for f in range(2):
        far_near[f] = out[f, pl.ds(tail * (rows - REACH), REACH)]
        outer = out[f, pl.ds(REACH + tail * (rows - HALO - REACH), REACH)]
        far_outer[f] = outer.astype(far_outer.dtype)


def side_kernel(
    before,
    mid,
    slope_z,
    now,
    coeffs,
    matrices,
    flux,
    base,
    slopes,
    p1,
    p,
    q,
    slope_p,
    slope_q,
    curve_p,
    curve_q,
):
    rows, width = before.shape[1], before.shape[2]
    own = pl.ds(REACH, rows)
    clear_pads(p1, width, REACH, rows)
    p1[:, YPAD : YPAD + width, :] = mid[0]

    def fluxes(row):
        _, parts = flux_row(row, width, p1, slope_z[row], before[0, row])
        for a in range(3):
            flux[a, row] = parts[a]

    each_row(rows, width, fluxes)
    clear_pads(p, width, REACH, rows)
    clear_sides(rows, p, q, slope_p, slope_q)
    p[own, YPAD : YPAD + width, :] = now[0]
    q[own] = now[1]

    def emit(row, next_p, next_q):
        base[0, row] = next_p
        base[1, row] = next_q

    block_step(
        rows,
        width,
        (p, q),
        (slope_p, slope_q),
        (curve_p, curve_q),
        matrices,
        lambda row: (mid[0, row + REACH], mid[1, row + REACH]),
        lambda row: [coeffs[c, row + REACH] for c in range(5)],
        emit,
    )
    slopes[0] = slope_p[own]
    slopes[1] = slope_q[own]


def late_kernel(
    now,
    mid,
    coeffs,
    on_chip,
    off_near,
    off_outer,
    base,
    own_slopes,
    inject,
    matrices,
    out,
    imaged,
    p,
    q,
    slope_p,
    slope_q,
    curve_p,
    curve_q,
    p1,
    q1,
):
    rows, width = now.shape[1], now.shape[2]
    inner = slice(YPAD, YPAD + width)
    near, far = side_starts(rows, HALO)
    inside = has_far_side()
    odd = lax.rem(lax.axis_index("gx"), 2)
    for begin in (REACH, rows + HALO):
        clear_pads(p, width, begin, REACH)
    clear_pads(p1, width, REACH, rows)

    def far_rows(part, f):
        return jnp.where(inside, part[f].astype(jnp.float32), 0.0)

    place(
        p,
        q,
        now,
        (
            (near, HALO, lambda f: on_chip[f]),
            (far + (1 - odd) * REACH, REACH, lambda f: far_rows(off_near, f)),
            (far + odd * REACH, REACH, lambda f: far_rows(off_outer, f)),
        ),
        width,
    )
    own = pl.ds(HALO, rows)
    slope_p[own], slope_q[own] = own_slopes[0], own_slopes[1]
    for begin in (0, rows + HALO):
        item = (lambda b, n: p[pl.ds(b, n), inner, :], slope_p, curve_p, begin)
        depth_rows((item,), HALO, width, matrices)
        item = (lambda b, n: q[pl.ds(b, n)], slope_q, curve_q, begin)
        depth_rows((item,), HALO, width, matrices)

    def keep(row, next_p, next_q):
        p1[row, inner, :] = next_p + inject[2, row]
        q1[row] = next_q

    for begin in (0, rows + REACH):
        time_step(
            begin,
            REACH,
            width,
            (p, q),
            lambda row: (mid[0, row], mid[1, row]),
            lambda row: [coeffs[c, row] for c in range(5)],
            (slope_p, slope_q),
            (curve_p, curve_q),
            keep,
        )
    for row in range(REACH, rows + REACH):
        result = add_border(
            row,
            rows,
            (lambda i: p[i + REACH, inner, :], lambda i: q[i + REACH]),
            (lambda i: slope_p[i + REACH], lambda i: slope_q[i + REACH]),
            [coeffs[c, row] for c in range(5)],
            (base[0, row - REACH], base[1, row - REACH]),
        )
        keep(row, *result)

    def emit(row, next_p, next_q):
        out[0, row] = next_p
        out[1, row] = next_q

    second_step(
        rows,
        width,
        p1,
        q1,
        (slope_p, slope_q),
        (curve_p, curve_q),
        lambda row: (now[0, row], now[1, row]),
        coeffs,
        inject.at[3],
        matrices,
        emit,
    )

    def fluxes(row):
        field, parts = flux_row(row, width, p1, slope_p[row + REACH], now[0, row])
        for a, value in enumerate((field, *parts)):
            imaged[a, row] = value

    each_row(rows, width, fluxes)


def image_kernel(
    arrived, mid, flux, imaged, offsets, wave, images, wave_out, block, lines, sems
):
    rows, width, depth = flux.shape[1:]
    whole = pltpu.make_async_copy(wave, wave_out, sems.at[0])
    whole.start()
    parts = arrived.shape[2]
    stride = lines.shape[0] // width
    for place, column in enumerate(exchange_order(width)):
        block_lines = arrived[place].astype(jnp.float32).reshape(stride, depth)
        lines[column * stride : (column + 1) * stride, :] = block_lines

    def source(n, row):
        begin = n * parts * rows + row
        return [lines[pl.ds(begin + c * rows, width, stride=stride), :] for c in range(parts)]

    def image_row(row):
        totals = [None] * NBIN

        def keep(b, term):
            totals[b] = term

        def finish(b, term):
            block[b, row] = (totals[b] + term).astype(block.dtype)

        early = [flux[a, row] for a in range(3)]
        image_terms(source(0, row), mid[0, row + REACH], early, offsets, keep)
        late = [imaged[a, row] for a in range(1, 4)]
        image_terms(source(1, row), imaged[0, row], late, offsets, finish)

    pieces = []
    size = rows // OUT_PIECES
    for piece in range(OUT_PIECES):
        each_row(size, width, lambda row: image_row(row + piece * size))
        part = pl.ds(piece * size, size)
        pieces.append(
            pltpu.make_async_copy(block.at[:, part], images.at[:, part], sems.at[1 + piece])
        )
        pieces[-1].start()
    for piece in pieces:
        piece.wait()
    whole.wait()


def local(
    wave_now,
    wave_prev,
    speed_term,
    thomsen_epsilon,
    thomsen_delta,
    tilt_angle,
    source_store,
    receiver_row,
    receiver_column,
    receiver_traces,
    angle_table,
):
    _, rows, width, depth = wave_now.shape
    count = lax.axis_size("gx")
    odd = lax.rem(lax.axis_index("gx"), 2)
    on_chip_pairs = [(i, i ^ 1) for i in range(count)]
    both_axes = ("shot", "gx")
    shots = lax.axis_size("shot")
    off_chip_pairs = []
    for shot in range(shots):
        at = shot * count
        for i in range(1, count - 1, 2):
            off_chip_pairs += [(at + i, at + i + 1), (at + i + 1, at + i)]
        other = ((shot + 1) % shots) * count
        if shots > 1:
            off_chip_pairs += [(at, other), (at + count - 1, other + count - 1)]

    f32 = jnp.float32
    ext, wide = rows + 2 * REACH, rows + 2 * HALO
    vmem = pl.BlockSpec(memory_space=pltpu.VMEM)
    in_hbm = pl.BlockSpec(memory_space=pltpu.HBM)
    plane = (width, depth)
    padded = (width + 2 * YPAD, depth)
    plane_bytes = 4 * width * depth
    line_flops = width * depth

    def planes(*lead):
        return jax.ShapeDtypeStruct(lead + plane, f32)

    def call(kernel, outs, ins, in_specs, scratch, grant, cost, out_specs=None):
        return pl.pallas_call(
            kernel,
            out_shape=outs,
            in_specs=in_specs,
            out_specs=out_specs or jax.tree.map(lambda _: vmem, outs),
            scratch_shapes=scratch,
            compiler_params=pltpu.CompilerParams(
                vmem_limit_bytes=4 * 1024 * 1024 + grant * plane_bytes
            ),
            cost_estimate=pl.CostEstimate(
                flops=cost * line_flops, bytes_accessed=cost * line_flops // 4, transcendentals=0
            ),
        )(*ins)

    def room(count, lines=plane):
        return pltpu.VMEM((count,) + lines, f32)

    medium = (speed_term, thomsen_epsilon, thomsen_delta, tilt_angle)
    matrices = jax.ShapeDtypeStruct((3, depth, 2 * depth), jnp.bfloat16)
    snaps, parts = source_store.shape[:2]
    by_owner = source_store.reshape(snaps, parts, count, rows, depth)
    sorted_shape = (count, snaps, parts, rows, depth)
    packed = planes(8 * REACH)
    tables = (receiver_row, receiver_column, receiver_traces, angle_table)
    far_pack, near_pack, sorted_source, own_coeffs, base, slopes, matrices, *small = call(
        pack_kernel,
        (
            packed,
            packed,
            jax.ShapeDtypeStruct(sorted_shape, source_store.dtype),
            planes(5, rows),
            planes(2, rows),
            planes(2, rows),
            matrices,
            *[jax.ShapeDtypeStruct(x.shape, x.dtype) for x in tables],
        ),
        [
            pltpu.with_memory_space_constraint(x, pltpu.HBM)
            for x in (wave_now, wave_prev, *medium, by_owner, *tables)
        ],
        [in_hbm] * 11,
        [
            pltpu.VMEM(sorted_shape, source_store.dtype),
            room(ext, padded),
            room(ext),
            pltpu.VMEM((2, rows) + plane, f32),
            pltpu.VMEM((4, rows) + plane, f32),
            *[room(ext)] * 4,
            pltpu.SemaphoreType.DMA((12 + count,)),
        ],
        16 * wide,
        200,
        (vmem, vmem, in_hbm, *[vmem] * 8),
    )
    off_chip = lax.ppermute(far_pack, both_axes, off_chip_pairs)
    on_chip = lax.ppermute(near_pack, "gx", on_chip_pairs)
    arrived = lax.all_to_all(
        sorted_source,
        "gx",
        split_axis=0,
        concat_axis=0,
        tiled=True,
        axis_index_groups=[exchange_order(count)],
    )
    inject, offsets = call(
        prep_kernel,
        (planes(STEPS, ext), jax.ShapeDtypeStruct((16, depth), f32)),
        small,
        [vmem] * 4,
        [],
        8 * wide,
        60 * rows,
    )
    now, far_near, far_outer, mid, coeffs, slope_z = call(
        early_kernel,
        (
            planes(2, rows),
            planes(2, REACH),
            jax.ShapeDtypeStruct((2, REACH) + plane, jnp.bfloat16),
            planes(2, ext),
            planes(5, ext),
            planes(rows),
        ),
        (wave_now, on_chip, off_chip, own_coeffs, base, slopes, inject, matrices),
        [vmem] * 8,
        [
            room(ext),
            room(ext),
            pltpu.VMEM((2, ext) + plane, f32),
            *[room(ext)] * 4,
            room(ext, padded),
        ],
        26 * wide,
        400 * rows,
    )

    def side(tail):
        if rows == HALO:
            return now
        return lax.dynamic_slice_in_dim(now, jnp.where(tail, rows - HALO, 0), HALO, axis=1)

    off_near = lax.ppermute(far_near, both_axes, off_chip_pairs)
    off_outer = lax.ppermute(far_outer, both_axes, off_chip_pairs)
    on_chip = lax.ppermute(side(odd == 0), "gx", on_chip_pairs)
    flux, base, slopes = call(
        side_kernel,
        (planes(3, rows), planes(2, rows), planes(2, rows)),
        (wave_now, mid, slope_z, now, coeffs, matrices),
        [vmem] * 6,
        [room(ext, padded), room(ext, padded), *[room(ext)] * 5],
        18 * wide,
        60 * rows,
    )
    final, imaged = call(
        late_kernel,
        (planes(2, rows), planes(4, rows)),
        (now, mid, coeffs, on_chip, off_near, off_outer, base, slopes, inject, matrices),
        [vmem] * 10,
        [room(wide, padded), *[room(wide)] * 5, room(ext, padded), room(ext)],
        28 * wide,
        400 * rows,
    )
    return call(
        image_kernel,
        (jax.ShapeDtypeStruct((NBIN, rows) + plane, jnp.bfloat16), planes(2, rows)),
        (arrived, mid, flux, imaged, offsets, final),
        [vmem] * 6,
        [
            pltpu.VMEM((NBIN, rows) + plane, jnp.bfloat16),
            pltpu.VMEM((sorted_source.size // depth, depth), f32),
            pltpu.SemaphoreType.DMA((1 + OUT_PIECES,)),
        ],
        16 * wide,
        60 * rows,
        (in_hbm, in_hbm),
    )


def solution(mesh):
    placed = (
        P("shot", "gx", None, None),
        P("shot", "gx", None, None),
        P("gx", None, None),
        P("gx", None, None),
        P("gx", None, None),
        P("gx", None, None),
        P("shot", None, None, "gx", None),
        P("shot"),
        P("shot"),
        P("shot", None),
        P(),
    )
    return jax.shard_map(
        local,
        mesh=mesh,
        in_specs=placed,
        out_specs=(P("shot", "gx", None, None), P("shot", "gx", None, None)),
        check_vma=False,
    )
```
